256 devices in a mesh: head: 4 (over x), grp: 4 (over y_hi, core), blk: 16 (over y_lo, z).
Axes of the slice: x: 4, y: 4 (y_hi: 2, y_lo: 2; y = y_hi * 2 + y_lo), z: 8, core: 2. Of those that a mesh axis runs over, the one named last changes fastest.
Arguments:
- tokens: bfloat16 [16384, 2880], P(('grp', 'blk'), 'head'), may hold values from -450 to 450
- norm_gain: float32 [2880], replicated, may hold values from 0.9 to 12
- w_query: bfloat16 [2880, 4096], P(None, 'head'), may hold values from -0.109375 to 0.109375
- w_key: bfloat16 [2880, 512], P(None, 'head'), may hold values from -0.109375 to 0.109375
- w_value: bfloat16 [2880, 512], P(None, 'head'), may hold values from -0.109375 to 0.109375
- sinks: float32 [64], P('head'), may hold values from 0 to 8
- doc_lengths: int32 [12], replicated, may hold values from 1 to 8192, 16384 in all
- tile_mask: int32 [128, 128], replicated, may hold values 0 or 1
Outputs:
- attended: bfloat16 [16384, 4096], P(('grp', 'blk'), 'head')
The draws below stay inside these ranges and needn't reach their ends.
Inputs may be any that keep to these rules, and one draw needn't show every extreme that they name: `doc_lengths`: the 12 lengths sum to 16384 and the longest is exactly 8192.
All inputs are finite; a program needn't handle non-finite values.
Results may differ from the reference program's by a relative error of at most 0.017.
The reference program's roundings to bfloat16 on the way count: a program that leaves them out, or rounds other values in their place, can miss the bound.
Values may be sent and summed in bfloat16 or wider, within the bound.
A program may use at most 64 MiB of HBM per device.

```python
import math
import jax
import jax.numpy as jnp
import numpy as np
from jax import lax

D = 2880
HEADS = 64
KVH = 8
HD = 64
TILE = 128
NDOCS = 12
L = 16384
MAXDOC = 8192
NT = 128


def draw_tokens(key, part):
    key_cols, key_rows, key_entries = jax.random.split(key, 3)
    col_scale = jnp.exp(jax.random.uniform(key_cols, (D,), jnp.float32, 0.0, math.log(10.0)))
    row_scale = jnp.exp(jax.random.uniform(key_rows, (L, 1), jnp.float32, 0.0, math.log(10.0)))
    entries = jnp.clip(jax.random.normal(key_entries, (L, D), jnp.float32), -4.5, 4.5)
    return (entries * col_scale[None, :] * row_scale).astype(jnp.bfloat16)


def draw_norm_gain(key, part):
    return jnp.exp(jax.random.uniform(key, (D,), jnp.float32, math.log(0.9), math.log(2.0)))


def with_ends(values, own_key, smallest, top_value):
    dims = values.shape
    index_at = [jax.random.randint(jax.random.fold_in(own_key, axis), (), 0, dims[axis]) for axis in range(len(dims))]
    values = values.at[tuple(index_at)].set(smallest)
    longest = dims.index(max(dims))
    index_at[longest] = (index_at[longest] + 1) % dims[longest]
    return values.at[tuple(index_at)].set(top_value)


def level_of(stream_key, dims, cuts, low, largest):
    level, own = 1.0, jax.random.fold_in(stream_key, 6)
    for position, parts in cuts:
        heights = jnp.exp(jax.random.uniform(jax.random.fold_in(own, position), (parts,), jnp.float32, low / len(cuts), largest / len(cuts)))
        level = level * jnp.repeat(heights, dims[position] // parts).reshape([-1 if axis == position else 1 for axis in range(len(dims))])
    return level


def length_profile(amount, total, limit, skew):
    weights = [(1 << 20) // math.isqrt(standing ** skew) + 1 for standing in range(2, amount + 1)]
    rest, given = total - limit - (amount - 1), [1] * (amount - 1)
    while rest > 0:
        movable = [i for i in range(amount - 1) if given[i] < limit]
        mass, left = sum([weights[i] for i in movable]), rest
        for i in movable:
            more = min(limit - given[i], max(1, left * weights[i] // mass), rest)
            given[i] = given[i] + more
            rest = rest - more
    return np.array([limit] + given)


def ragged_sizes(stream_key, number_of, total, reach, lean):
    if number_of == 2:
        one = jax.random.randint(stream_key, (), max(1, total - reach), min(reach, total - 1) + 1)
        return jnp.stack([one, total - one])
    tallies = jnp.asarray(length_profile(number_of, total, reach, lean), jnp.int32)
    twos = (number_of - 1) // 2
    donor, taker = tallies[1:1 + 2 * twos:2], tallies[2:2 + 2 * twos:2]
    slack = jnp.minimum(donor - 1, reach - taker)
    moved = jax.random.randint(jax.random.fold_in(stream_key, 1), (twos,), 0, 1 << 20) % (slack + 1)
    tallies = tallies.at[1:1 + 2 * twos:2].set(donor - moved).at[2:2 + 2 * twos:2].set(taker + moved)
    return tallies[jax.random.permutation(jax.random.fold_in(stream_key, 2), number_of)]


def scatter_about(key, extent, spread, bound, shards=(), kind=jnp.bfloat16):
    values = jax.random.normal(key, extent, jnp.float32) * spread
    if len(shards) > 0:
        values = level_of(key, extent, shards, -0.22, 0.18) * values
    return jnp.clip(values, min=-bound, max=bound).astype(kind)


def setup_inputs(seed: int = 0) -> dict:
    streams_of = jax.random.split(jax.random.key(seed), 9)
    tokens = draw_tokens(jax.random.fold_in(streams_of[8], 71), 0)
    norm_gain = draw_norm_gain(jax.random.fold_in(streams_of[8], 71), 0)
    w_query = scatter_about(streams_of[2], (D, HEADS * HD), D ** -0.5, 0.109375, ((1, 4),))
    w_key = scatter_about(streams_of[3], (D, KVH * HD), D ** -0.5, 0.109375, ((1, 4),))
    w_value = scatter_about(streams_of[4], (D, KVH * HD), D ** -0.5, 0.109375, ((1, 4),))
    sinks = jnp.clip(8.0 * jax.random.uniform(streams_of[5], (HEADS,), jnp.float32) ** level_of(streams_of[5], (HEADS,), ((0, 4),), -0.2, 0.2), 0.0, 8.0)
    doc_lengths = ragged_sizes(streams_of[6], NDOCS, L, MAXDOC, 2).astype(jnp.int32)
    tile_mask = with_ends((jax.random.randint(streams_of[7], (NT, NT), 0, 4) < 3).astype(jnp.int32), jax.random.fold_in(streams_of[7], 1), 0, 1)
    return {"tokens": tokens, "norm_gain": norm_gain, "w_query": w_query, "w_key": w_key, "w_value": w_value, "sinks": sinks, "doc_lengths": doc_lengths, "tile_mask": tile_mask}


epsilon = 1e-05
rope_base = 150000.0

def rotate(projected, positions, head_size):
    row_count = projected.shape[0]
    head_count = projected.shape[1] // head_size
    half_size = head_size // 2
    shaped = projected.reshape(row_count, head_count, head_size)
    frequency = rope_base ** (-2.0 * jnp.arange(half_size, dtype=jnp.float32) / head_size)
    angles = positions.astype(jnp.float32)[:, None] * frequency[None, :]
    cosine = jnp.cos(angles)[:, None, :]
    sine_part = jnp.sin(angles)[:, None, :]
    first_half = shaped[:, :, :half_size]
    second_half = shaped[:, :, half_size:]
    turned = jnp.concatenate([first_half * cosine - second_half * sine_part, second_half * cosine + first_half * sine_part], axis=2)
    return turned.reshape(row_count, head_count * head_size)

def doc_index(positions, doc_ends):
    return lax.optimization_barrier(jnp.sum((doc_ends[None, :] <= positions[:, None]).astype(jnp.int32), axis=1))

def reference(tokens, norm_gain, w_query, w_key, w_value, sinks, doc_lengths, tile_mask):
    widened = tokens.astype(jnp.float32)
    normed = (widened * lax.rsqrt(lax.optimization_barrier(jnp.mean(widened * widened, axis=1, keepdims=True)) + epsilon) * norm_gain[None, :]).astype(jnp.bfloat16)
    positions = jnp.arange(L, dtype=jnp.int32)
    queries = rotate(jnp.dot(normed, w_query, preferred_element_type=jnp.float32), positions, HD).astype(jnp.bfloat16)
    key_rows = rotate(jnp.dot(normed, w_key, preferred_element_type=jnp.float32), positions, HD).astype(jnp.bfloat16)
    value_rows = jnp.dot(normed, w_value, preferred_element_type=jnp.float32).astype(jnp.bfloat16)
    doc_ends = jnp.cumsum(doc_lengths).astype(jnp.int32)
    doc_ids = doc_index(positions, doc_ends)
    tile_ids = positions // TILE
    per_group = HEADS // KVH
    sink_heads = sinks.reshape(KVH, per_group)
    score_scale = HD ** (-0.5)
    block_rows = math.gcd(L, 512)
    block_count = L // block_rows
    key_heads = jnp.transpose(key_rows.astype(jnp.float32).reshape(L, KVH, HD), (1, 0, 2))
    value_heads = jnp.transpose(value_rows.astype(jnp.float32).reshape(L, KVH, HD), (1, 0, 2))

    def one_block(first_row):
        first_row = first_row.astype(jnp.int32)
        query_pos = first_row + jnp.arange(block_rows, dtype=jnp.int32)
        query_doc = lax.dynamic_slice_in_dim(doc_ids, first_row, block_rows, 0)
        query_tiles = query_pos // TILE
        listed = tile_mask[query_tiles][:, tile_ids] == 1
        same_tile = query_tiles[:, None] == tile_ids[None, :]
        allowed = (query_doc[:, None] == doc_ids[None, :]) & (positions[None, :] <= query_pos[:, None]) & (listed | same_tile)
        query_block = lax.dynamic_slice_in_dim(queries, first_row, block_rows, 0).astype(jnp.float32).reshape(block_rows, KVH, per_group, HD)
        query_heads = jnp.transpose(query_block, (1, 0, 2, 3))

        def one_head(packed):
            query_head, key_head, value_head, sink_logit = packed
            scores = jnp.einsum('qxd,kd->qxk', query_head, key_head) * score_scale
            masked = jnp.where(allowed[:, None, :], scores, -1e+30)
            row_max = jnp.maximum(sink_logit[None, :], lax.optimization_barrier(jnp.max(masked, axis=2)))
            weights = jnp.where(allowed[:, None, :], jnp.exp(masked - row_max[..., None]), 0.0)
            denominator = jnp.exp(sink_logit[None, :] - row_max) + lax.optimization_barrier(jnp.sum(weights, axis=2))
            rounded = lax.optimization_barrier(weights.astype(jnp.bfloat16)).astype(jnp.float32)
            return jnp.einsum('qxk,kd->qxd', rounded, value_head) / denominator[..., None]
        blended = lax.map(one_head, (query_heads, key_heads, value_heads, sink_heads))
        return jnp.transpose(blended, (1, 0, 2, 3)).reshape(block_rows, HEADS * HD).astype(jnp.bfloat16)
    starts = jnp.arange(block_count, dtype=jnp.int32) * block_rows
    outputs = lax.map(one_block, starts)
    return outputs.reshape(L, HEADS * HD)
```

```python
import functools

import jax
import jax.numpy as jnp
from jax import lax
from jax.experimental import pallas as pl
from jax.experimental.pallas import tpu as pltpu
from jax.sharding import PartitionSpec as P

MESH = pl.DeviceIdType.MESH
HD = 64
TILE = 128
ROWS = 256
NT = 128
CH = 4
EPS = 1e-05
ROPE_BASE = 150000.0
BF = jnp.bfloat16
F32 = jnp.float32


def place():
    h = lax.axis_index("head")
    g = lax.axis_index("grp")
    b = lax.axis_index("blk")
    c = g % 2
    y = (g // 2) * 2 + b // 8
    z = b % 8
    return h, g, b, c, y, z


def member(i, low):
    core, half, flip = i // 4, (i // 2) % 2, i % 2
    grp = half * 2 + core
    blk = low * (1 - flip) + (15 - low) * flip
    return grp, blk


def low_of(b):
    flip = b // 8
    return b * (1 - flip) + (15 - b) * flip


def own_member(g, b):
    return (g % 2) * 4 + (g // 2) * 2 + b // 8


def shard_id(yy, zz, core):
    return (yy // 2) * 32 + core * 16 + (yy % 2) * 8 + zz


def turned(x, cos, sin):
    lane = lax.broadcasted_iota(jnp.int32, x.shape, 1)
    other = jnp.where(lane % 64 < 32, pltpu.roll(x, 96, 1), pltpu.roll(x, 32, 1))
    return x * cos + other * sin


def project_kernel(
    tok, gain, cos, sin, wq_hbm, wk_hbm, wv_hbm,
    kv_out, q_out,
    xb, wq, wkv, kvs, qs,
    wsem, xs_sem, xr_sem, ks_sem, kr_sem, ps_sem, qs_sem, qr_sem,
):
    h, g, b, c, y, z = place()
    me = own_member(g, b)
    low = low_of(b)
    feats = tok.shape[1]

    copies_w = [
        pltpu.make_async_copy(wk_hbm, wkv.at[:, 0:128], wsem.at[0]),
        pltpu.make_async_copy(wv_hbm, wkv.at[:, 128:256], wsem.at[1]),
        pltpu.make_async_copy(wq_hbm, wq, wsem.at[2]),
    ]
    for cp in copies_w:
        cp.start()

    def plane(dy, dz):
        yy = (y + dy + 4) % 4
        zz = (z + dz + 8) % 8
        return {"grp": (yy // 2) * 2 + c, "blk": (yy % 2) * 8 + zz}

    partner = {"grp": (g // 2) * 2 + 1 - c}
    barrier = pltpu.get_barrier_semaphore()
    for d in range(1, 4):
        pl.semaphore_signal(barrier, inc=1, device_id={"head": (h + d) % 4}, device_id_type=MESH)
    for dy, dz in ((1, 0), (-1, 0), (0, 1), (0, -1)):
        pl.semaphore_signal(barrier, inc=1, device_id=plane(dy, dz), device_id_type=MESH)
    for d in range(1, 8):
        grp, blk = member((me + d) % 8, low)
        pl.semaphore_signal(barrier, inc=1, device_id={"grp": grp, "blk": blk}, device_id_type=MESH)
    pl.semaphore_wait(barrier, 14)

    sent = []
    for d in (1, 3, 2):
        cp = pltpu.make_async_remote_copy(
            tok, xb.at[h], xs_sem.at[d - 1], xr_sem.at[d - 1],
            device_id={"head": (h + d) % 4}, device_id_type=MESH)
        cp.start()
        sent.append(cp)
    xb[h] = tok[...]
    for cp in sent:
        cp.wait_recv()

    total = jnp.zeros((ROWS, 1), F32)
    for i in range(4):
        w = xb[i].astype(F32)
        total = total + jnp.sum(w * w, axis=1, keepdims=True)
    scale = lax.rsqrt(total / (4 * feats) + EPS)
    for i in range(4):
        w = xb[i].astype(F32) * scale * gain[:, i * feats:(i + 1) * feats]
        xb[i] = w.astype(BF)

    copies_w[0].wait()
    copies_w[1].wait()
    kvp = jnp.zeros((ROWS, 256), F32)
    for i in range(4):
        kvp = kvp + jnp.dot(xb[i], wkv[i * feats:(i + 1) * feats, :], preferred_element_type=F32)
    k = turned(kvp[:, :128], cos[...], sin[...])
    v = kvp[:, 128:]
    lane = lax.broadcasted_iota(jnp.int32, (128, 128), 1)
    k0, k1 = k[:128], k[128:]
    kvs[0, 0:128, :] = jnp.where(lane < 64, k0, pltpu.roll(k1, 64, 1)).astype(BF)
    kvs[1, 0:128, :] = jnp.where(lane < 64, pltpu.roll(k0, 64, 1), k1).astype(BF)
    for e in range(2):
        vt = v[128 * e:128 * (e + 1)].T.astype(BF)
        for cc in range(2):
            kvs[cc, 128 + 64 * e:192 + 64 * e, :] = vt[64 * cc:64 * (cc + 1)]
    own = shard_id(y, z, c)
    other = shard_id(y, z, 1 - c)
    pcopy = pltpu.make_async_remote_copy(
        kvs.at[1 - c], kv_out.at[own], ps_sem, kr_sem.at[own], device_id=partner, device_id_type=MESH)
    pcopy.start()
    kv_out[own] = kvs[c]

    sends = []

    def send(sid, target):
        cp = pltpu.make_async_remote_copy(
            kv_out.at[sid], kv_out.at[sid], ks_sem.at[len(sends)], kr_sem.at[sid],
            device_id=target, device_id_type=MESH)
        cp.start()
        sends.append(cp)

    def arrived(sid):
        pltpu.make_async_remote_copy(
            kv_out.at[sid], kv_out.at[sid], ps_sem, kr_sem.at[sid],
            device_id=partner, device_id_type=MESH).wait_recv()

    def block(dy, dz, core):
        return shard_id((y + dy + 4) % 4, (z + dz + 8) % 8, core)

    arrived(other)
    a0, b0 = block(0, 0, 0), block(0, 0, 1)
    for sid in (a0, b0):
        for dy, dz in ((0, 1), (0, -1), (1, 0), (-1, 0)):
            send(sid, plane(dy, dz))

    copies_w[2].wait()

    def q_block(n, carry):
        acc = jnp.zeros((ROWS, 256), F32)
        cols = pl.ds(pl.multiple_of(n * 256, 256), 256)
        for i in range(4):
            acc = acc + jnp.dot(xb[i], wq[i * feats:(i + 1) * feats, cols], preferred_element_type=F32)
        for u in range(2):
            qs[n * 2 + u] = (turned(acc[:, u * 128:(u + 1) * 128], cos[...], sin[...]) * 0.125).astype(BF)
        return carry

    lax.fori_loop(0, 4, q_block, 0)
    qsent = []
    for d in range(1, 8):
        i = (me + d) % 8
        grp, blk = member(i, low)
        cp = pltpu.make_async_remote_copy(
            qs.at[i], q_out.at[me], qs_sem.at[d - 1], qr_sem.at[d - 1],
            device_id={"grp": grp, "blk": blk}, device_id_type=MESH)
        cp.start()
        qsent.append(cp)
    q_out[me] = qs[me]

    events = []
    for dz in range(-4, 4):
        for dy in (0, -1, 1, 2):
            if (dy, dz) != (0, 0):
                events.append((abs(dz) + abs(dy), 0, dy, dz))
    for dz in range(-3, 5):
        for dy in (0, -1, 1, 2):
            if (dy, dz) != (0, 0):
                events.append((abs(dz) + abs(dy), 1, dy, dz))
    events.sort(key=lambda e: e[0])
    for hops, part, dy, dz in events:
        sid = block(dy, dz, part)
        arrived(sid)
        if part == 0:
            if dy == 0:
                if dz < 0 and dz > -4:
                    send(sid, plane(0, 1))
                if dz > 0 and dz < 3:
                    send(sid, plane(0, -1))
                send(sid, plane(1, 0))
                send(sid, plane(-1, 0))
            elif dy == -1 and dz % 2 == 0:
                send(sid, plane(1, 0))
            elif dy == 1 and dz % 2 == 1:
                send(sid, plane(-1, 0))
        else:
            if dz == 0:
                send(sid, plane(0, 1))
                send(sid, plane(0, -1))
                if dy == 1:
                    sgn = 1 - 2 * c
                    yy = (y - sgn + 4) % 4
                    send(shard_id(yy, z, 1), plane(sgn, 0))
            elif dz > 0 and dz < 4:
                send(sid, plane(0, -1))
            elif dz < 0 and dz > -3:
                send(sid, plane(0, 1))

    for cp in qsent:
        cp.wait_recv()
    for cp in sent + sends + qsent + [pcopy]:
        cp.wait_send()


def attend_kernel(meta, ends, sinks, q_ref, kv_ref, o_ref, qsel):
    lane = lax.broadcasted_iota(jnp.int32, (1, 256), 1)
    sub = lax.broadcasted_iota(jnp.int32, (TILE, 256), 0)
    base = meta[0, 123]
    sink = jnp.where(lane < 128, sinks[base], sinks[base + 1])

    def one_tile(n, carry0):
        m_idx = n // 2
        e = n % 2
        tile = meta[n, 120]
        nch = meta[n, 121]
        nf = meta[n, 122]
        qt = q_ref[m_idx, pl.ds(pl.multiple_of(e * 128, 128), 128), :].astype(F32).T.astype(BF)
        qt = jnp.concatenate([qt[:64], qt[64:]], axis=1)
        zero = jnp.zeros_like(qt)
        qsel[0] = jnp.concatenate([qt, zero], axis=0)
        qsel[1] = jnp.concatenate([zero, qt], axis=0)
        qpos = tile * TILE + lane % 128
        first = jnp.zeros_like(qpos)
        for d in range(12):
            first = jnp.maximum(first, jnp.where(ends[d] <= qpos, ends[d], 0))

        def step(ci, carry, masked):
            mx, den, acc = carry
            parts, vts = [], []
            for u in range(CH):
                j = meta[n, ci * CH + u]
                jj = j % 128
                s = jj // 2
                par = jj % 2
                sc = jnp.dot(kv_ref[s, 0:128, :], qsel[par], preferred_element_type=F32)
                if masked:
                    kpos = sub + j * TILE
                    sc = jnp.where((kpos <= qpos) & (kpos >= first), sc, -1e30)
                parts.append(sc)
                vts.append(kv_ref[s, pl.ds(pl.multiple_of(128 + 64 * par, 64), 64), :])
            sc = jnp.concatenate(parts, axis=0)
            vt = jnp.concatenate(vts, axis=1)
            new = jnp.maximum(mx, jnp.max(sc, axis=0, keepdims=True))
            p = jnp.exp(sc - new)
            alpha = jnp.exp(mx - new)
            den = den * alpha + jnp.sum(p, axis=0, keepdims=True)
            acc = acc * alpha + jnp.dot(vt, p.astype(BF), preferred_element_type=F32)
            return new, den, acc

        carry = (sink, jnp.ones((1, 256), F32), jnp.zeros((64, 256), F32))
        carry = step(0, carry, True)
        carry = lax.fori_loop(1, nf, lambda ci, cr: step(ci, cr, False), carry)
        carry = lax.fori_loop(jnp.maximum(1, nf), nch, lambda ci, cr: step(ci, cr, True), carry)
        _, den, acc = carry
        out = acc / den
        out = jnp.concatenate([out[:, :128], out[:, 128:]], axis=0)
        o_ref[m_idx, pl.ds(pl.multiple_of(e * 128, 128), 128), :] = out.T.astype(BF)
        return carry0

    lax.fori_loop(0, 16, one_tile, 0)


def return_kernel(o_ref, out_ref, s_sem, r_sem):
    h, g, b, c, y, z = place()
    me = own_member(g, b)
    low = low_of(b)
    barrier = pltpu.get_barrier_semaphore()
    for d in range(1, 8):
        grp, blk = member((me + d) % 8, low)
        pl.semaphore_signal(barrier, inc=1, device_id={"grp": grp, "blk": blk}, device_id_type=MESH)
    pl.semaphore_wait(barrier, 7)
    cols = pl.ds(pl.multiple_of(me * 128, 128), 128)
    sent = []
    for d in range(1, 8):
        i = (me + d) % 8
        grp, blk = member(i, low)
        cp = pltpu.make_async_remote_copy(
            o_ref.at[i], out_ref.at[:, cols], s_sem.at[d - 1], r_sem.at[d - 1],
            device_id={"grp": grp, "blk": blk}, device_id_type=MESH)
        cp.start()
        sent.append(cp)
    out_ref[:, cols] = o_ref[me]
    for cp in sent:
        cp.wait()


def key_lists(doc_lengths, tile_mask):
    g = lax.axis_index("grp")
    b = lax.axis_index("blk")
    low = low_of(b)
    i = jnp.arange(16, dtype=jnp.int32) // 2
    e = jnp.arange(16, dtype=jnp.int32) % 2
    grp, blk = member(i, low)
    tile = (grp * 16 + blk) * 2 + e
    ends = jnp.cumsum(doc_lengths).astype(jnp.int32)

    def start_of(p):
        return jnp.max(jnp.where(ends[None, :] <= p[:, None], ends[None, :], 0), axis=1)

    first = start_of(tile * TILE)
    last = start_of(tile * TILE + TILE - 1)
    j = jnp.arange(NT, dtype=jnp.int32)
    pick = (tile[:, None] == j[None, :]).astype(F32)
    rows = jnp.dot(pick, tile_mask.astype(F32), preferred_element_type=F32) > 0.5
    active = (rows | (j[None, :] == tile[:, None])) & (j[None, :] <= tile[:, None]) & (j[None, :] >= (first // TILE)[:, None])
    act = active.astype(F32)
    later = (j[:, None] > j[None, :]).astype(F32)
    behind = jnp.dot(act, later, preferred_element_type=F32).astype(jnp.int32)
    n = jnp.sum(active.astype(jnp.int32), axis=1)
    pad = (CH - n % CH) % CH
    pos = jnp.where(active, behind + pad[:, None], -1)
    hit = pos[:, :, None] == j[None, None, :]
    lists = jnp.sum(jnp.where(hit, j[None, :, None], 0), axis=1)
    lists = jnp.where(j[None, :] < pad[:, None], 128, lists)
    nch = (n + pad) // CH
    nf = jnp.where(first == last, nch - 1, 1)
    me = own_member(g, b)
    for col, val in ((120, tile), (121, nch), (122, nf), (123, jnp.full((16,), me * 2, jnp.int32))):
        lists = jnp.where(j[None, :] == col, val[:, None], lists)
    return lists, ends


def body(tokens, norm_gain, w_query, w_key, w_value, sinks, doc_lengths, tile_mask):
    g = lax.axis_index("grp")
    b = lax.axis_index("blk")
    pos = (g * 16 + b) * ROWS + jnp.arange(ROWS, dtype=jnp.int32)
    half = HD // 2
    freq = ROPE_BASE ** (-2.0 * jnp.arange(half, dtype=F32) / HD)
    ang = pos.astype(F32)[:, None] * freq[None, :]
    cos1, sin1 = jnp.cos(ang), jnp.sin(ang)
    cos = jnp.concatenate([cos1] * 4, axis=1)
    sin = jnp.concatenate([-sin1, sin1, -sin1, sin1], axis=1)
    lists, ends = key_lists(doc_lengths, tile_mask)

    vm = pl.BlockSpec(memory_space=pltpu.VMEM)
    anym = pl.BlockSpec(memory_space=pl.ANY)
    smem = pl.BlockSpec(memory_space=pltpu.SMEM)
    feats = tokens.shape[1]
    dma = pltpu.SemaphoreType.DMA
    kv, q = pl.pallas_call(
        project_kernel,
        out_shape=(jax.ShapeDtypeStruct((64, 256, 128), BF), jax.ShapeDtypeStruct((8, 256, 128), BF)),
        in_specs=[vm, vm, vm, vm, anym, anym, anym],
        out_specs=(vm, vm),
        scratch_shapes=[
            pltpu.VMEM((4, ROWS, feats), BF),
            pltpu.VMEM((4 * feats, 1024), BF),
            pltpu.VMEM((4 * feats, 256), BF),
            pltpu.VMEM((2, 256, 128), BF),
            pltpu.VMEM((8, 256, 128), BF),
            dma((3,)), dma((3,)), dma((3,)), dma((64,)), dma((64,)), dma, dma((7,)), dma((7,)),
        ],
        compiler_params=pltpu.CompilerParams(collective_id=0, has_side_effects=True),
        name="project",
    )(tokens, norm_gain[None, :], cos, sin, w_query, w_key, w_value)
    o = pl.pallas_call(
        attend_kernel,
        out_shape=jax.ShapeDtypeStruct((8, 256, 128), BF),
        in_specs=[smem, smem, smem, vm, vm],
        out_specs=vm,
        scratch_shapes=[pltpu.VMEM((2, 128, 256), BF)],
        name="attend",
    )(lists, ends, sinks, q, kv)
    return pl.pallas_call(
        return_kernel,
        out_shape=jax.ShapeDtypeStruct((ROWS, 1024), BF),
        in_specs=[vm],
        out_specs=vm,
        scratch_shapes=[dma((7,)), dma((7,))],
        compiler_params=pltpu.CompilerParams(collective_id=1, has_side_effects=True),
        name="give_back",
    )(o)


def solution(mesh):
    in_specs = (
        P(("grp", "blk"), "head"),
        P(),
        P(None, "head"),
        P(None, "head"),
        P(None, "head"),
        P("head"),
        P(),
        P(),
    )
    out_specs = P(("grp", "blk"), "head")
    return jax.shard_map(body, mesh=mesh, in_specs=in_specs, out_specs=out_specs, check_vma=False)
```

```python
import functools

import jax
import jax.numpy as jnp
from jax import lax
from jax.experimental import pallas as pl
from jax.experimental.pallas import tpu as pltpu
from jax.sharding import PartitionSpec as P

MESH = pl.DeviceIdType.MESH
HD = 64
TILE = 128
ROWS = 256
NT = 128
CH = 4
EPS = 1e-05
ROPE_BASE = 150000.0
LOG2E = 1.4426950408889634
BF = jnp.bfloat16
F32 = jnp.float32

def place():
    h = lax.axis_index("head")
    g = lax.axis_index("grp")
    b = lax.axis_index("blk")
    c = g % 2
    y = (g // 2) * 2 + b // 8
    z = b % 8
    return h, c, y, z


def device(yy, zz, core):
    return {"grp": (yy // 2) * 2 + core, "blk": (yy % 2) * 8 + zz}


def shard_id(yy, zz, core):
    return (yy // 2) * 32 + core * 16 + (yy % 2) * 8 + zz


def turned(x, cos, sin):
    lane = lax.broadcasted_iota(jnp.int32, x.shape, 1)
    other = jnp.where(lane % 64 < 32, pltpu.roll(x, 96, 1), pltpu.roll(x, 32, 1))
    return x * cos + other * sin


def angles(base):
    lane = lax.broadcasted_iota(jnp.int32, (1, 128), 1)
    freq = jnp.zeros((1, 128), F32)
    for i in range(HD // 2):
        freq = jnp.where(lane % 32 == i, ROPE_BASE ** (-2.0 * i / HD), freq)
    pos = lax.broadcasted_iota(jnp.int32, (ROWS, 128), 0) + base
    ang = pos.astype(F32) * freq
    sin = jnp.sin(ang)
    return jnp.cos(ang), jnp.where(lane % 64 < 32, -sin, sin)


def doc_start(doc_len, pos):
    end = jnp.int32(0)
    first = jnp.zeros_like(pos)
    for d in range(doc_len.shape[0]):
        end = end + doc_len[d]
        first = jnp.maximum(first, jnp.where(end <= pos, end, 0))
    return first


def key_lists(doc_len, tile_mask, z, lists):
    n = lax.broadcasted_iota(jnp.int32, (1, 128), 1)
    i = n // 2
    yy, core = i % 4, i // 4
    tile = shard_id(yy, z, core) * 2 + n % 2
    first = doc_start(doc_len, tile * TILE)
    last = doc_start(doc_len, tile * TILE + TILE - 1)
    j = lax.broadcasted_iota(jnp.int32, (NT, 128), 0)
    k = lax.broadcasted_iota(jnp.int32, (NT, 128), 1)
    pick = jnp.where(j == tile, 1.0, 0.0).astype(BF)
    listed = jnp.dot(tile_mask[...].astype(F32).T.astype(BF), pick, preferred_element_type=F32) > 0.5
    active = (listed | (j == tile)) & (j <= tile) & (j * TILE + TILE > first)
    act = jnp.where(active, 1.0, 0.0).astype(BF)
    lower = jnp.where(k < j, 1.0, 0.0).astype(BF)
    before = jnp.dot(lower, act, preferred_element_type=F32).astype(jnp.int32)
    spot = jnp.where(active, jnp.where(j == tile, 0, before + 1), -1)
    count = jnp.sum(jnp.where(active, 1, 0), axis=0, keepdims=True)
    for r in range(16):
        hit = spot[:, r:r + 1] == k
        lists[r:r + 1, :] = jnp.sum(jnp.where(hit, j - NT, 0), axis=0, keepdims=True) + NT
    lists[16:17, :] = tile
    lists[17:18, :] = (count + CH - 1) // CH
    lists[18:19, :] = jnp.where(first == last, 0, 1)
    lists[19:24, :] = jnp.zeros((5, 128), jnp.int32)


def project_kernel(
    doc_len, tok_hbm, gain_hbm, mask_hbm, wq_hbm, wk_hbm, wv_hbm,
    kk_out, vt_out, q_out, lists,
    xb, gain, mask, wq, wkv, kvs, kvb, qs,
    wsem, xs_sem, xr_sem, ks_sem, kr_sem, ps_sem, qs_sem, qr_sem,
):
    h, c, y, z = place()
    me = c * 4 + y
    feats = xb.shape[2]
    half = ROWS // 2

    copies = [
        pltpu.make_async_copy(tok_hbm, xb.at[h], wsem.at[0]),
        pltpu.make_async_copy(gain_hbm, gain.at[0], wsem.at[1]),
        pltpu.make_async_copy(mask_hbm, mask, wsem.at[2]),
        pltpu.make_async_copy(wk_hbm, wkv.at[:, 0:128], wsem.at[3]),
        pltpu.make_async_copy(wv_hbm, wkv.at[:, 128:256], wsem.at[4]),
        pltpu.make_async_copy(wq_hbm, wq, wsem.at[5]),
    ]
    for cp in copies:
        cp.start()

    def plane(dy, dz):
        return device((y + dy + 4) % 4, (z + dz + 8) % 8, c)

    def mate(d):
        i = (me + d) % 8
        return i, device(i % 4, z, i // 4)

    partner = device(y, z, 1 - c)
    ahead, behind, across = (h + 1) % 4, (h + 3) % 4, (h + 2) % 4
    barrier = pltpu.get_barrier_semaphore()
    for x in (ahead, behind):
        pl.semaphore_signal(barrier, inc=1, device_id={"head": x}, device_id_type=MESH)
    for dz in (1, -1):
        pl.semaphore_signal(barrier, inc=1, device_id=plane(0, dz), device_id_type=MESH)
    for d in range(1, 8):
        pl.semaphore_signal(barrier, inc=1, device_id=mate(d)[1], device_id_type=MESH)
    pl.semaphore_wait(barrier, 11)
    copies[0].wait()

    xsent = []
    top, low = pl.ds(0, half), pl.ds(half, half)

    def xsend(n, src, rows, to):
        cp = pltpu.make_async_remote_copy(
            xb.at[src, rows], xb.at[src, rows], xs_sem.at[n], xr_sem.at[n],
            device_id={"head": to}, device_id_type=MESH)
        cp.start()
        xsent.append(cp)

    def xwait(n, src, rows):
        pltpu.make_async_remote_copy(
            xb.at[src, rows], xb.at[src, rows], xs_sem.at[n], xr_sem.at[n],
            device_id={"head": ahead}, device_id_type=MESH).wait_recv()

    xsend(0, h, top, ahead)
    xsend(1, h, low, behind)
    xsend(2, h, low, ahead)
    xsend(3, h, top, behind)
    cos, sin = angles(shard_id(y, z, c) * ROWS)
    xwait(0, behind, top)
    xsend(4, behind, top, ahead)
    xwait(1, ahead, low)
    xsend(5, ahead, low, behind)

    copies[2].wait()
    key_lists(doc_len, mask, z, lists)
    kk_out[NT] = jnp.zeros((TILE, 128), BF)
    vt_out[NT] = jnp.zeros((80, 128), BF)
    copies[1].wait()

    def squares(i):
        w = xb[i].astype(F32)
        return jnp.sum(w * w, axis=1, keepdims=True)

    total = squares(h)
    xwait(2, behind, low)
    total = total + squares(behind)
    xwait(3, ahead, top)
    total = total + squares(ahead)
    xwait(4, across, top)
    xwait(5, across, low)
    total = total + squares(across)
    scale = lax.rsqrt(total / (4 * feats) + EPS)
    for cp in xsent:
        cp.wait_send()
    copies[3].wait()
    copies[4].wait()
    kvp = jnp.zeros((ROWS, 256), F32)
    for i in range(4):
        w = xb[i].astype(F32) * scale * gain[:, i * feats:(i + 1) * feats]
        w = w.astype(BF)
        xb[i] = w
        kvp = kvp + jnp.dot(w, wkv[i * feats:(i + 1) * feats, :], preferred_element_type=F32)
    k = turned(kvp[:, :128], cos, sin)
    v = kvp[:, 128:]
    lane = lax.broadcasted_iota(jnp.int32, (64, 128), 1)
    for e in range(2):
        k0, k1 = k[128 * e:128 * e + 64], k[128 * e + 64:128 * e + 128]
        vt = v[128 * e:128 * (e + 1)].T.astype(BF)
        kvs[0, 128 * e:128 * e + 64, :] = jnp.where(lane < 64, k0, pltpu.roll(k1, 64, 1)).astype(BF)
        kvs[1, 128 * e:128 * e + 64, :] = jnp.where(lane < 64, pltpu.roll(k0, 64, 1), k1).astype(BF)
        for cc in range(2):
            kvs[cc, 128 * e + 64:128 * e + 128, :] = vt[64 * cc:64 * (cc + 1)]
    own = shard_id(y, z, c)
    other = shard_id(y, z, 1 - c)
    pcopy = pltpu.make_async_remote_copy(
        kvs.at[1 - c], kvb.at[own], ps_sem, kr_sem.at[own], device_id=partner, device_id_type=MESH)
    pcopy.start()
    kvb[own] = kvs[c]

    sends = []

    def send(sid, target):
        cp = pltpu.make_async_remote_copy(
            kvb.at[sid], kvb.at[sid], ks_sem.at[len(sends)], kr_sem.at[sid],
            device_id=target, device_id_type=MESH)
        cp.start()
        sends.append(cp)

    def arrived(sid):
        pltpu.make_async_remote_copy(
            kvb.at[sid], kvb.at[sid], ps_sem, kr_sem.at[sid],
            device_id=partner, device_id_type=MESH).wait_recv()

    def unpack(sid):
        for e in range(2):
            k2 = kvb[sid, 128 * e:128 * e + 64, :].astype(F32)
            r2 = pltpu.roll(k2, 64, 1)
            kk_out[sid * 2 + e, 0:64, :] = jnp.where(lane < 64, k2, r2).astype(BF)
            kk_out[sid * 2 + e, 64:128, :] = jnp.where(lane < 64, r2, k2).astype(BF)
            vt_out[sid * 2 + e, 0:64, :] = kvb[sid, 128 * e + 64:128 * e + 128, :]
            vt_out[sid * 2 + e, 64:80, :] = jnp.ones((16, 128), BF)

    def block(dy, dz, core):
        return shard_id((y + dy + 4) % 4, (z + dz + 8) % 8, core)

    def q_block(n):
        acc = jnp.zeros((ROWS, 256), F32)
        for i in range(4):
            acc = acc + jnp.dot(
                xb[i], wq[i * feats:(i + 1) * feats, n * 256:(n + 1) * 256], preferred_element_type=F32)
        for u in range(2):
            qs[n * 2 + u] = (turned(acc[:, u * 128:(u + 1) * 128], cos, sin) * 0.125).astype(BF)

    for sid in (own, other):
        if sid is other:
            arrived(other)
        for dy, dz in ((0, 1), (0, -1), (1, 0), (-1, 0)):
            send(sid, plane(dy, dz))

    events = []
    for dz in range(-4, 4):
        for dy in (0, -1, 1, 2):
            if (dy, dz) != (0, 0):
                events.append((abs(dz) + abs(dy), 0, dy, dz))
    for dz in range(-3, 5):
        for dy in (0, -1, 1, 2):
            if (dy, dz) != (0, 0):
                events.append((abs(dz) + abs(dy), 1, dy, dz))
    events.sort(key=lambda e: e[0])

    copies[5].wait()
    q_block(0)
    qsent = []
    fresh = [own, other]
    for at, (hops, part, dy, dz) in enumerate(events):
        sid = block(dy, dz, part)
        arrived(sid)
        if part == 0:
            if dy == 0:
                if dz < 0 and dz > -4:
                    send(sid, plane(0, 1))
                if dz > 0 and dz < 3:
                    send(sid, plane(0, -1))
                send(sid, plane(1, 0))
                send(sid, plane(-1, 0))
            elif dy == -1 and dz % 2 == 0:
                send(sid, plane(1, 0))
            elif dy == 1 and dz % 2 == 1:
                send(sid, plane(-1, 0))
        else:
            if dz == 0:
                send(sid, plane(0, 1))
                send(sid, plane(0, -1))
                if dy == 1:
                    sgn = 1 - 2 * c
                    send(shard_id((y - sgn + 4) % 4, z, 1), plane(sgn, 0))
            elif dz > 0 and dz < 4:
                send(sid, plane(0, -1))
            elif dz < 0 and dz > -3:
                send(sid, plane(0, 1))
        fresh.append(sid)
        nexthop = events[at + 1][0] if at + 1 < len(events) else 99
        if nexthop != hops:
            if hops == 1:
                q_block(1)
                q_block(2)
            if hops == 2:
                q_block(3)
                for d in range(1, 8):
                    i, target = mate(d)
                    cp = pltpu.make_async_remote_copy(
                        qs.at[i], q_out.at[me], qs_sem.at[d - 1], qr_sem.at[d - 1],
                        device_id=target, device_id_type=MESH)
                    cp.start()
                    qsent.append(cp)
                q_out[me] = qs[me]
            if hops > 2:
                for s in fresh:
                    unpack(s)
                fresh = []
    for cp in qsent:
        cp.wait_recv()
    for cp in sends + qsent + [pcopy]:
        cp.wait_send()


def attend_kernel(meta, doc_len, sinks, q_ref, kk_ref, vt_ref, o_ref, qsel, mref, aref, buf0, buf1, buf2, buf3, steps):
    bufs = ((buf0, buf1), (buf2, buf3))
    _, c, y, _ = place()
    base = (c * 4 + y) * 2
    lane = lax.broadcasted_iota(jnp.int32, (1, 256), 1)
    sub = lax.broadcasted_iota(jnp.int32, (TILE, 256), 0)
    sink = jnp.where(lane < 128, sinks[base], sinks[base + 1]) * LOG2E

    def prep(n4, cr):
        for u in range(4):
            n = n4 * 4 + u
            qt = (q_ref[n >> 1, 128 * (u & 1):128 * (u & 1) + 128, :].astype(F32) * LOG2E).T
            qt = jnp.concatenate([qt[:64], qt[64:]], axis=1)
            hi = qt.astype(BF)
            lo = (qt - hi.astype(F32)).astype(BF)
            qsel[n] = jnp.concatenate([hi, lo], axis=0)
        return cr

    lax.fori_loop(0, 4, prep, 0)

    def clear(n, cr):
        mref[n] = sink
        aref[n] = jnp.concatenate([jnp.zeros((64, 256), F32), jnp.ones((16, 256), F32)], axis=0)
        return cr

    lax.fori_loop(0, 18, clear, 0)

    counts = []
    for s in range(2):
        def add(i, cr):
            n = i * 2 + s
            nch = meta[17, n]
            multi = meta[18, n]
            c0, c1, c2 = cr
            single = 1 - multi
            steps[s * 4 + multi * 3, c0] = n << 7

            def put(ci, cc):
                a, m = cc
                steps[s * 4 + 1 + multi, jnp.where(multi == 1, m, a)] = (n << 7) + ci * CH
                return a + single, m + multi

            c1, c2 = lax.fori_loop(single, nch, put, (c1, c2))
            return c0 + single, c1, c2

        z0 = jnp.int32(0)
        counts.append(lax.fori_loop(0, 8, add, (z0, z0, z0)))
    totals = []
    for kind in range(3):
        mx = jnp.maximum(counts[0][kind], counts[1][kind])
        if kind < 2:
            mx = (mx + 1) & ~1
        for s in range(2):
            def fill(k, cr):
                steps[s * 4 + kind, k] = (16 + s) << 7
                return cr
            lax.fori_loop(counts[s][kind], mx + 1, fill, 0)
        totals.append(mx)

    def scores(s, kind, k):
        w = steps[s * 4 + kind, k]
        nn = (w >> 7) & 15
        c0 = w & 127
        ks = [kk_ref[meta[nn, c0 + u]] for u in range(CH)]
        return jnp.dot(jnp.concatenate(ks, axis=0), qsel[nn], preferred_element_type=F32)

    def absorb(s, kind, k, sc):
        w = steps[s * 4 + kind, k]
        n = w >> 7
        nn = n & 15
        c0 = w & 127
        js = [meta[nn, c0 + u] for u in range(CH)]
        vt = jnp.concatenate([vt_ref[js[u]] for u in range(CH)], axis=1)
        if kind != 1:
            qpos = meta[16, nn] * TILE + (lane & 127)
            first = doc_start(doc_len, qpos)
            parts = []
            for u in range(CH):
                part = sc[u * 128:(u + 1) * 128]
                off = js[u] * TILE
                if kind == 2 or u == 0:
                    part = jnp.where((sub <= qpos - off) & (sub >= first - off), part, -1e30)
                elif u == 1:
                    part = jnp.where(sub >= first - off, part, -1e30)
                parts.append(part)
            sc = jnp.concatenate(parts, axis=0)
        mx = mref[n]
        new = jnp.maximum(mx, jnp.max(sc, axis=0, keepdims=True))
        p = jnp.exp2(sc - new).astype(BF)
        alpha = jnp.exp2(mx - new)
        mref[n] = new
        aref[n] = aref[n] * alpha + jnp.dot(vt, p, preferred_element_type=F32)

    for kind in range(2):
        for s in range(2):
            bufs[s][0][...] = scores(s, kind, 0)

        def it(k2, cr):
            for ph in range(2):
                k = k2 * 2 + ph
                for s in range(2):
                    bufs[s][1 - ph][...] = scores(s, kind, k + 1)
                    absorb(s, kind, k, bufs[s][ph][...])
            return cr

        lax.fori_loop(0, totals[kind] >> 1, it, 0)

    def full(k, cr):
        for s in range(2):
            absorb(s, 2, k, scores(s, 2, k))
        return cr

    lax.fori_loop(0, totals[2], full, 0)

    def fin(n2, cr):
        for u in range(2):
            a = aref[n2 * 2 + u]
            out = a[:64] / a[64:65]
            out = jnp.concatenate([out[:, :128], out[:, 128:]], axis=0)
            o_ref[n2, 128 * u:128 * u + 128, :] = out.T.astype(BF)
        return cr

    lax.fori_loop(0, 8, fin, 0)


def return_kernel(o_ref, out_ref, s_sem, r_sem):
    h, c, y, z = place()
    me = c * 4 + y
    barrier = pltpu.get_barrier_semaphore()

    def mate(d):
        i = (me + d) % 8
        return i, device(i % 4, z, i // 4)

    for d in range(1, 8):
        pl.semaphore_signal(barrier, inc=1, device_id=mate(d)[1], device_id_type=MESH)
    pl.semaphore_wait(barrier, 7)
    cols = pl.ds(pl.multiple_of(me * 128, 128), 128)
    sent = []
    for d in range(1, 8):
        i, target = mate(d)
        cp = pltpu.make_async_remote_copy(
            o_ref.at[i], out_ref.at[:, cols], s_sem.at[d - 1], r_sem.at[d - 1],
            device_id=target, device_id_type=MESH)
        cp.start()
        sent.append(cp)
    out_ref[:, cols] = o_ref[me]
    for cp in sent:
        cp.wait()


def body(tokens, norm_gain, w_query, w_key, w_value, sinks, doc_lengths, tile_mask):
    vm = pl.BlockSpec(memory_space=pltpu.VMEM)
    anym = pl.BlockSpec(memory_space=pl.ANY)
    smem = pl.BlockSpec(memory_space=pltpu.SMEM)
    feats = tokens.shape[1]
    dma = pltpu.SemaphoreType.DMA
    kk, vt, q, lists = pl.pallas_call(
        project_kernel,
        out_shape=(
            jax.ShapeDtypeStruct((NT + 1, TILE, 128), BF),
            jax.ShapeDtypeStruct((NT + 1, 80, 128), BF),
            jax.ShapeDtypeStruct((8, ROWS, 128), BF),
            jax.ShapeDtypeStruct((24, 128), jnp.int32),
        ),
        in_specs=[smem] + [anym] * 6,
        out_specs=(vm, vm, vm, vm),
        scratch_shapes=[
            pltpu.VMEM((4, ROWS, feats), BF),
            pltpu.VMEM((1, 4 * feats), F32),
            pltpu.VMEM((NT, NT), jnp.int32),
            pltpu.VMEM((4 * feats, 1024), BF),
            pltpu.VMEM((4 * feats, 256), BF),
            pltpu.VMEM((2, ROWS, 128), BF),
            pltpu.VMEM((64, ROWS, 128), BF),
            pltpu.VMEM((8, ROWS, 128), BF),
            dma((6,)), dma((6,)), dma((6,)), dma((64,)), dma((64,)), dma, dma((7,)), dma((7,)),
        ],
        compiler_params=pltpu.CompilerParams(collective_id=0, has_side_effects=True),
        name="project",
    )(doc_lengths, tokens, norm_gain, tile_mask, w_query, w_key, w_value)
    o = pl.pallas_call(
        attend_kernel,
        out_shape=jax.ShapeDtypeStruct((8, ROWS, 128), BF),
        in_specs=[smem, smem, smem, vm, vm, vm],
        out_specs=vm,
        scratch_shapes=[
            pltpu.VMEM((16, 128, 256), BF),
            pltpu.VMEM((18, 1, 256), F32),
            pltpu.VMEM((18, 80, 256), F32),
        ] + [pltpu.VMEM((CH * TILE, 256), F32)] * 4 + [pltpu.SMEM((8, 256), jnp.int32)],
        name="attend",
    )(lists, doc_lengths, sinks, q, kk, vt)
    return pl.pallas_call(
        return_kernel,
        out_shape=jax.ShapeDtypeStruct((ROWS, 1024), BF),
        in_specs=[vm],
        out_specs=vm,
        scratch_shapes=[dma((7,)), dma((7,))],
        compiler_params=pltpu.CompilerParams(collective_id=1, has_side_effects=True),
        name="give_back",
    )(o)


def solution(mesh):
    in_specs = (
        P(("grp", "blk"), "head"),
        P(),
        P(None, "head"),
        P(None, "head"),
        P(None, "head"),
        P("head"),
        P(),
        P(),
    )
    out_specs = P(("grp", "blk"), "head")
    return jax.shard_map(body, mesh=mesh, in_specs=in_specs, out_specs=out_specs, check_vma=False)
```

```python
import functools

import jax
import jax.numpy as jnp
from jax import lax
from jax.experimental import pallas as pl
from jax.experimental.pallas import tpu as pltpu
from jax.sharding import PartitionSpec as P

MESH = pl.DeviceIdType.MESH
HD = 64
TILE = 128
ROWS = 256
NT = 128
CH = 4
EPS = 1e-05
ROPE_BASE = 150000.0
LOG2E = 1.4426950408889634
ORDER = (
    (0, -1, 0),
    (0, 0, -1),
    (0, 0, 1),
    (0, 1, 0),
    (1, -1, 0),
    (1, 0, -1),
    (1, 0, 1),
    (1, 1, 0),
    (0, 0, -2),
    (0, 0, 2),
    (0, 1, -1),
    (0, 2, 0),
    (0, -1, -1),
    (0, 1, 1),
    (1, -1, -1),
    (1, -1, 1),
    (0, -1, 1),
    (1, 0, -2),
    (1, 0, 2),
    (0, 1, -2),
    (1, 1, -1),
    (1, 1, 1),
    (1, 2, 0),
    (0, 1, 2),
    (0, -1, -2),
    (0, 0, -3),
    (0, 0, 3),
    (0, 2, -1),
    (0, -1, 2),
    (1, -1, -2),
    (1, -1, 2),
    (0, 2, 1),
    (1, 0, -3),
    (1, 0, 3),
    (0, 1, -3),
    (0, 2, -2),
    (1, 1, -2),
    (1, 1, 2),
    (0, -1, -3),
    (0, 1, 3),
    (1, 2, -1),
    (1, 2, 1),
    (0, -1, 3),
    (0, 2, -3),
    (0, 0, -4),
    (1, -1, 3),
    (0, 2, 2),
    (0, 2, 3),
    (1, -1, -3),
    (1, 1, 3),
    (1, 0, -4),
    (1, 2, 2),
    (0, -1, -4),
    (0, 1, -4),
    (1, 1, -3),
    (1, 1, 4),
    (1, 2, -2),
    (1, 2, 3),
    (0, 2, -4),
    (1, -1, -4),
    (1, 2, -3),
    (1, 2, 4),
)
BF = jnp.bfloat16
F32 = jnp.float32

def place():
    h = lax.axis_index("head")
    g = lax.axis_index("grp")
    b = lax.axis_index("blk")
    c = g % 2
    y = (g // 2) * 2 + b // 8
    z = b % 8
    return h, c, y, z


def device(yy, zz, core):
    return {"grp": (yy // 2) * 2 + core, "blk": (yy % 2) * 8 + zz}


def shard_id(yy, zz, core):
    return (yy // 2) * 32 + core * 16 + (yy % 2) * 8 + zz


class Swap:
    def __init__(self, src, dst, relay, sems, c, y, z):
        self.src, self.dst, self.relay = src, dst, relay
        self.s_sem, self.r_sem, self.q_sem = sems
        self.c, self.y, self.z = c, y, z
        self.me = c * 4 + y
        self.up, self.down, self.far = (y + 1) % 4, (y + 3) % 4, (y + 2) % 4
        self.sent = []

    def go(self, src, dst, r_sem, target):
        cp = pltpu.make_async_remote_copy(
            src, dst, self.s_sem.at[len(self.sent)], r_sem, device_id=target, device_id_type=MESH)
        cp.start()
        self.sent.append(cp)

    def await_at(self, dst, r_sem):
        pltpu.make_async_remote_copy(
            dst, dst, self.s_sem.at[0], r_sem,
            device_id=device(self.y, self.z, 1 - self.c), device_id_type=MESH).wait_recv()

    def start(self):
        c, z, me = self.c, self.z, self.me
        self.go(self.src(self.far), self.relay.at[0], self.q_sem.at[0], device(self.up, z, c))
        self.go(self.src(4 + self.far), self.relay.at[1], self.q_sem.at[1], device(self.down, z, c))
        for core in range(2):
            self.go(self.src(core * 4 + self.up), self.dst(me), self.r_sem.at[me], device(self.up, z, core))
            self.go(self.src(core * 4 + self.down), self.dst(me), self.r_sem.at[me], device(self.down, z, core))
        self.go(self.src((1 - c) * 4 + self.y), self.dst(me), self.r_sem.at[me], device(self.y, z, 1 - c))

    def forward(self):
        c, z = self.c, self.z
        below, above = c * 4 + self.down, c * 4 + self.up
        self.await_at(self.relay.at[0], self.q_sem.at[0])
        self.go(self.relay.at[0], self.dst(below), self.r_sem.at[below], device(self.up, z, 0))
        self.await_at(self.relay.at[1], self.q_sem.at[1])
        self.go(self.relay.at[1], self.dst(above), self.r_sem.at[above], device(self.down, z, 1))

    def finish(self):
        for d in range(1, 8):
            i = (self.me + d) % 8
            self.await_at(self.dst(i), self.r_sem.at[i])
        for cp in self.sent:
            cp.wait_send()


def turned(x, cos, sin):
    lane = lax.broadcasted_iota(jnp.int32, x.shape, 1)
    other = jnp.where(lane % 64 < 32, pltpu.roll(x, 96, 1), pltpu.roll(x, 32, 1))
    return x * cos + other * sin


def angles(base):
    lane = lax.broadcasted_iota(jnp.int32, (1, 128), 1)
    freq = jnp.zeros((1, 128), F32)
    for i in range(HD // 2):
        freq = jnp.where(lane % 32 == i, ROPE_BASE ** (-2.0 * i / HD), freq)
    pos = lax.broadcasted_iota(jnp.int32, (ROWS, 128), 0) + base
    ang = pos.astype(F32) * freq
    sin = jnp.sin(ang)
    return jnp.cos(ang), jnp.where(lane % 64 < 32, -sin, sin)


def doc_start(doc_len, pos):
    end = jnp.int32(0)
    first = jnp.zeros_like(pos)
    for d in range(doc_len.shape[0]):
        end = end + doc_len[d]
        first = jnp.maximum(first, jnp.where(end <= pos, end, 0))
    return first


def key_lists(doc_len, tile_mask, z, lists):
    n = lax.broadcasted_iota(jnp.int32, (1, 128), 1)
    i = n // 2
    yy, core = i % 4, i // 4
    tile = shard_id(yy, z, core) * 2 + n % 2
    first = doc_start(doc_len, tile * TILE)
    last = doc_start(doc_len, tile * TILE + TILE - 1)
    j = lax.broadcasted_iota(jnp.int32, (NT, 128), 0)
    k = lax.broadcasted_iota(jnp.int32, (NT, 128), 1)
    pick = jnp.where(j == tile, 1.0, 0.0).astype(BF)
    listed = jnp.dot(tile_mask[...].astype(F32).T.astype(BF), pick, preferred_element_type=F32) > 0.5
    active = (listed | (j == tile)) & (j <= tile) & (j * TILE + TILE > first)
    act = jnp.where(active, 1.0, 0.0).astype(BF)
    lower = jnp.where(k < j, 1.0, 0.0).astype(BF)
    before = jnp.dot(lower, act, preferred_element_type=F32).astype(jnp.int32)
    spot = jnp.where(active, jnp.where(j == tile, 0, before + 1), -1)
    count = jnp.sum(jnp.where(active, 1, 0), axis=0, keepdims=True)
    for r in range(16):
        hit = spot[:, r:r + 1] == k
        lists[r:r + 1, :] = jnp.sum(jnp.where(hit, j - NT, 0), axis=0, keepdims=True) + NT
    lists[16:17, :] = tile
    lists[17:18, :] = (count + CH - 1) // CH
    lists[18:19, :] = jnp.where(first == last, 0, 1)
    lists[19:24, :] = jnp.zeros((5, 128), jnp.int32)


def project_kernel(
    doc_len, tok_hbm, gain_hbm, mask_hbm, wq_hbm, wk_hbm, wv_hbm,
    kv_out, q_out, lists,
    xt, xb, gain, mask, wq, wkv, kvs, kvb, kvu, qs, relay,
    wsem, xs_sem, xr_sem, ks_sem, kr_sem, ps_sem, us_sem, qs_sem, qr_sem, qq_sem,
):
    h, c, y, z = place()
    me = c * 4 + y
    feats = xb.shape[2]
    half = ROWS // 2

    copies = [
        pltpu.make_async_copy(tok_hbm, xt.at[h], wsem.at[0]),
        pltpu.make_async_copy(gain_hbm, gain.at[0], wsem.at[1]),
        pltpu.make_async_copy(mask_hbm, mask, wsem.at[2]),
        pltpu.make_async_copy(wk_hbm, wkv.at[:, 0:128], wsem.at[3]),
        pltpu.make_async_copy(wv_hbm, wkv.at[:, 128:256], wsem.at[4]),
        pltpu.make_async_copy(wq_hbm, wq, wsem.at[5]),
    ]
    for cp in copies:
        cp.start()

    def plane(dy, dz):
        return device((y + dy + 4) % 4, (z + dz + 8) % 8, c)

    def mate(d):
        i = (me + d) % 8
        return i, device(i % 4, z, i // 4)

    partner = device(y, z, 1 - c)
    ahead, behind, across = (h + 1) % 4, (h + 3) % 4, (h + 2) % 4
    barrier = pltpu.get_barrier_semaphore()
    for x in (ahead, behind):
        pl.semaphore_signal(barrier, inc=1, device_id={"head": x}, device_id_type=MESH)
    for dz in (1, -1):
        pl.semaphore_signal(barrier, inc=1, device_id=plane(0, dz), device_id_type=MESH)
    for d in range(1, 8):
        pl.semaphore_signal(barrier, inc=1, device_id=mate(d)[1], device_id_type=MESH)
    pl.semaphore_wait(barrier, 11)
    copies[0].wait()

    xsent = []
    top, low = pl.ds(0, half), pl.ds(half, half)

    def xsend(n, src, rows, to):
        cp = pltpu.make_async_remote_copy(
            xt.at[src, :, rows], xt.at[src, :, rows], xs_sem.at[n], xr_sem.at[n],
            device_id={"head": to}, device_id_type=MESH)
        cp.start()
        xsent.append(cp)

    def xwait(n, src, rows):
        pltpu.make_async_remote_copy(
            xt.at[src, :, rows], xt.at[src, :, rows], xs_sem.at[n], xr_sem.at[n],
            device_id={"head": ahead}, device_id_type=MESH).wait_recv()

    xsend(0, h, top, ahead)
    xsend(1, h, low, behind)
    xsend(2, h, low, ahead)
    xsend(3, h, top, behind)
    cos, sin = angles(shard_id(y, z, c) * ROWS)
    xwait(0, behind, top)
    xsend(4, behind, top, ahead)
    xwait(1, ahead, low)
    xsend(5, ahead, low, behind)

    copies[2].wait()
    key_lists(doc_len, mask, z, lists)
    kvu[64] = jnp.zeros((2, 208, 128), BF)
    copies[1].wait()

    def squares(i):
        w = xt[i].astype(F32).T
        xb[i] = w.astype(BF)
        return jnp.sum(w * w, axis=1, keepdims=True)

    total = squares(h)
    xwait(2, behind, low)
    total = total + squares(behind)
    xwait(3, ahead, top)
    total = total + squares(ahead)
    xwait(4, across, top)
    xwait(5, across, low)
    total = total + squares(across)
    scale = lax.rsqrt(total / (4 * feats) + EPS)
    for cp in xsent:
        cp.wait_send()
    copies[3].wait()
    copies[4].wait()
    kvp = jnp.zeros((ROWS, 256), F32)
    for i in range(4):
        w = xb[i].astype(F32) * scale * gain[:, i * feats:(i + 1) * feats]
        w = w.astype(BF)
        xb[i] = w
        kvp = kvp + jnp.dot(w, wkv[i * feats:(i + 1) * feats, :], preferred_element_type=F32)
    k = turned(kvp[:, :128], cos, sin)
    v = kvp[:, 128:]
    lane = lax.broadcasted_iota(jnp.int32, (64, 128), 1)
    for e in range(2):
        k0, k1 = k[128 * e:128 * e + 64], k[128 * e + 64:128 * e + 128]
        vt = v[128 * e:128 * (e + 1)].T.astype(BF)
        kvs[0, 128 * e:128 * e + 64, :] = jnp.where(lane < 64, k0, pltpu.roll(k1, 64, 1)).astype(BF)
        kvs[1, 128 * e:128 * e + 64, :] = jnp.where(lane < 64, pltpu.roll(k0, 64, 1), k1).astype(BF)
        for cc in range(2):
            kvs[cc, 128 * e + 64:128 * e + 128, :] = vt[64 * cc:64 * (cc + 1)]
    own = shard_id(y, z, c)
    other = shard_id(y, z, 1 - c)
    pcopy = pltpu.make_async_remote_copy(
        kvs.at[1 - c], kvb.at[own], ps_sem, kr_sem.at[own], device_id=partner, device_id_type=MESH)
    pcopy.start()
    kvb[own] = kvs[c]

    sends, outs = [], []
    null = pltpu.make_async_copy(kvu.at[64], kv_out.at[64], us_sem.at[64])
    null.start()
    outs.append(null)

    def send(sid, target):
        cp = pltpu.make_async_remote_copy(
            kvb.at[sid], kvb.at[sid], ks_sem.at[len(sends)], kr_sem.at[sid],
            device_id=target, device_id_type=MESH)
        cp.start()
        sends.append(cp)

    def arrived(sid):
        pltpu.make_async_remote_copy(
            kvb.at[sid], kvb.at[sid], ps_sem, kr_sem.at[sid],
            device_id=partner, device_id_type=MESH).wait_recv()

    def unpack(sid):
        for e in range(2):
            k2 = kvb[sid, 128 * e:128 * e + 64, :].astype(F32)
            r2 = pltpu.roll(k2, 64, 1)
            kvu[sid, e, 0:64, :] = jnp.where(lane < 64, k2, r2).astype(BF)
            kvu[sid, e, 64:128, :] = jnp.where(lane < 64, r2, k2).astype(BF)
            kvu[sid, e, 128:192, :] = kvb[sid, 128 * e + 64:128 * e + 128, :]
            kvu[sid, e, 192:208, :] = jnp.ones((16, 128), BF)
        cp = pltpu.make_async_copy(kvu.at[sid], kv_out.at[sid], us_sem.at[sid])
        cp.start()
        outs.append(cp)

    def block(dy, dz, core):
        return shard_id((y + dy + 4) % 4, (z + dz + 8) % 8, core)

    def q_block(n):
        acc = jnp.zeros((ROWS, 256), F32)
        for i in range(4):
            acc = acc + jnp.dot(
                xb[i], wq[i * feats:(i + 1) * feats, n * 256:(n + 1) * 256], preferred_element_type=F32)
        for u in range(2):
            qs[n * 2 + u] = (turned(acc[:, u * 128:(u + 1) * 128], cos, sin) * 0.125).astype(BF)

    for sid in (own, other):
        if sid is other:
            arrived(other)
        for dy, dz in ((0, 1), (0, -1), (1, 0), (-1, 0)):
            send(sid, plane(dy, dz))

    swap = Swap(lambda i: qs.at[i], lambda m: q_out.at[m], relay, (qs_sem, qr_sem, qq_sem), c, y, z)
    copies[5].wait()
    q_block(0)
    fresh = [own, other]
    seen = set()
    for at, (part, dy, dz) in enumerate(ORDER):
        sid = block(dy, dz, part)
        arrived(sid)
        seen.add((part, dy, dz))
        low_z, high_z = (-4, 3) if part == 0 or dy in (0, -1) else (-3, 4)
        if part == 1 or dy == 0:
            if dz <= 0 and dz > low_z:
                send(sid, plane(0, 1))
            if dz >= 0 and dz < high_z:
                send(sid, plane(0, -1))
        if part == 0:
            if dy == 0:
                send(sid, plane(1, 0))
                send(sid, plane(-1, 0))
            elif dy == -1 and dz % 2 == 0:
                send(sid, plane(1, 0))
            elif dy == 1 and dz % 2 == 1:
                send(sid, plane(-1, 0))
        elif dz == 0 and dy in (1, -1) and (1, -dy, 0) in seen:
            sgn = 1 - 2 * c
            send(shard_id((y - sgn + 4) % 4, z, 1), plane(sgn, 0))
        fresh.append(sid)
        if at == 5:
            q_block(1)
        if at == 9:
            q_block(2)
        if at == 13:
            q_block(3)
            swap.start()
            q_out[me] = qs[me]
        if at == 26:
            swap.forward()
        if at > 14:
            for _ in range(2):
                if fresh:
                    unpack(fresh.pop(0))
    for sid in fresh:
        unpack(sid)
    swap.finish()
    for cp in outs:
        cp.wait()
    for cp in sends + [pcopy]:
        cp.wait_send()


def attend_kernel(
    meta, doc_len, sinks, q_ref, kv_hbm, o_ref,
    kv, qsel, mref, aref, buf0, buf1, buf2, buf3, steps, sem,
):
    load = pltpu.make_async_copy(kv_hbm, kv, sem)
    load.start()
    bufs = ((buf0, buf1), (buf2, buf3))
    _, c, y, _ = place()
    base = (c * 4 + y) * 2
    lane = lax.broadcasted_iota(jnp.int32, (1, 256), 1)
    sub = lax.broadcasted_iota(jnp.int32, (TILE, 256), 0)
    sink = jnp.where(lane < 128, sinks[base], sinks[base + 1]) * LOG2E

    def prep(n4, cr):
        for u in range(4):
            n = n4 * 4 + u
            qt = (q_ref[n >> 1, 128 * (u & 1):128 * (u & 1) + 128, :].astype(F32) * LOG2E).T
            qt = jnp.concatenate([qt[:64], qt[64:]], axis=1)
            hi = qt.astype(BF)
            lo = (qt - hi.astype(F32)).astype(BF)
            qsel[n] = jnp.concatenate([hi, lo], axis=0)
        return cr

    lax.fori_loop(0, 4, prep, 0)

    def clear(n, cr):
        mref[n] = sink
        aref[n] = jnp.concatenate([jnp.zeros((64, 256), F32), jnp.ones((16, 256), F32)], axis=0)
        return cr

    lax.fori_loop(0, 18, clear, 0)

    counts = []
    for s in range(2):
        def add(i, cr):
            n = i * 2 + s
            steps[s * 2, i] = n << 7

            def put(ci, k):
                steps[s * 2 + 1, k] = (n << 7) + ci * CH
                return k + 1

            return lax.fori_loop(1, meta[17, n], put, cr)

        counts.append(lax.fori_loop(0, 8, add, jnp.int32(0)))
        steps[s * 2, 8] = (16 + s) << 7
    most = (jnp.maximum(counts[0], counts[1]) + 1) & ~1
    for s in range(2):
        def fill(k, cr):
            steps[s * 2 + 1, k] = (16 + s) << 7
            return cr
        lax.fori_loop(counts[s], most + 1, fill, 0)
    totals = (jnp.int32(8), most)
    load.wait()

    def scores(s, kind, k):
        w = steps[s * 2 + kind, k]
        nn = (w >> 7) & 15
        c0 = w & 127
        js = [meta[nn, c0 + u] for u in range(CH)]
        ks = [kv[j >> 1, j & 1, 0:128, :] for j in js]
        return jnp.dot(jnp.concatenate(ks, axis=0), qsel[nn], preferred_element_type=F32)

    def absorb(s, kind, k, sc):
        w = steps[s * 2 + kind, k]
        n = w >> 7
        nn = n & 15
        c0 = w & 127
        js = [meta[nn, c0 + u] for u in range(CH)]
        vt = jnp.concatenate([kv[j >> 1, j & 1, 128:208, :] for j in js], axis=1)
        mx, acc = mref[n], aref[n]
        if kind == 0:
            qpos = meta[16, nn] * TILE + (lane & 127)
            first = doc_start(doc_len, qpos)
            inside = first > meta[16, nn] * TILE
            mx = jnp.where(inside, sink, mx)
            acc = jnp.where(inside, jnp.concatenate([jnp.zeros((64, 256), F32), jnp.ones((16, 256), F32)], axis=0), acc)
            parts = []
            for u in range(CH):
                part = sc[u * 128:(u + 1) * 128]
                off = js[u] * TILE
                ok = sub >= first - off
                if u == 0:
                    ok = ok & (sub <= qpos - off)
                parts.append(jnp.where(ok, part, -1e30))
            sc = jnp.concatenate(parts, axis=0)
        new = jnp.maximum(mx, jnp.max(sc, axis=0, keepdims=True))
        p = jnp.exp2(sc - new).astype(BF)
        alpha = jnp.exp2(mx - new)
        mref[n] = new
        aref[n] = acc * alpha + jnp.dot(vt, p, preferred_element_type=F32)

    for kind in (1, 0):
        for s in range(2):
            bufs[s][0][...] = scores(s, kind, 0)

        def it(k2, cr):
            for ph in range(2):
                k = k2 * 2 + ph
                for s in range(2):
                    bufs[s][1 - ph][...] = scores(s, kind, k + 1)
                    absorb(s, kind, k, bufs[s][ph][...])
            return cr

        lax.fori_loop(0, totals[kind] >> 1, it, 0)

    def fin(n2, cr):
        for u in range(2):
            a = aref[n2 * 2 + u]
            out = a[:64] / a[64:65]
            out = jnp.concatenate([out[:, :128], out[:, 128:]], axis=0)
            o_ref[n2, 128 * u:128 * u + 128, :] = out.T.astype(BF)
        return cr

    lax.fori_loop(0, 8, fin, 0)


def return_kernel(o_ref, out_ref, relay, s_sem, r_sem, q_sem):
    h, c, y, z = place()
    me = c * 4 + y
    barrier = pltpu.get_barrier_semaphore()
    for d in range(1, 8):
        i = (me + d) % 8
        pl.semaphore_signal(barrier, inc=1, device_id=device(i % 4, z, i // 4), device_id_type=MESH)
    pl.semaphore_wait(barrier, 7)

    def cols(m):
        return pl.ds(pl.multiple_of(m * 128, 128), 128)

    swap = Swap(lambda i: o_ref.at[i], lambda m: out_ref.at[:, cols(m)], relay, (s_sem, r_sem, q_sem), c, y, z)
    swap.start()
    out_ref[:, cols(me)] = o_ref[me]
    swap.forward()
    swap.finish()


def body(tokens, norm_gain, w_query, w_key, w_value, sinks, doc_lengths, tile_mask):
    vm = pl.BlockSpec(memory_space=pltpu.VMEM)
    anym = pl.BlockSpec(memory_space=pl.ANY)
    smem = pl.BlockSpec(memory_space=pltpu.SMEM)
    feats = tokens.shape[1]
    dma = pltpu.SemaphoreType.DMA
    kv, q, lists = pl.pallas_call(
        project_kernel,
        out_shape=(
            jax.ShapeDtypeStruct((65, 2, 208, 128), BF),
            jax.ShapeDtypeStruct((8, ROWS, 128), BF),
            jax.ShapeDtypeStruct((24, 128), jnp.int32),
        ),
        in_specs=[smem] + [anym] * 6,
        out_specs=(anym, vm, vm),
        scratch_shapes=[
            pltpu.VMEM((4, feats, ROWS), BF),
            pltpu.VMEM((4, ROWS, feats), BF),
            pltpu.VMEM((1, 4 * feats), F32),
            pltpu.VMEM((NT, NT), jnp.int32),
            pltpu.VMEM((4 * feats, 1024), BF),
            pltpu.VMEM((4 * feats, 256), BF),
            pltpu.VMEM((2, ROWS, 128), BF),
            pltpu.VMEM((64, ROWS, 128), BF),
            pltpu.VMEM((65, 2, 208, 128), BF),
            pltpu.VMEM((8, ROWS, 128), BF),
            pltpu.VMEM((2, ROWS, 128), BF),
            dma((6,)), dma((6,)), dma((6,)), dma((64,)), dma((64,)), dma, dma((65,)), dma((9,)), dma((8,)), dma((2,)),
        ],
        compiler_params=pltpu.CompilerParams(collective_id=0, has_side_effects=True),
        name="project",
    )(doc_lengths, tokens.T, norm_gain, tile_mask, w_query, w_key, w_value)
    o = pl.pallas_call(
        attend_kernel,
        out_shape=jax.ShapeDtypeStruct((8, ROWS, 128), BF),
        in_specs=[smem, smem, smem, vm, anym],
        out_specs=vm,
        scratch_shapes=[
            pltpu.VMEM((65, 2, 208, 128), BF),
            pltpu.VMEM((16, 128, 256), BF),
            pltpu.VMEM((18, 1, 256), F32),
            pltpu.VMEM((18, 80, 256), F32),
        ] + [pltpu.VMEM((CH * TILE, 256), F32)] * 4 + [pltpu.SMEM((4, 256), jnp.int32), dma],
        name="attend",
    )(lists, doc_lengths, sinks, q, kv)
    return pl.pallas_call(
        return_kernel,
        out_shape=jax.ShapeDtypeStruct((ROWS, 1024), BF),
        in_specs=[vm],
        out_specs=vm,
        scratch_shapes=[pltpu.VMEM((2, ROWS, 128), BF), dma((9,)), dma((8,)), dma((2,))],
        compiler_params=pltpu.CompilerParams(collective_id=1, has_side_effects=True),
        name="give_back",
    )(o)


def solution(mesh):
    in_specs = (
        P(("grp", "blk"), "head"),
        P(),
        P(None, "head"),
        P(None, "head"),
        P(None, "head"),
        P("head"),
        P(),
        P(),
    )
    out_specs = P(("grp", "blk"), "head")
    return jax.shard_map(body, mesh=mesh, in_specs=in_specs, out_specs=out_specs, check_vma=False)
```

```python
import functools

import jax
import jax.numpy as jnp
from jax import lax
from jax.experimental import pallas as pl
from jax.experimental.pallas import tpu as pltpu
from jax.sharding import PartitionSpec as P

MESH = pl.DeviceIdType.MESH
HD = 64
TILE = 128
ROWS = 256
NT = 128
CH = 4
EPS = 1e-05
ROPE_BASE = 150000.0
LOG2E = 1.4426950408889634
ORDER = (
    (0, -1, 0, 0), (0, 0, -1, 0), (0, 0, 1, 0), (0, 1, 0, 0), (1, -1, 0, 0), (1, 0, -1, 0),
    (1, 0, 1, 0), (1, 1, 0, 0), (2, 0, 0, 1), (0, 0, -2, 0), (0, 0, 2, 0), (0, 1, -1, 0),
    (0, 2, 0, 0), (0, -1, -1, 0), (0, 1, 1, 0), (1, -1, -1, 0), (1, -1, 1, 0), (0, -1, 1, 0),
    (0, 1, 0, 1), (1, 0, -2, 0), (1, 0, 2, 0), (1, 1, -1, 0), (1, 1, 0, 1), (1, 1, 1, 0),
    (1, 2, 0, 0), (0, -1, 0, 1), (0, 0, -1, 1), (0, 0, 1, 1), (0, 1, -2, 0), (1, -1, 0, 1),
    (1, 0, -1, 1), (1, 0, 1, 1), (0, 1, 2, 0), (0, -1, -2, 0), (0, 0, -3, 0), (0, 0, 3, 0),
    (0, 2, -1, 0), (0, -1, 2, 0), (1, -1, -2, 0), (1, -1, 2, 0), (0, 2, 1, 0), (1, 0, -3, 0),
    (1, 0, 3, 0), (0, 1, -1, 1), (0, 2, 0, 1), (1, 1, -2, 0), (1, 1, 1, 1), (0, -1, -1, 1),
    (0, 1, 1, 1), (1, 1, -1, 1), (1, 1, 2, 0), (0, -1, 1, 1), (0, 1, -3, 0), (1, 2, -1, 0),
    (1, 2, 1, 0), (0, 1, 3, 0), (1, 2, 0, 1), (0, 0, -2, 1), (0, 0, 2, 1), (0, 2, -2, 0),
    (1, -1, -1, 1), (1, -1, 1, 1), (0, 2, -1, 1), (0, -1, -3, 0), (1, 0, -2, 1), (1, 0, 2, 1),
    (0, -1, 3, 0), (0, 2, 1, 1), (0, 0, -4, 0), (1, -1, 3, 0), (0, 2, -3, 0), (0, 2, 2, 0),
    (1, -1, -3, 0), (1, 1, 2, 1), (0, -1, -2, 1), (0, 2, 3, 0), (1, 0, -4, 0), (1, 1, 3, 0),
    (0, 1, -2, 1), (0, -1, 2, 1), (1, 1, -3, 0), (1, 2, 2, 0), (0, 1, 2, 1), (1, 1, -2, 1),
    (1, 2, 1, 1), (0, 0, 3, 1), (1, 2, -2, 0), (0, -1, -4, 0), (0, 1, -4, 0), (1, -1, 2, 1),
    (1, 2, -1, 1), (0, 0, -3, 1), (1, 0, 3, 1), (0, 2, -2, 1), (1, -1, -2, 1), (1, 1, 3, 1),
    (0, 2, 2, 1), (1, 0, -3, 1), (1, 1, 4, 0), (1, -1, -4, 0), (1, 2, 3, 0), (0, -1, 3, 1),
    (0, 1, 3, 1), (1, 1, -3, 1), (1, 2, 2, 1), (0, 2, -4, 0), (1, -1, 3, 1), (1, 2, -3, 0),
    (0, -1, -3, 1), (0, 1, -3, 1), (1, 2, -2, 1), (1, 1, 4, 1), (0, 0, -4, 1), (1, -1, -3, 1),
    (1, 2, 4, 0), (0, 2, 3, 1), (1, 0, -4, 1), (1, 2, 3, 1), (0, 2, -3, 1), (1, 2, -3, 1),
    (0, -1, -4, 1), (0, 1, -4, 1), (1, -1, -4, 1), (1, 2, 4, 1), (0, 2, -4, 1),
)
BF = jnp.bfloat16
F32 = jnp.float32

def place():
    h = lax.axis_index("head")
    g = lax.axis_index("grp")
    b = lax.axis_index("blk")
    c = g % 2
    y = (g // 2) * 2 + b // 8
    z = b % 8
    return h, c, y, z


def device(yy, zz, core):
    return {"grp": (yy // 2) * 2 + core, "blk": (yy % 2) * 8 + zz}


def shard_id(yy, zz, core):
    return (yy // 2) * 32 + core * 16 + (yy % 2) * 8 + zz


class Swap:
    def __init__(self, src, dst, relay, sems, c, y, z):
        self.src, self.dst, self.relay = src, dst, relay
        self.s_sem, self.r_sem, self.q_sem = sems
        self.c, self.y, self.z = c, y, z
        self.me = c * 4 + y
        self.up, self.down, self.far = (y + 1) % 4, (y + 3) % 4, (y + 2) % 4
        self.sent = []

    def go(self, src, dst, r_sem, target):
        cp = pltpu.make_async_remote_copy(
            src, dst, self.s_sem.at[len(self.sent)], r_sem, device_id=target, device_id_type=MESH)
        cp.start()
        self.sent.append(cp)

    def await_at(self, dst, r_sem):
        pltpu.make_async_remote_copy(
            dst, dst, self.s_sem.at[0], r_sem,
            device_id=device(self.y, self.z, 1 - self.c), device_id_type=MESH).wait_recv()

    def start(self):
        c, z, me = self.c, self.z, self.me
        self.go(self.src(self.far), self.relay.at[0], self.q_sem.at[0], device(self.up, z, c))
        self.go(self.src(4 + self.far), self.relay.at[1], self.q_sem.at[1], device(self.down, z, c))
        for core in range(2):
            self.go(self.src(core * 4 + self.up), self.dst(me), self.r_sem.at[me], device(self.up, z, core))
            self.go(self.src(core * 4 + self.down), self.dst(me), self.r_sem.at[me], device(self.down, z, core))
        self.go(self.src((1 - c) * 4 + self.y), self.dst(me), self.r_sem.at[me], device(self.y, z, 1 - c))

    def forward(self):
        c, z = self.c, self.z
        below, above = c * 4 + self.down, c * 4 + self.up
        self.await_at(self.relay.at[0], self.q_sem.at[0])
        self.go(self.relay.at[0], self.dst(below), self.r_sem.at[below], device(self.up, z, 0))
        self.await_at(self.relay.at[1], self.q_sem.at[1])
        self.go(self.relay.at[1], self.dst(above), self.r_sem.at[above], device(self.down, z, 1))

    def finish(self):
        for d in range(1, 8):
            i = (self.me + d) % 8
            self.await_at(self.dst(i), self.r_sem.at[i])
        for cp in self.sent:
            cp.wait_send()


def turned(x, cos, sin):
    lane = lax.broadcasted_iota(jnp.int32, x.shape, 1)
    other = jnp.where(lane % 64 < 32, pltpu.roll(x, 96, 1), pltpu.roll(x, 32, 1))
    return x * cos + other * sin


def angles(base):
    lane = lax.broadcasted_iota(jnp.int32, (1, 128), 1)
    freq = jnp.zeros((1, 128), F32)
    for i in range(HD // 2):
        freq = jnp.where(lane % 32 == i, ROPE_BASE ** (-2.0 * i / HD), freq)
    pos = lax.broadcasted_iota(jnp.int32, (ROWS, 128), 0) + base
    ang = pos.astype(F32) * freq
    sin = jnp.sin(ang)
    return jnp.cos(ang), jnp.where(lane % 64 < 32, -sin, sin)


def doc_start(doc_len, pos):
    end = jnp.int32(0)
    first = jnp.zeros_like(pos)
    for d in range(doc_len.shape[0]):
        end = end + doc_len[d]
        first = jnp.maximum(first, jnp.where(end <= pos, end, 0))
    return first


def key_lists(doc_len, tile_mask, z, lists):
    n = lax.broadcasted_iota(jnp.int32, (1, 128), 1)
    i = n // 2
    yy, core = i % 4, i // 4
    tile = shard_id(yy, z, core) * 2 + n % 2
    first = doc_start(doc_len, tile * TILE)
    last = doc_start(doc_len, tile * TILE + TILE - 1)
    j = lax.broadcasted_iota(jnp.int32, (NT, 128), 0)
    k = lax.broadcasted_iota(jnp.int32, (NT, 128), 1)
    pick = jnp.where(j == tile, 1.0, 0.0).astype(BF)
    listed = jnp.dot(tile_mask[...].astype(F32).T.astype(BF), pick, preferred_element_type=F32) > 0.5
    active = (listed | (j == tile)) & (j <= tile) & (j * TILE + TILE > first)
    act = jnp.where(active, 1.0, 0.0).astype(BF)
    lower = jnp.where(k < j, 1.0, 0.0).astype(BF)
    before = jnp.dot(lower, act, preferred_element_type=F32).astype(jnp.int32)
    spot = jnp.where(active, jnp.where(j == tile, 0, before + 1), -1)
    count = jnp.sum(jnp.where(active, 1, 0), axis=0, keepdims=True)
    for r in range(16):
        hit = spot[:, r:r + 1] == k
        lists[r:r + 1, :] = jnp.sum(jnp.where(hit, j - NT, 0), axis=0, keepdims=True) + NT
    lists[16:17, :] = tile
    lists[17:18, :] = (count + CH - 1) // CH
    lists[18:19, :] = jnp.where(first == last, 0, 1)
    lists[19:24, :] = jnp.zeros((5, 128), jnp.int32)


def project_kernel(
    doc_len, tok_hbm, gain_hbm, mask_hbm, wq_hbm, wk_hbm, wv_hbm,
    kv_out, q_out, lists,
    xt, xb, gain, mask, wq, wkv, kvs, kvb, kvu, qs, relay,
    wsem, xs_sem, xr_sem, ks_sem, kr_sem, ps_sem, us_sem, qs_sem, qr_sem, qq_sem,
):
    h, c, y, z = place()
    me = c * 4 + y
    feats = xb.shape[2]
    half = ROWS // 2

    copies = [
        pltpu.make_async_copy(tok_hbm, xt.at[h], wsem.at[0]),
        pltpu.make_async_copy(gain_hbm, gain.at[0], wsem.at[1]),
        pltpu.make_async_copy(mask_hbm, mask, wsem.at[2]),
        pltpu.make_async_copy(wk_hbm, wkv.at[:, 0:128], wsem.at[3]),
        pltpu.make_async_copy(wv_hbm, wkv.at[:, 128:256], wsem.at[4]),
        pltpu.make_async_copy(wq_hbm, wq, wsem.at[5]),
    ]
    for cp in copies:
        cp.start()

    def plane(dy, dz):
        return device((y + dy + 4) % 4, (z + dz + 8) % 8, c)

    def mate(d):
        i = (me + d) % 8
        return i, device(i % 4, z, i // 4)

    partner = device(y, z, 1 - c)
    ahead, behind, across = (h + 1) % 4, (h + 3) % 4, (h + 2) % 4
    barrier = pltpu.get_barrier_semaphore()
    for x in (ahead, behind):
        pl.semaphore_signal(barrier, inc=1, device_id={"head": x}, device_id_type=MESH)
    for dz in (1, -1):
        pl.semaphore_signal(barrier, inc=1, device_id=plane(0, dz), device_id_type=MESH)
    for d in range(1, 8):
        pl.semaphore_signal(barrier, inc=1, device_id=mate(d)[1], device_id_type=MESH)
    pl.semaphore_wait(barrier, 11)
    copies[0].wait()

    xsent = []
    cut = (feats // 32) * 16
    lo, hi, every = pl.ds(0, cut), pl.ds(cut, feats - cut), pl.ds(0, feats)
    ups, downs = pl.ds(0, half), pl.ds(half, half)

    def xref(src, part, rows):
        return xt.at[src, part, rows]

    def xsend(n, src, part, rows, to):
        cp = pltpu.make_async_remote_copy(
            xref(src, part, rows), xref(src, part, rows), xs_sem.at[n], xr_sem.at[n],
            device_id={"head": to}, device_id_type=MESH)
        cp.start()
        xsent.append(cp)

    def xwait(n, src, part, rows):
        pltpu.make_async_remote_copy(
            xref(src, part, rows), xref(src, part, rows), xs_sem.at[n], xr_sem.at[n],
            device_id={"head": ahead}, device_id_type=MESH).wait_recv()

    xsend(0, h, every, ups, ahead)
    xsend(1, h, every, ups, behind)
    xsend(2, h, lo, downs, ahead)
    xsend(3, h, hi, downs, behind)
    cos, sin = angles(shard_id(y, z, c) * ROWS)

    copies[2].wait()
    key_lists(doc_len, mask, z, lists)
    copies[1].wait()

    def squares(i, e):
        w = xt[i, :, 128 * e:128 * e + 128].astype(F32).T
        xb[i, 128 * e:128 * e + 128, :] = w.astype(BF)
        return jnp.sum(w * w, axis=1, keepdims=True)

    total0 = squares(h, 0)
    xwait(0, behind, every, ups)
    xsend(4, behind, lo, ups, ahead)
    xwait(1, ahead, every, ups)
    xsend(5, ahead, hi, ups, behind)
    total0 = total0 + squares(behind, 0)
    xwait(2, behind, lo, downs)
    xsend(6, behind, lo, downs, ahead)
    xwait(3, ahead, hi, downs)
    xsend(7, ahead, hi, downs, behind)
    xsend(8, h, hi, downs, ahead)
    xsend(9, h, lo, downs, behind)
    total0 = total0 + squares(ahead, 0)
    total1 = squares(h, 1)
    kvu[64] = jnp.zeros((2, 208, 128), BF)
    copies[3].wait()
    copies[4].wait()
    lane = lax.broadcasted_iota(jnp.int32, (64, 128), 1)
    own = shard_id(y, z, c)
    other = shard_id(y, z, 1 - c)
    sends, outs, pcopies = [], [], []
    null = pltpu.make_async_copy(kvu.at[64], kv_out.at[64], us_sem.at[64])
    null.start()
    outs.append(null)

    def piece(sid, e):
        return kvb.at[sid, 128 * e:128 * e + 128]

    def send(sid, e, target):
        cp = pltpu.make_async_remote_copy(
            piece(sid, e), piece(sid, e), ks_sem.at[len(sends)], kr_sem.at[e, sid],
            device_id=target, device_id_type=MESH)
        cp.start()
        sends.append(cp)

    def arrived(sid, e):
        pltpu.make_async_remote_copy(
            piece(sid, e), piece(sid, e), ps_sem.at[e], kr_sem.at[e, sid],
            device_id=partner, device_id_type=MESH).wait_recv()

    def keys_values(e, total):
        rows = slice(128 * e, 128 * e + 128)
        scale = lax.rsqrt(total / (4 * feats) + EPS)
        kvp = jnp.zeros((128, 256), F32)
        for i in range(4):
            w = xb[i, rows, :].astype(F32) * scale * gain[:, i * feats:(i + 1) * feats]
            w = w.astype(BF)
            xb[i, rows, :] = w
            kvp = kvp + jnp.dot(w, wkv[i * feats:(i + 1) * feats, :], preferred_element_type=F32)
        k = turned(kvp[:, :128], cos[rows], sin[rows])
        k0, k1 = k[:64], k[64:]
        vt = kvp[:, 128:].T.astype(BF)
        kvs[0, 128 * e:128 * e + 64, :] = jnp.where(lane < 64, k0, pltpu.roll(k1, 64, 1)).astype(BF)
        kvs[1, 128 * e:128 * e + 64, :] = jnp.where(lane < 64, pltpu.roll(k0, 64, 1), k1).astype(BF)
        for cc in range(2):
            kvs[cc, 128 * e + 64:128 * e + 128, :] = vt[64 * cc:64 * (cc + 1)]
        cp = pltpu.make_async_remote_copy(
            kvs.at[1 - c, rows], piece(own, e), ps_sem.at[e], kr_sem.at[e, own],
            device_id=partner, device_id_type=MESH)
        cp.start()
        pcopies.append(cp)
        kvb[own, rows] = kvs[c, rows]
        for sid in (own, other):
            if sid is other:
                arrived(other, e)
            for dy, dz in ((0, 1), (0, -1), (1, 0), (-1, 0)):
                send(sid, e, plane(dy, dz))

    def unpack(sid):
        for e in range(2):
            k2 = kvb[sid, 128 * e:128 * e + 64, :].astype(F32)
            r2 = pltpu.roll(k2, 64, 1)
            kvu[sid, e, 0:64, :] = jnp.where(lane < 64, k2, r2).astype(BF)
            kvu[sid, e, 64:128, :] = jnp.where(lane < 64, r2, k2).astype(BF)
            kvu[sid, e, 128:192, :] = kvb[sid, 128 * e + 64:128 * e + 128, :]
            kvu[sid, e, 192:208, :] = jnp.ones((16, 128), BF)
        cp = pltpu.make_async_copy(kvu.at[sid], kv_out.at[sid], us_sem.at[sid])
        cp.start()
        outs.append(cp)

    def block(dy, dz, core):
        return shard_id((y + dy + 4) % 4, (z + dz + 8) % 8, core)

    def q_block(n):
        acc = jnp.zeros((ROWS, 256), F32)
        for i in range(4):
            acc = acc + jnp.dot(
                xb[i], wq[i * feats:(i + 1) * feats, n * 256:(n + 1) * 256], preferred_element_type=F32)
        for u in range(2):
            qs[n * 2 + u] = (turned(acc[:, u * 128:(u + 1) * 128], cos, sin) * 0.125).astype(BF)

    xwait(4, across, lo, ups)
    xwait(5, across, hi, ups)
    total0 = total0 + squares(across, 0)
    keys_values(0, total0)

    swap = Swap(lambda i: qs.at[i], lambda m: q_out.at[m], relay, (qs_sem, qr_sem, qq_sem), c, y, z)
    fresh = []
    seen = set()
    since = None
    for part, dy, dz, e in ORDER:
        if part == 2:
            xwait(8, behind, hi, downs)
            total1 = total1 + squares(behind, 1)
            xwait(9, ahead, lo, downs)
            total1 = total1 + squares(ahead, 1)
            xwait(6, across, lo, downs)
            xwait(7, across, hi, downs)
            total1 = total1 + squares(across, 1)
            keys_values(1, total1)
            copies[5].wait()
            fresh += [own, other]
            since = 0
            continue
        sid = block(dy, dz, part)
        arrived(sid, e)
        seen.add((part, dy, dz, e))
        low_z, high_z = (-4, 3) if part == 0 or dy in (0, -1) else (-3, 4)
        if part == 1 or dy == 0:
            if dz <= 0 and dz > low_z:
                send(sid, e, plane(0, 1))
            if dz >= 0 and dz < high_z:
                send(sid, e, plane(0, -1))
        if part == 0:
            if dy == 0:
                send(sid, e, plane(1, 0))
                send(sid, e, plane(-1, 0))
            elif dy == -1 and dz % 2 == 0:
                send(sid, e, plane(1, 0))
            elif dy == 1 and dz % 2 == 1:
                send(sid, e, plane(-1, 0))
        elif dz == 0 and dy in (1, -1) and (1, -dy, 0, e) in seen:
            sgn = 1 - 2 * c
            send(shard_id((y - sgn + 4) % 4, z, 1), e, plane(sgn, 0))
        if (part, dy, dz, 1 - e) in seen:
            fresh.append(sid)
        if since is not None:
            since += 1
            if since in (2, 6, 10, 14):
                q_block(since // 4)
            if since == 14:
                swap.start()
                q_out[me] = qs[me]
            if since == 40:
                swap.forward()
            if since > 16 and fresh:
                unpack(fresh.pop(0))
    for sid in fresh:
        unpack(sid)
    swap.finish()
    for cp in outs:
        cp.wait()
    for cp in xsent + sends + pcopies:
        cp.wait_send()


def attend_kernel(
    meta, doc_len, sinks, q_ref, kv_hbm, o_ref,
    kv, qsel, mref, aref, buf0, buf1, buf2, buf3, steps, sem,
):
    load = pltpu.make_async_copy(kv_hbm, kv, sem)
    load.start()
    bufs = ((buf0, buf1), (buf2, buf3))
    _, c, y, _ = place()
    base = (c * 4 + y) * 2
    lane = lax.broadcasted_iota(jnp.int32, (1, 256), 1)
    sub = lax.broadcasted_iota(jnp.int32, (TILE, 256), 0)
    sink = jnp.where(lane < 128, sinks[base], sinks[base + 1]) * LOG2E

    def prep(n4, cr):
        for u in range(4):
            n = n4 * 4 + u
            qt = (q_ref[n >> 1, 128 * (u & 1):128 * (u & 1) + 128, :].astype(F32) * LOG2E).T
            qt = jnp.concatenate([qt[:64], qt[64:]], axis=1)
            hi = qt.astype(BF)
            lo = (qt - hi.astype(F32)).astype(BF)
            qsel[n] = jnp.concatenate([hi, lo], axis=0)
        return cr

    lax.fori_loop(0, 4, prep, 0)

    def clear(n, cr):
        mref[n] = sink
        aref[n] = jnp.concatenate([jnp.zeros((64, 256), F32), jnp.ones((16, 256), F32)], axis=0)
        return cr

    lax.fori_loop(0, 18, clear, 0)

    counts = []
    for s in range(2):
        def add(i, cr):
            n = i * 2 + s
            steps[s * 2, i] = n << 7

            def put(ci, k):
                steps[s * 2 + 1, k] = (n << 7) + ci * CH
                return k + 1

            return lax.fori_loop(1, meta[17, n], put, cr)

        counts.append(lax.fori_loop(0, 8, add, jnp.int32(0)))
        steps[s * 2, 8] = (16 + s) << 7
    most = (jnp.maximum(counts[0], counts[1]) + 1) & ~1
    for s in range(2):
        def fill(k, cr):
            steps[s * 2 + 1, k] = (16 + s) << 7
            return cr
        lax.fori_loop(counts[s], most + 1, fill, 0)
    totals = (jnp.int32(8), most)
    load.wait()

    def scores(s, kind, k):
        w = steps[s * 2 + kind, k]
        nn = (w >> 7) & 15
        c0 = w & 127
        js = [meta[nn, c0 + u] for u in range(CH)]
        ks = [kv[j >> 1, j & 1, 0:128, :] for j in js]
        return jnp.dot(jnp.concatenate(ks, axis=0), qsel[nn], preferred_element_type=F32)

    def absorb(s, kind, k, sc):
        w = steps[s * 2 + kind, k]
        n = w >> 7
        nn = n & 15
        c0 = w & 127
        js = [meta[nn, c0 + u] for u in range(CH)]
        vt = jnp.concatenate([kv[j >> 1, j & 1, 128:208, :] for j in js], axis=1)
        mx, acc = mref[n], aref[n]
        if kind == 0:
            qpos = meta[16, nn] * TILE + (lane & 127)
            first = doc_start(doc_len, qpos)
            inside = first > meta[16, nn] * TILE
            mx = jnp.where(inside, sink, mx)
            acc = jnp.where(inside, jnp.concatenate([jnp.zeros((64, 256), F32), jnp.ones((16, 256), F32)], axis=0), acc)
            parts = []
            for u in range(CH):
                part = sc[u * 128:(u + 1) * 128]
                off = js[u] * TILE
                ok = sub >= first - off
                if u == 0:
                    ok = ok & (sub <= qpos - off)
                parts.append(jnp.where(ok, part, -1e30))
            sc = jnp.concatenate(parts, axis=0)
        new = jnp.maximum(mx, jnp.max(sc, axis=0, keepdims=True))
        p = jnp.exp2(sc - new).astype(BF)
        alpha = jnp.exp2(mx - new)
        mref[n] = new
        aref[n] = acc * alpha + jnp.dot(vt, p, preferred_element_type=F32)

    for kind in (1, 0):
        for s in range(2):
            bufs[s][0][...] = scores(s, kind, 0)

        def it(k2, cr):
            for ph in range(2):
                k = k2 * 2 + ph
                for s in range(2):
                    bufs[s][1 - ph][...] = scores(s, kind, k + 1)
                    absorb(s, kind, k, bufs[s][ph][...])
            return cr

        lax.fori_loop(0, totals[kind] >> 1, it, 0)

    def fin(n2, cr):
        for u in range(2):
            a = aref[n2 * 2 + u]
            out = a[:64] / a[64:65]
            out = jnp.concatenate([out[:, :128], out[:, 128:]], axis=0)
            o_ref[n2, 128 * u:128 * u + 128, :] = out.T.astype(BF)
        return cr

    lax.fori_loop(0, 8, fin, 0)


def return_kernel(o_ref, out_ref, relay, s_sem, r_sem, q_sem):
    h, c, y, z = place()
    me = c * 4 + y
    barrier = pltpu.get_barrier_semaphore()
    for d in range(1, 8):
        i = (me + d) % 8
        pl.semaphore_signal(barrier, inc=1, device_id=device(i % 4, z, i // 4), device_id_type=MESH)
    pl.semaphore_wait(barrier, 7)

    def cols(m):
        return pl.ds(pl.multiple_of(m * 128, 128), 128)

    swap = Swap(lambda i: o_ref.at[i], lambda m: out_ref.at[:, cols(m)], relay, (s_sem, r_sem, q_sem), c, y, z)
    swap.start()
    out_ref[:, cols(me)] = o_ref[me]
    swap.forward()
    swap.finish()


def body(tokens, norm_gain, w_query, w_key, w_value, sinks, doc_lengths, tile_mask):
    vm = pl.BlockSpec(memory_space=pltpu.VMEM)
    anym = pl.BlockSpec(memory_space=pl.ANY)
    smem = pl.BlockSpec(memory_space=pltpu.SMEM)
    feats = tokens.shape[1]
    dma = pltpu.SemaphoreType.DMA
    kv, q, lists = pl.pallas_call(
        project_kernel,
        out_shape=(
            jax.ShapeDtypeStruct((65, 2, 208, 128), BF),
            jax.ShapeDtypeStruct((8, ROWS, 128), BF),
            jax.ShapeDtypeStruct((24, 128), jnp.int32),
        ),
        in_specs=[smem] + [anym] * 6,
        out_specs=(anym, vm, vm),
        scratch_shapes=[
            pltpu.VMEM((4, feats, ROWS), BF),
            pltpu.VMEM((4, ROWS, feats), BF),
            pltpu.VMEM((1, 4 * feats), F32),
            pltpu.VMEM((NT, NT), jnp.int32),
            pltpu.VMEM((4 * feats, 1024), BF),
            pltpu.VMEM((4 * feats, 256), BF),
            pltpu.VMEM((2, ROWS, 128), BF),
            pltpu.VMEM((64, ROWS, 128), BF),
            pltpu.VMEM((65, 2, 208, 128), BF),
            pltpu.VMEM((8, ROWS, 128), BF),
            pltpu.VMEM((2, ROWS, 128), BF),
            dma((6,)), dma((10,)), dma((10,)), dma((124,)), dma((2, 64)), dma((2,)), dma((65,)),
            dma((9,)), dma((8,)), dma((2,)),
        ],
        compiler_params=pltpu.CompilerParams(collective_id=0, has_side_effects=True),
        name="project",
    )(doc_lengths, tokens.T, norm_gain, tile_mask, w_query, w_key, w_value)
    o = pl.pallas_call(
        attend_kernel,
        out_shape=jax.ShapeDtypeStruct((8, ROWS, 128), BF),
        in_specs=[smem, smem, smem, vm, anym],
        out_specs=vm,
        scratch_shapes=[
            pltpu.VMEM((65, 2, 208, 128), BF),
            pltpu.VMEM((16, 128, 256), BF),
            pltpu.VMEM((18, 1, 256), F32),
            pltpu.VMEM((18, 80, 256), F32),
        ] + [pltpu.VMEM((CH * TILE, 256), F32)] * 4 + [pltpu.SMEM((4, 256), jnp.int32), dma],
        name="attend",
    )(lists, doc_lengths, sinks, q, kv)
    return pl.pallas_call(
        return_kernel,
        out_shape=jax.ShapeDtypeStruct((ROWS, 1024), BF),
        in_specs=[vm],
        out_specs=vm,
        scratch_shapes=[pltpu.VMEM((2, ROWS, 128), BF), dma((9,)), dma((8,)), dma((2,))],
        compiler_params=pltpu.CompilerParams(collective_id=1, has_side_effects=True),
        name="give_back",
    )(o)


def solution(mesh):
    in_specs = (
        P(("grp", "blk"), "head"),
        P(),
        P(None, "head"),
        P(None, "head"),
        P(None, "head"),
        P("head"),
        P(),
        P(),
    )
    out_specs = P(("grp", "blk"), "head")
    return jax.shard_map(body, mesh=mesh, in_specs=in_specs, out_specs=out_specs, check_vma=False)
```

```python
import functools

import jax
import jax.numpy as jnp
from jax import lax
from jax.experimental import pallas as pl
from jax.experimental.pallas import tpu as pltpu
from jax.sharding import PartitionSpec as P

MESH = pl.DeviceIdType.MESH
HD = 64
TILE = 128
ROWS = 256
NT = 128
CH = 4
EPS = 1e-05
ROPE_BASE = 150000.0
LOG2E = 1.4426950408889634
ACTIONS = (
    (0, 0, 0, -1), (0, 0, 0, 1), (0, 1, -1, 0), (0, 1, 1, 0), (1, 0, 0, -1), (2, 0, 0, 1), (5, 1, -1, 0),
    (4, 0, 0, -1), (1, 1, -1, 0), (2, 1, 1, 0), (6, 0, 0, 0), (6, 1, 0, 0), (1, 1, 1, 0), (2, 1, -1, 0),
    (6, 0, 0, 0), (6, 1, 0, 0), (0, 1, 0, -1), (0, 1, 0, 1), (0, 0, -1, 0), (0, 0, 1, 0), (1, 1, 0, -1),
    (2, 1, 0, 1), (6, 0, 0, 0), (6, 1, 0, 0), (6, 0, 0, 0), (6, 1, 0, 0), (0, 0, 0, -2), (0, 0, 0, 2),
    (0, 1, 2, 0), (0, 0, 1, -1), (1, 0, 0, -2), (2, 1, 2, 0), (1, 1, 2, 0), (2, 0, 0, 2), (3, 0, 0, -2),
    (4, 0, 0, 1), (0, 1, -1, -1), (0, 1, 1, 1), (1, 1, -1, -1), (2, 1, 1, 1), (3, 0, 0, 2), (4, 0, 0, -2),
    (0, 1, 1, -1), (0, 1, -1, 1), (1, 1, 1, -1), (2, 1, -1, 1), (3, 0, 0, -1), (4, 0, 0, 2), (0, 1, 0, -2),
    (0, 1, 0, 2), (3, 0, 0, 1), (0, 0, 0, -3), (0, 1, 2, 1), (1, 0, 0, -3), (2, 1, 2, 1), (4, 0, 0, -3),
    (1, 1, 0, -2), (2, 1, 0, 2), (3, 0, -1, 0), (0, 1, 2, -1), (0, 0, 0, 3), (0, 0, -1, -2), (0, 0, 1, 1),
    (4, 0, 0, 3), (1, 1, 2, -1), (3, 0, 0, -3), (4, 0, 1, -1), (0, 1, -1, -2), (0, 1, 1, 2), (0, 0, -1, 2),
    (0, 0, 1, -2), (2, 1, 1, 2), (1, 1, -1, -2), (3, 0, 0, 3), (4, 0, 1, 1), (0, 1, 1, -2), (0, 1, -1, 2),
    (0, 0, -1, -1), (0, 0, 1, 2), (2, 1, -1, 2), (1, 1, 1, -2), (0, 0, 0, -4), (0, 1, 2, 2), (0, 0, -1, 1),
    (0, 0, 1, -3), (2, 1, 2, 2), (3, 0, 0, -4), (4, 0, 0, -4), (3, 0, -1, -2), (4, 0, 1, -3), (0, 1, 0, -3),
    (0, 1, 0, 3), (0, 0, 2, 0), (0, 0, 1, 3), (1, 1, 0, -3), (3, 0, -1, 2), (4, 0, 1, 3), (0, 1, 2, -2),
    (0, 1, 1, 3), (0, 0, -1, -3), (0, 0, 2, -1), (2, 1, 1, 3), (1, 1, 2, -2), (0, 1, -1, -3), (0, 1, -1, 3),
    (0, 0, -1, 3), (0, 0, 2, 1), (1, 1, -1, -3), (0, 1, 1, -3), (0, 1, 2, 3), (0, 0, -1, -4), (0, 0, 1, -4),
    (2, 1, 2, 3), (3, 0, -1, -4), (0, 1, 0, -4), (0, 0, 2, -2), (0, 0, 2, -3), (0, 1, 1, 4), (0, 1, 2, -3),
    (0, 0, 2, 2), (0, 0, 2, 3), (0, 1, -1, -4), (0, 1, 2, 4), (0, 0, 2, -4),
)
BF = jnp.bfloat16
F32 = jnp.float32

def place():
    h = lax.axis_index("head")
    g = lax.axis_index("grp")
    b = lax.axis_index("blk")
    c = g % 2
    y = (g // 2) * 2 + b // 8
    z = b % 8
    return h, c, y, z


def device(yy, zz, core):
    return {"grp": (yy // 2) * 2 + core, "blk": (yy % 2) * 8 + zz}


def shard_id(yy, zz, core):
    return (yy // 2) * 32 + core * 16 + (yy % 2) * 8 + zz


class Swap:
    def __init__(self, src, dst, relay, sems, c, y, z):
        self.src, self.dst, self.relay = src, dst, relay
        self.s_sem, self.r_sem, self.q_sem = sems
        self.c, self.y, self.z = c, y, z
        self.me = c * 4 + y
        self.up, self.down, self.far = (y + 1) % 4, (y + 3) % 4, (y + 2) % 4
        self.sent = []

    def go(self, src, dst, r_sem, target):
        cp = pltpu.make_async_remote_copy(
            src, dst, self.s_sem.at[len(self.sent)], r_sem, device_id=target, device_id_type=MESH)
        cp.start()
        self.sent.append(cp)

    def await_at(self, dst, r_sem):
        pltpu.make_async_remote_copy(
            dst, dst, self.s_sem.at[0], r_sem,
            device_id=device(self.y, self.z, 1 - self.c), device_id_type=MESH).wait_recv()

    def queue(self):
        c, z, me = self.c, self.z, self.me
        ups = [(self.far, self.relay.at[0], self.q_sem.at[0], device(self.up, z, c))]
        downs = [(4 + self.far, self.relay.at[1], self.q_sem.at[1], device(self.down, z, c))]
        for core in range(2):
            ups.append((core * 4 + self.up, self.dst(me), self.r_sem.at[me], device(self.up, z, core)))
            downs.append((core * 4 + self.down, self.dst(me), self.r_sem.at[me], device(self.down, z, core)))
        self.side = ((1 - c) * 4 + self.y, self.dst(me), self.r_sem.at[me], device(self.y, z, 1 - c))
        return ups, downs

    def step(self, entry):
        i, dst, r_sem, target = entry
        self.go(self.src(i), dst, r_sem, target)

    def start(self):
        for pair in zip(*self.queue()):
            for entry in pair:
                self.step(entry)
        self.step(self.side)

    def forward(self):
        c, z = self.c, self.z
        below, above = c * 4 + self.down, c * 4 + self.up
        self.await_at(self.relay.at[0], self.q_sem.at[0])
        self.go(self.relay.at[0], self.dst(below), self.r_sem.at[below], device(self.up, z, 0))
        self.await_at(self.relay.at[1], self.q_sem.at[1])
        self.go(self.relay.at[1], self.dst(above), self.r_sem.at[above], device(self.down, z, 1))

    def finish(self):
        for d in range(1, 8):
            i = (self.me + d) % 8
            self.await_at(self.dst(i), self.r_sem.at[i])
        for cp in self.sent:
            cp.wait_send()


def turned(x, cos, sin):
    lane = lax.broadcasted_iota(jnp.int32, x.shape, 1)
    other = jnp.where(lane % 64 < 32, pltpu.roll(x, 96, 1), pltpu.roll(x, 32, 1))
    return x * cos + other * sin


def angles(base):
    lane = lax.broadcasted_iota(jnp.int32, (1, 128), 1)
    freq = jnp.zeros((1, 128), F32)
    for i in range(HD // 2):
        freq = jnp.where(lane % 32 == i, ROPE_BASE ** (-2.0 * i / HD), freq)
    pos = lax.broadcasted_iota(jnp.int32, (ROWS, 128), 0) + base
    ang = pos.astype(F32) * freq
    sin = jnp.sin(ang)
    return jnp.cos(ang), jnp.where(lane % 64 < 32, -sin, sin)


def doc_start(doc_len, pos):
    end = jnp.int32(0)
    first = jnp.zeros_like(pos)
    for d in range(doc_len.shape[0]):
        end = end + doc_len[d]
        first = jnp.maximum(first, jnp.where(end <= pos, end, 0))
    return first


def key_lists(doc_len, tile_mask, z, lists):
    n = lax.broadcasted_iota(jnp.int32, (1, 128), 1)
    i = n // 2
    yy, core = i % 4, i // 4
    tile = shard_id(yy, z, core) * 2 + n % 2
    first = doc_start(doc_len, tile * TILE)
    last = doc_start(doc_len, tile * TILE + TILE - 1)
    j = lax.broadcasted_iota(jnp.int32, (NT, 128), 0)
    k = lax.broadcasted_iota(jnp.int32, (NT, 128), 1)
    pick = jnp.where(j == tile, 1.0, 0.0).astype(BF)
    listed = jnp.dot(tile_mask[...].astype(F32).T.astype(BF), pick, preferred_element_type=F32) > 0.5
    active = (listed | (j == tile)) & (j <= tile) & (j * TILE + TILE > first)
    act = jnp.where(active, 1.0, 0.0).astype(BF)
    lower = jnp.where(k < j, 1.0, 0.0).astype(BF)
    before = jnp.dot(lower, act, preferred_element_type=F32).astype(jnp.int32)
    spot = jnp.where(active, jnp.where(j == tile, 0, before + 1), -1)
    count = jnp.sum(jnp.where(active, 1, 0), axis=0, keepdims=True)
    for r in range(16):
        hit = spot[:, r:r + 1] == k
        lists[r:r + 1, :] = jnp.sum(jnp.where(hit, j - NT, 0), axis=0, keepdims=True) + NT
    lists[16:17, :] = tile
    lists[17:18, :] = (count + CH - 1) // CH
    lists[18:19, :] = jnp.where(first == last, 0, 1)
    lists[19:24, :] = jnp.zeros((5, 128), jnp.int32)


def project_kernel(
    doc_len, tok_hbm, gain_hbm, mask_hbm, wq_hbm, wk_hbm, wv_hbm,
    kv_out, q_out, lists,
    xt, xb, gain, mask, wq, wkv, kvs, kvb, kvu, qs, relay,
    wsem, xs_sem, xr_sem, ks_sem, kr_sem, ps_sem, us_sem, qs_sem, qr_sem, qq_sem,
):
    h, c, y, z = place()
    me = c * 4 + y
    feats = xb.shape[2]
    half = ROWS // 2

    copies = [
        pltpu.make_async_copy(tok_hbm, xt.at[h], wsem.at[0]),
        pltpu.make_async_copy(gain_hbm, gain.at[0], wsem.at[1]),
        pltpu.make_async_copy(mask_hbm, mask, wsem.at[2]),
        pltpu.make_async_copy(wk_hbm, wkv.at[:, 0:128], wsem.at[3]),
        pltpu.make_async_copy(wv_hbm, wkv.at[:, 128:256], wsem.at[4]),
        pltpu.make_async_copy(wq_hbm, wq, wsem.at[5]),
    ]
    for cp in copies:
        cp.start()

    def plane(dy, dz):
        return device((y + dy + 4) % 4, (z + dz + 8) % 8, c)

    def mate(d):
        i = (me + d) % 8
        return i, device(i % 4, z, i // 4)

    partner = device(y, z, 1 - c)
    ahead, behind, across = (h + 1) % 4, (h + 3) % 4, (h + 2) % 4
    barrier = pltpu.get_barrier_semaphore()
    for x in (ahead, behind):
        pl.semaphore_signal(barrier, inc=1, device_id={"head": x}, device_id_type=MESH)
    for dz in (1, -1):
        pl.semaphore_signal(barrier, inc=1, device_id=plane(0, dz), device_id_type=MESH)
    for d in range(1, 8):
        pl.semaphore_signal(barrier, inc=1, device_id=mate(d)[1], device_id_type=MESH)
    pl.semaphore_wait(barrier, 11)
    copies[0].wait()

    xsent = []
    top, low = pl.ds(0, half), pl.ds(half, half)

    def xsend(n, src, rows, to):
        cp = pltpu.make_async_remote_copy(
            xt.at[src, :, rows], xt.at[src, :, rows], xs_sem.at[n], xr_sem.at[n],
            device_id={"head": to}, device_id_type=MESH)
        cp.start()
        xsent.append(cp)

    def xwait(n, src, rows):
        pltpu.make_async_remote_copy(
            xt.at[src, :, rows], xt.at[src, :, rows], xs_sem.at[n], xr_sem.at[n],
            device_id={"head": ahead}, device_id_type=MESH).wait_recv()

    xsend(0, h, top, ahead)
    xsend(1, h, low, behind)
    xsend(2, h, low, ahead)
    xsend(3, h, top, behind)
    cos, sin = angles(shard_id(y, z, c) * ROWS)
    xwait(0, behind, top)
    xsend(4, behind, top, ahead)
    xwait(1, ahead, low)
    xsend(5, ahead, low, behind)

    copies[2].wait()
    key_lists(doc_len, mask, z, lists)
    kvu[64] = jnp.zeros((2, 208, 128), BF)
    copies[1].wait()

    def squares(i):
        w = xt[i].astype(F32).T
        xb[i] = w.astype(BF)
        return jnp.sum(w * w, axis=1, keepdims=True)

    total = squares(h)
    xwait(2, behind, low)
    total = total + squares(behind)
    xwait(3, ahead, top)
    total = total + squares(ahead)
    xwait(4, across, top)
    xwait(5, across, low)
    total = total + squares(across)
    scale = lax.rsqrt(total / (4 * feats) + EPS)
    for cp in xsent:
        cp.wait_send()
    copies[3].wait()
    copies[4].wait()
    kvp = jnp.zeros((ROWS, 256), F32)
    for i in range(4):
        w = xb[i].astype(F32) * scale * gain[:, i * feats:(i + 1) * feats]
        w = w.astype(BF)
        xb[i] = w
        kvp = kvp + jnp.dot(w, wkv[i * feats:(i + 1) * feats, :], preferred_element_type=F32)
    k = turned(kvp[:, :128], cos, sin)
    v = kvp[:, 128:]
    lane = lax.broadcasted_iota(jnp.int32, (64, 128), 1)
    for e in range(2):
        k0, k1 = k[128 * e:128 * e + 64], k[128 * e + 64:128 * e + 128]
        vt = v[128 * e:128 * (e + 1)].T.astype(BF)
        kvs[0, 128 * e:128 * e + 64, :] = jnp.where(lane < 64, k0, pltpu.roll(k1, 64, 1)).astype(BF)
        kvs[1, 128 * e:128 * e + 64, :] = jnp.where(lane < 64, pltpu.roll(k0, 64, 1), k1).astype(BF)
        for cc in range(2):
            kvs[cc, 128 * e + 64:128 * e + 128, :] = vt[64 * cc:64 * (cc + 1)]
    own = shard_id(y, z, c)
    other = shard_id(y, z, 1 - c)
    pcopy = pltpu.make_async_remote_copy(
        kvs.at[1 - c], kvb.at[own], ps_sem, kr_sem.at[own], device_id=partner, device_id_type=MESH)
    pcopy.start()
    kvb[own] = kvs[c]

    sends, outs = [], []
    null = pltpu.make_async_copy(kvu.at[64], kv_out.at[64], us_sem.at[64])
    null.start()
    outs.append(null)

    def send(sid, target):
        cp = pltpu.make_async_remote_copy(
            kvb.at[sid], kvb.at[sid], ks_sem.at[len(sends)], kr_sem.at[sid],
            device_id=target, device_id_type=MESH)
        cp.start()
        sends.append(cp)

    def arrived(sid):
        pltpu.make_async_remote_copy(
            kvb.at[sid], kvb.at[sid], ps_sem, kr_sem.at[sid],
            device_id=partner, device_id_type=MESH).wait_recv()

    def unpack(sid):
        for e in range(2):
            k2 = kvb[sid, 128 * e:128 * e + 64, :].astype(F32)
            r2 = pltpu.roll(k2, 64, 1)
            kvu[sid, e, 0:64, :] = jnp.where(lane < 64, k2, r2).astype(BF)
            kvu[sid, e, 64:128, :] = jnp.where(lane < 64, r2, k2).astype(BF)
            kvu[sid, e, 128:192, :] = kvb[sid, 128 * e + 64:128 * e + 128, :]
            kvu[sid, e, 192:208, :] = jnp.ones((16, 128), BF)
        cp = pltpu.make_async_copy(kvu.at[sid], kv_out.at[sid], us_sem.at[sid])
        cp.start()
        outs.append(cp)

    def block(dy, dz, core):
        return shard_id((y + dy + 4) % 4, (z + dz + 8) % 8, core)

    def q_block(n):
        acc = jnp.zeros((ROWS, 256), F32)
        for i in range(4):
            acc = acc + jnp.dot(
                xb[i], wq[i * feats:(i + 1) * feats, n * 256:(n + 1) * 256], preferred_element_type=F32)
        for u in range(2):
            qs[n * 2 + u] = (turned(acc[:, u * 128:(u + 1) * 128], cos, sin) * 0.125).astype(BF)

    for sid in (own, other):
        if sid is other:
            arrived(other)
        for dy, dz in ((0, 1), (0, -1), (1, 0), (-1, 0)):
            send(sid, plane(dy, dz))

    swap = Swap(lambda i: qs.at[i], lambda m: q_out.at[m], relay, (qs_sem, qr_sem, qq_sem), c, y, z)
    copies[5].wait()
    for n in range(4):
        q_block(n)
    lines = swap.queue()
    swap.step(swap.side)
    q_out[me] = qs[me]
    fresh = [own, other]
    waits = 0
    for op, part, dy, dz in ACTIONS:
        if op == 6:
            if lines[part]:
                swap.step(lines[part].pop(0))
            continue
        sid = block(dy, dz, part)
        if op == 0:
            arrived(sid)
            fresh.append(sid)
            waits += 1
            if waits == 32:
                swap.forward()
            if waits > 12 and waits % 4 != 0:
                unpack(fresh.pop(0))
        elif op == 5:
            sgn = 1 - 2 * c
            send(shard_id((y - sgn + 4) % 4, z, 1), plane(sgn, 0))
        else:
            send(sid, plane(*((0, 1), (0, -1), (1, 0), (-1, 0))[op - 1]))
    for sid in fresh:
        unpack(sid)
    swap.finish()
    for cp in outs:
        cp.wait()
    for cp in sends + [pcopy]:
        cp.wait_send()


def attend_kernel(
    meta, doc_len, sinks, q_ref, kv_hbm, o_ref,
    kv, qsel, mref, aref, buf0, buf1, buf2, buf3, steps, sem,
):
    load = pltpu.make_async_copy(kv_hbm, kv, sem)
    load.start()
    bufs = ((buf0, buf1), (buf2, buf3))
    _, c, y, _ = place()
    base = (c * 4 + y) * 2
    lane = lax.broadcasted_iota(jnp.int32, (1, 256), 1)
    sub = lax.broadcasted_iota(jnp.int32, (TILE, 256), 0)
    sink = jnp.where(lane < 128, sinks[base], sinks[base + 1]) * LOG2E

    def prep(n4, cr):
        for u in range(4):
            n = n4 * 4 + u
            qt = (q_ref[n >> 1, 128 * (u & 1):128 * (u & 1) + 128, :].astype(F32) * LOG2E).T
            qt = jnp.concatenate([qt[:64], qt[64:]], axis=1)
            hi = qt.astype(BF)
            lo = (qt - hi.astype(F32)).astype(BF)
            qsel[n] = jnp.concatenate([hi, lo], axis=0)
        return cr

    lax.fori_loop(0, 4, prep, 0)

    def clear(n, cr):
        mref[n] = sink
        aref[n] = jnp.concatenate([jnp.zeros((64, 256), F32), jnp.ones((16, 256), F32)], axis=0)
        return cr

    lax.fori_loop(0, 18, clear, 0)

    counts = []
    for s in range(2):
        def add(i, cr):
            n = i * 2 + s
            steps[s * 2, i] = n << 7

            def put(ci, k):
                steps[s * 2 + 1, k] = (n << 7) + ci * CH
                return k + 1

            return lax.fori_loop(1, meta[17, n], put, cr)

        counts.append(lax.fori_loop(0, 8, add, jnp.int32(0)))
        steps[s * 2, 8] = (16 + s) << 7
    most = (jnp.maximum(counts[0], counts[1]) + 1) & ~1
    for s in range(2):
        def fill(k, cr):
            steps[s * 2 + 1, k] = (16 + s) << 7
            return cr
        lax.fori_loop(counts[s], most + 1, fill, 0)
    totals = (jnp.int32(8), most)
    load.wait()

    def scores(s, kind, k):
        w = steps[s * 2 + kind, k]
        nn = (w >> 7) & 15
        c0 = w & 127
        js = [meta[nn, c0 + u] for u in range(CH)]
        ks = [kv[j >> 1, j & 1, 0:128, :] for j in js]
        return jnp.dot(jnp.concatenate(ks, axis=0), qsel[nn], preferred_element_type=F32)

    def absorb(s, kind, k, sc):
        w = steps[s * 2 + kind, k]
        n = w >> 7
        nn = n & 15
        c0 = w & 127
        js = [meta[nn, c0 + u] for u in range(CH)]
        vt = jnp.concatenate([kv[j >> 1, j & 1, 128:208, :] for j in js], axis=1)
        mx, acc = mref[n], aref[n]
        if kind == 0:
            qpos = meta[16, nn] * TILE + (lane & 127)
            first = doc_start(doc_len, qpos)
            inside = first > meta[16, nn] * TILE
            mx = jnp.where(inside, sink, mx)
            acc = jnp.where(inside, jnp.concatenate([jnp.zeros((64, 256), F32), jnp.ones((16, 256), F32)], axis=0), acc)
            parts = []
            for u in range(CH):
                part = sc[u * 128:(u + 1) * 128]
                off = js[u] * TILE
                ok = sub >= first - off
                if u == 0:
                    ok = ok & (sub <= qpos - off)
                parts.append(jnp.where(ok, part, -1e30))
            sc = jnp.concatenate(parts, axis=0)
        new = jnp.maximum(mx, jnp.max(sc, axis=0, keepdims=True))
        p = jnp.exp2(sc - new).astype(BF)
        alpha = jnp.exp2(mx - new)
        mref[n] = new
        aref[n] = acc * alpha + jnp.dot(vt, p, preferred_element_type=F32)

    for kind in (1, 0):
        for s in range(2):
            bufs[s][0][...] = scores(s, kind, 0)

        def it(k2, cr):
            for ph in range(2):
                k = k2 * 2 + ph
                for s in range(2):
                    bufs[s][1 - ph][...] = scores(s, kind, k + 1)
                    absorb(s, kind, k, bufs[s][ph][...])
            return cr

        lax.fori_loop(0, totals[kind] >> 1, it, 0)

    def fin(n2, cr):
        for u in range(2):
            a = aref[n2 * 2 + u]
            out = a[:64] / a[64:65]
            out = jnp.concatenate([out[:, :128], out[:, 128:]], axis=0)
            o_ref[n2, 128 * u:128 * u + 128, :] = out.T.astype(BF)
        return cr

    lax.fori_loop(0, 8, fin, 0)


def return_kernel(o_ref, out_ref, relay, s_sem, r_sem, q_sem):
    h, c, y, z = place()
    me = c * 4 + y
    barrier = pltpu.get_barrier_semaphore()
    for d in range(1, 8):
        i = (me + d) % 8
        pl.semaphore_signal(barrier, inc=1, device_id=device(i % 4, z, i // 4), device_id_type=MESH)
    pl.semaphore_wait(barrier, 7)

    def cols(m):
        return pl.ds(pl.multiple_of(m * 128, 128), 128)

    swap = Swap(lambda i: o_ref.at[i], lambda m: out_ref.at[:, cols(m)], relay, (s_sem, r_sem, q_sem), c, y, z)
    swap.start()
    out_ref[:, cols(me)] = o_ref[me]
    swap.forward()
    swap.finish()


def body(tokens, norm_gain, w_query, w_key, w_value, sinks, doc_lengths, tile_mask):
    vm = pl.BlockSpec(memory_space=pltpu.VMEM)
    anym = pl.BlockSpec(memory_space=pl.ANY)
    smem = pl.BlockSpec(memory_space=pltpu.SMEM)
    feats = tokens.shape[1]
    dma = pltpu.SemaphoreType.DMA
    kv, q, lists = pl.pallas_call(
        project_kernel,
        out_shape=(
            jax.ShapeDtypeStruct((65, 2, 208, 128), BF),
            jax.ShapeDtypeStruct((8, ROWS, 128), BF),
            jax.ShapeDtypeStruct((24, 128), jnp.int32),
        ),
        in_specs=[smem] + [anym] * 6,
        out_specs=(anym, vm, vm),
        scratch_shapes=[
            pltpu.VMEM((4, feats, ROWS), BF),
            pltpu.VMEM((4, ROWS, feats), BF),
            pltpu.VMEM((1, 4 * feats), F32),
            pltpu.VMEM((NT, NT), jnp.int32),
            pltpu.VMEM((4 * feats, 1024), BF),
            pltpu.VMEM((4 * feats, 256), BF),
            pltpu.VMEM((2, ROWS, 128), BF),
            pltpu.VMEM((64, ROWS, 128), BF),
            pltpu.VMEM((65, 2, 208, 128), BF),
            pltpu.VMEM((8, ROWS, 128), BF),
            pltpu.VMEM((2, ROWS, 128), BF),
            dma((6,)), dma((6,)), dma((6,)), dma((64,)), dma((64,)), dma, dma((65,)), dma((9,)), dma((8,)), dma((2,)),
        ],
        compiler_params=pltpu.CompilerParams(collective_id=0, has_side_effects=True),
        name="project",
    )(doc_lengths, tokens.T, norm_gain, tile_mask, w_query, w_key, w_value)
    o = pl.pallas_call(
        attend_kernel,
        out_shape=jax.ShapeDtypeStruct((8, ROWS, 128), BF),
        in_specs=[smem, smem, smem, vm, anym],
        out_specs=vm,
        scratch_shapes=[
            pltpu.VMEM((65, 2, 208, 128), BF),
            pltpu.VMEM((16, 128, 256), BF),
            pltpu.VMEM((18, 1, 256), F32),
            pltpu.VMEM((18, 80, 256), F32),
        ] + [pltpu.VMEM((CH * TILE, 256), F32)] * 4 + [pltpu.SMEM((4, 256), jnp.int32), dma],
        name="attend",
    )(lists, doc_lengths, sinks, q, kv)
    return pl.pallas_call(
        return_kernel,
        out_shape=jax.ShapeDtypeStruct((ROWS, 1024), BF),
        in_specs=[vm],
        out_specs=vm,
        scratch_shapes=[pltpu.VMEM((2, ROWS, 128), BF), dma((9,)), dma((8,)), dma((2,))],
        compiler_params=pltpu.CompilerParams(collective_id=1, has_side_effects=True),
        name="give_back",
    )(o)


def solution(mesh):
    in_specs = (
        P(("grp", "blk"), "head"),
        P(),
        P(None, "head"),
        P(None, "head"),
        P(None, "head"),
        P("head"),
        P(),
        P(),
    )
    out_specs = P(("grp", "blk"), "head")
    return jax.shard_map(body, mesh=mesh, in_specs=in_specs, out_specs=out_specs, check_vma=False)
```

```python
import functools

import jax
import jax.numpy as jnp
from jax import lax
from jax.experimental import pallas as pl
from jax.experimental.pallas import tpu as pltpu
from jax.sharding import PartitionSpec as P

MESH = pl.DeviceIdType.MESH
HD = 64
TILE = 128
ROWS = 256
NT = 128
CH = 4
EPS = 1e-05
ROPE_BASE = 150000.0
LOG2E = 1.4426950408889634
ACTIONS = (
    (0, 0, 0, -1), (0, 0, 0, 1), (0, 1, -1, 0), (0, 1, 1, 0), (1, 0, 0, -1), (2, 0, 0, 1), (5, 1, -1, 0),
    (4, 0, 0, -1), (1, 1, -1, 0), (2, 1, 1, 0), (6, 0, 0, 0), (6, 1, 0, 0), (1, 1, 1, 0), (2, 1, -1, 0),
    (6, 0, 0, 0), (6, 1, 0, 0), (0, 1, 0, -1), (0, 1, 0, 1), (0, 0, -1, 0), (0, 0, 1, 0), (1, 1, 0, -1),
    (2, 1, 0, 1), (6, 0, 0, 0), (6, 1, 0, 0), (6, 0, 0, 0), (6, 1, 0, 0), (0, 0, 0, -2), (0, 0, 0, 2),
    (0, 1, 2, 0), (0, 0, 1, -1), (1, 0, 0, -2), (2, 1, 2, 0), (1, 1, 2, 0), (2, 0, 0, 2), (3, 0, 0, -2),
    (4, 0, 0, 1), (0, 1, -1, -1), (0, 1, 1, 1), (1, 1, -1, -1), (2, 1, 1, 1), (3, 0, 0, 2), (4, 0, 0, -2),
    (0, 1, 1, -1), (0, 1, -1, 1), (1, 1, 1, -1), (2, 1, -1, 1), (3, 0, 0, -1), (4, 0, 0, 2), (0, 1, 0, -2),
    (0, 1, 0, 2), (3, 0, 0, 1), (0, 0, 0, -3), (0, 1, 2, 1), (1, 0, 0, -3), (2, 1, 2, 1), (4, 0, 0, -3),
    (1, 1, 0, -2), (2, 1, 0, 2), (3, 0, -1, 0), (0, 1, 2, -1), (0, 0, 0, 3), (0, 0, -1, -2), (0, 0, 1, 1),
    (4, 0, 0, 3), (1, 1, 2, -1), (3, 0, 0, -3), (4, 0, 1, -1), (0, 1, -1, -2), (0, 1, 1, 2), (0, 0, -1, 2),
    (0, 0, 1, -2), (2, 1, 1, 2), (1, 1, -1, -2), (3, 0, 0, 3), (4, 0, 1, 1), (0, 1, 1, -2), (0, 1, -1, 2),
    (0, 0, -1, -1), (0, 0, 1, 2), (2, 1, -1, 2), (1, 1, 1, -2), (0, 0, 0, -4), (0, 1, 2, 2), (0, 0, -1, 1),
    (0, 0, 1, -3), (2, 1, 2, 2), (3, 0, 0, -4), (4, 0, 0, -4), (3, 0, -1, -2), (4, 0, 1, -3), (0, 1, 0, -3),
    (0, 1, 0, 3), (0, 0, 2, 0), (0, 0, 1, 3), (1, 1, 0, -3), (3, 0, -1, 2), (4, 0, 1, 3), (0, 1, 2, -2),
    (0, 1, 1, 3), (0, 0, -1, -3), (0, 0, 2, -1), (2, 1, 1, 3), (1, 1, 2, -2), (0, 1, -1, -3), (0, 1, -1, 3),
    (0, 0, -1, 3), (0, 0, 2, 1), (1, 1, -1, -3), (0, 1, 1, -3), (0, 1, 2, 3), (0, 0, -1, -4), (0, 0, 1, -4),
    (2, 1, 2, 3), (3, 0, -1, -4), (0, 1, 0, -4), (0, 0, 2, -2), (0, 0, 2, -3), (0, 1, 1, 4), (0, 1, 2, -3),
    (0, 0, 2, 2), (0, 0, 2, 3), (0, 1, -1, -4), (0, 1, 2, 4), (0, 0, 2, -4),
)
BF = jnp.bfloat16
F32 = jnp.float32

def place():
    h = lax.axis_index("head")
    g = lax.axis_index("grp")
    b = lax.axis_index("blk")
    c = g % 2
    y = (g // 2) * 2 + b // 8
    z = b % 8
    return h, c, y, z


def device(yy, zz, core):
    return {"grp": (yy // 2) * 2 + core, "blk": (yy % 2) * 8 + zz}


def shard_id(yy, zz, core):
    return (yy // 2) * 32 + core * 16 + (yy % 2) * 8 + zz


class Swap:
    def __init__(self, src, dst, relay, sems, c, y, z):
        self.src, self.dst, self.relay = src, dst, relay
        self.s_sem, self.r_sem, self.q_sem = sems
        self.c, self.y, self.z = c, y, z
        self.me = c * 4 + y
        self.up, self.down, self.far = (y + 1) % 4, (y + 3) % 4, (y + 2) % 4
        self.sent = []

    def go(self, src, dst, r_sem, target):
        cp = pltpu.make_async_remote_copy(
            src, dst, self.s_sem.at[len(self.sent)], r_sem, device_id=target, device_id_type=MESH)
        cp.start()
        self.sent.append(cp)

    def await_at(self, dst, r_sem):
        pltpu.make_async_remote_copy(
            dst, dst, self.s_sem.at[0], r_sem,
            device_id=device(self.y, self.z, 1 - self.c), device_id_type=MESH).wait_recv()

    def queue(self):
        c, z, me = self.c, self.z, self.me
        ups = [(self.far, self.relay.at[0], self.q_sem.at[0], device(self.up, z, c))]
        downs = [(4 + self.far, self.relay.at[1], self.q_sem.at[1], device(self.down, z, c))]
        for core in range(2):
            ups.append((core * 4 + self.up, self.dst(me), self.r_sem.at[me], device(self.up, z, core)))
            downs.append((core * 4 + self.down, self.dst(me), self.r_sem.at[me], device(self.down, z, core)))
        self.side = ((1 - c) * 4 + self.y, self.dst(me), self.r_sem.at[me], device(self.y, z, 1 - c))
        return ups, downs

    def step(self, entry):
        i, dst, r_sem, target = entry
        self.go(self.src(i), dst, r_sem, target)

    def start(self):
        for pair in zip(*self.queue()):
            for entry in pair:
                self.step(entry)
        self.step(self.side)

    def forward(self):
        c, z = self.c, self.z
        below, above = c * 4 + self.down, c * 4 + self.up
        self.await_at(self.relay.at[0], self.q_sem.at[0])
        self.go(self.relay.at[0], self.dst(below), self.r_sem.at[below], device(self.up, z, 0))
        self.await_at(self.relay.at[1], self.q_sem.at[1])
        self.go(self.relay.at[1], self.dst(above), self.r_sem.at[above], device(self.down, z, 1))

    def finish(self):
        for d in range(1, 8):
            i = (self.me + d) % 8
            self.await_at(self.dst(i), self.r_sem.at[i])
        for cp in self.sent:
            cp.wait_send()


def turned(x, cos, sin):
    lane = lax.broadcasted_iota(jnp.int32, x.shape, 1)
    other = jnp.where(lane % 64 < 32, pltpu.roll(x, 96, 1), pltpu.roll(x, 32, 1))
    return x * cos + other * sin


def angles(base):
    lane = lax.broadcasted_iota(jnp.int32, (1, 128), 1)
    freq = jnp.zeros((1, 128), F32)
    for i in range(HD // 2):
        freq = jnp.where(lane % 32 == i, ROPE_BASE ** (-2.0 * i / HD), freq)
    pos = lax.broadcasted_iota(jnp.int32, (ROWS, 128), 0) + base
    ang = pos.astype(F32) * freq
    sin = jnp.sin(ang)
    return jnp.cos(ang), jnp.where(lane % 64 < 32, -sin, sin)


def doc_start(doc_len, pos):
    end = jnp.int32(0)
    first = jnp.zeros_like(pos)
    for d in range(doc_len.shape[0]):
        end = end + doc_len[d]
        first = jnp.maximum(first, jnp.where(end <= pos, end, 0))
    return first


def key_lists(doc_len, tile_mask, z, lists):
    n = lax.broadcasted_iota(jnp.int32, (1, 128), 1)
    i = n // 2
    yy, core = i % 4, i // 4
    tile = shard_id(yy, z, core) * 2 + n % 2
    first = doc_start(doc_len, tile * TILE)
    last = doc_start(doc_len, tile * TILE + TILE - 1)
    j = lax.broadcasted_iota(jnp.int32, (NT, 128), 0)
    k = lax.broadcasted_iota(jnp.int32, (NT, 128), 1)
    pick = jnp.where(j == tile, 1.0, 0.0).astype(BF)
    listed = jnp.dot(tile_mask[...].astype(F32).T.astype(BF), pick, preferred_element_type=F32) > 0.5
    active = (listed | (j == tile)) & (j <= tile) & (j * TILE + TILE > first)
    act = jnp.where(active, 1.0, 0.0).astype(BF)
    lower = jnp.where(k < j, 1.0, 0.0).astype(BF)
    before = jnp.dot(lower, act, preferred_element_type=F32).astype(jnp.int32)
    spot = jnp.where(active, jnp.where(j == tile, 0, before + 1), -1)
    count = jnp.sum(jnp.where(active, 1, 0), axis=0, keepdims=True)
    for r in range(16):
        hit = spot[:, r:r + 1] == k
        lists[r:r + 1, :] = jnp.sum(jnp.where(hit, j - NT, 0), axis=0, keepdims=True) + NT
    lists[16:17, :] = tile
    lists[17:18, :] = (count + CH - 1) // CH
    lists[18:19, :] = jnp.where(first == last, 0, 1)
    lists[19:24, :] = jnp.zeros((5, 128), jnp.int32)


def project_kernel(
    doc_len, tok_hbm, gain_hbm, mask_hbm, wq_hbm, wk_hbm, wv_hbm,
    kv_out, q_out, lists,
    xt, xb, gain, mask, wq, wkv, kvs, kvb, kvu, qs, relay,
    wsem, xs_sem, xr_sem, ks_sem, kr_sem, ps_sem, us_sem, qs_sem, qr_sem, qq_sem,
):
    h, c, y, z = place()
    me = c * 4 + y
    feats = xb.shape[2]
    half = ROWS // 2

    copies = [
        pltpu.make_async_copy(tok_hbm, xt.at[h], wsem.at[0]),
        pltpu.make_async_copy(gain_hbm, gain.at[0], wsem.at[1]),
        pltpu.make_async_copy(mask_hbm, mask, wsem.at[2]),
        pltpu.make_async_copy(wk_hbm, wkv.at[:, 0:128], wsem.at[3]),
        pltpu.make_async_copy(wv_hbm, wkv.at[:, 128:256], wsem.at[4]),
        pltpu.make_async_copy(wq_hbm, wq, wsem.at[5]),
    ]
    for cp in copies:
        cp.start()

    def plane(dy, dz):
        return device((y + dy + 4) % 4, (z + dz + 8) % 8, c)

    def mate(d):
        i = (me + d) % 8
        return i, device(i % 4, z, i // 4)

    partner = device(y, z, 1 - c)
    ahead, behind, across = (h + 1) % 4, (h + 3) % 4, (h + 2) % 4
    barrier = pltpu.get_barrier_semaphore()
    for x in (ahead, behind):
        pl.semaphore_signal(barrier, inc=1, device_id={"head": x}, device_id_type=MESH)
    for dz in (1, -1):
        pl.semaphore_signal(barrier, inc=1, device_id=plane(0, dz), device_id_type=MESH)
    for d in range(1, 8):
        pl.semaphore_signal(barrier, inc=1, device_id=mate(d)[1], device_id_type=MESH)
    pl.semaphore_wait(barrier, 11)
    copies[0].wait()

    xsent = []
    top, low = pl.ds(0, half), pl.ds(half, half)

    def xsend(n, src, rows, to):
        cp = pltpu.make_async_remote_copy(
            xt.at[src, :, rows], xt.at[src, :, rows], xs_sem.at[n], xr_sem.at[n],
            device_id={"head": to}, device_id_type=MESH)
        cp.start()
        xsent.append(cp)

    def xwait(n, src, rows):
        pltpu.make_async_remote_copy(
            xt.at[src, :, rows], xt.at[src, :, rows], xs_sem.at[n], xr_sem.at[n],
            device_id={"head": ahead}, device_id_type=MESH).wait_recv()

    xsend(0, h, top, ahead)
    xsend(1, h, low, behind)
    xsend(2, h, low, ahead)
    xsend(3, h, top, behind)
    cos, sin = angles(shard_id(y, z, c) * ROWS)
    xwait(0, behind, top)
    xsend(4, behind, top, ahead)
    xwait(1, ahead, low)
    xsend(5, ahead, low, behind)

    copies[2].wait()
    key_lists(doc_len, mask, z, lists)
    kvu[64] = jnp.zeros((2, 208, 128), BF)
    copies[1].wait()

    def squares(i):
        w = xt[i].astype(F32).T
        xb[i] = w.astype(BF)
        return jnp.sum(w * w, axis=1, keepdims=True)

    total = squares(h)
    xwait(2, behind, low)
    total = total + squares(behind)
    xwait(3, ahead, top)
    total = total + squares(ahead)
    xwait(4, across, top)
    xwait(5, across, low)
    total = total + squares(across)
    scale = lax.rsqrt(total / (4 * feats) + EPS)
    for cp in xsent:
        cp.wait_send()
    copies[3].wait()
    copies[4].wait()
    kvp = jnp.zeros((ROWS, 256), F32)
    for i in range(4):
        w = xb[i].astype(F32) * scale * gain[:, i * feats:(i + 1) * feats]
        w = w.astype(BF)
        xb[i] = w
        kvp = kvp + jnp.dot(w, wkv[i * feats:(i + 1) * feats, :], preferred_element_type=F32)
    k = turned(kvp[:, :128], cos, sin)
    v = kvp[:, 128:]
    lane = lax.broadcasted_iota(jnp.int32, (64, 128), 1)
    for e in range(2):
        k0, k1 = k[128 * e:128 * e + 64], k[128 * e + 64:128 * e + 128]
        vt = v[128 * e:128 * (e + 1)].T.astype(BF)
        kvs[0, 128 * e:128 * e + 64, :] = jnp.where(lane < 64, k0, pltpu.roll(k1, 64, 1)).astype(BF)
        kvs[1, 128 * e:128 * e + 64, :] = jnp.where(lane < 64, pltpu.roll(k0, 64, 1), k1).astype(BF)
        for cc in range(2):
            kvs[cc, 128 * e + 64:128 * e + 128, :] = vt[64 * cc:64 * (cc + 1)]
    own = shard_id(y, z, c)
    other = shard_id(y, z, 1 - c)
    pcopy = pltpu.make_async_remote_copy(
        kvs.at[1 - c], kvb.at[own], ps_sem, kr_sem.at[own], device_id=partner, device_id_type=MESH)
    pcopy.start()
    kvb[own] = kvs[c]

    sends, outs = [], []
    null = pltpu.make_async_copy(kvu.at[64], kv_out.at[64], us_sem.at[64])
    null.start()
    outs.append(null)

    def send(sid, target):
        cp = pltpu.make_async_remote_copy(
            kvb.at[sid], kvb.at[sid], ks_sem.at[len(sends)], kr_sem.at[sid],
            device_id=target, device_id_type=MESH)
        cp.start()
        sends.append(cp)

    def arrived(sid):
        pltpu.make_async_remote_copy(
            kvb.at[sid], kvb.at[sid], ps_sem, kr_sem.at[sid],
            device_id=partner, device_id_type=MESH).wait_recv()

    def unpack(sid):
        for e in range(2):
            k2 = kvb[sid, 128 * e:128 * e + 64, :].astype(F32)
            r2 = pltpu.roll(k2, 64, 1)
            kvu[sid, e, 0:64, :] = jnp.where(lane < 64, k2, r2).astype(BF)
            kvu[sid, e, 64:128, :] = jnp.where(lane < 64, r2, k2).astype(BF)
            kvu[sid, e, 128:192, :] = kvb[sid, 128 * e + 64:128 * e + 128, :]
            kvu[sid, e, 192:208, :] = jnp.ones((16, 128), BF)
        cp = pltpu.make_async_copy(kvu.at[sid], kv_out.at[sid], us_sem.at[sid])
        cp.start()
        outs.append(cp)

    def block(dy, dz, core):
        return shard_id((y + dy + 4) % 4, (z + dz + 8) % 8, core)

    def q_block(n):
        acc = jnp.zeros((ROWS, 256), F32)
        for i in range(4):
            acc = acc + jnp.dot(
                xb[i], wq[i * feats:(i + 1) * feats, n * 256:(n + 1) * 256], preferred_element_type=F32)
        for u in range(2):
            qs[n * 2 + u] = (turned(acc[:, u * 128:(u + 1) * 128], cos, sin) * 0.125).astype(BF)

    for sid in (own, other):
        if sid is other:
            arrived(other)
        for dy, dz in ((0, 1), (0, -1), (1, 0), (-1, 0)):
            send(sid, plane(dy, dz))

    swap = Swap(lambda i: qs.at[i], lambda m: q_out.at[m], relay, (qs_sem, qr_sem, qq_sem), c, y, z)
    copies[5].wait()
    for n in range(4):
        q_block(n)
    lines = swap.queue()
    swap.step(swap.side)
    q_out[me] = qs[me]
    fresh = [own, other]
    waits = 0
    for op, part, dy, dz in ACTIONS:
        if op == 6:
            if lines[part]:
                swap.step(lines[part].pop(0))
            continue
        sid = block(dy, dz, part)
        if op == 0:
            arrived(sid)
            fresh.append(sid)
            waits += 1
            if waits == 32:
                swap.forward()
            if waits > 12 and waits % 4 != 0:
                unpack(fresh.pop(0))
        elif op == 5:
            sgn = 1 - 2 * c
            send(shard_id((y - sgn + 4) % 4, z, 1), plane(sgn, 0))
        else:
            send(sid, plane(*((0, 1), (0, -1), (1, 0), (-1, 0))[op - 1]))
    for sid in fresh:
        unpack(sid)
    swap.finish()
    for cp in outs:
        cp.wait()
    for cp in sends + [pcopy]:
        cp.wait_send()


def attend_kernel(
    meta, doc_len, sinks, q_ref, kv_hbm, o_ref,
    kv, qsel, mref, aref, buf0, buf1, buf2, buf3, tops, firsts, steps, sem,
):
    load = pltpu.make_async_copy(kv_hbm, kv, sem)
    load.start()
    bufs = ((buf0, buf1), (buf2, buf3))
    _, c, y, _ = place()
    base = (c * 4 + y) * 2
    lane = lax.broadcasted_iota(jnp.int32, (1, 256), 1)
    sub = lax.broadcasted_iota(jnp.int32, (TILE, 256), 0)
    sink = jnp.where(lane < 128, sinks[base], sinks[base + 1]) * LOG2E

    blank = jnp.concatenate([jnp.zeros((64, 256), F32), jnp.ones((16, 256), F32)], axis=0)

    def prep(n4, cr):
        for u in range(4):
            n = n4 * 4 + u
            qt = (q_ref[n >> 1, 128 * (u & 1):128 * (u & 1) + 128, :].astype(F32) * LOG2E).T
            qt = jnp.concatenate([qt[:64], qt[64:]], axis=1)
            hi = qt.astype(BF)
            lo = (qt - hi.astype(F32)).astype(BF)
            qsel[n] = jnp.concatenate([hi, lo], axis=0)
            tile = meta[16, n] * TILE
            firsts[n] = doc_start(doc_len, tile + (lane & 127)) - tile
            mref[n] = sink
            aref[n] = blank
        return cr

    lax.fori_loop(0, 4, prep, 0)

    for n in range(16, 18):
        mref[n] = sink
        aref[n] = blank

    counts = []
    for s in range(2):
        def add(i, cr):
            n = i * 2 + s
            steps[s * 2, i] = n << 7

            def put(ci, k):
                steps[s * 2 + 1, k] = (n << 7) + ci * CH
                return k + 1

            return lax.fori_loop(1, meta[17, n], put, cr)

        counts.append(lax.fori_loop(0, 8, add, jnp.int32(0)))
        steps[s * 2, 8] = (16 + s) << 7
    most = (jnp.maximum(counts[0], counts[1]) + 1) & ~1
    for s in range(2):
        def fill(k, cr):
            steps[s * 2 + 1, k] = (16 + s) << 7
            return cr
        lax.fori_loop(counts[s], most + 1, fill, 0)
    totals = (jnp.int32(8), most)
    load.wait()

    def scores(s, kind, k, ph):
        w = steps[s * 2 + kind, k]
        nn = (w >> 7) & 15
        c0 = w & 127
        js = [meta[nn, c0 + u] for u in range(CH)]
        ks = [kv[j >> 1, j & 1, 0:128, :] for j in js]
        sc = jnp.dot(jnp.concatenate(ks, axis=0), qsel[nn], preferred_element_type=F32)
        if kind == 0:
            first = firsts[nn]
            parts = []
            for u in range(CH):
                if u == 0:
                    ok = (sub >= first) & (sub <= (lane & 127))
                else:
                    ok = sub >= first + (meta[16, nn] - js[u]) * TILE
                parts.append(jnp.where(ok, sc[u * 128:(u + 1) * 128], -1e30))
            sc = jnp.concatenate(parts, axis=0)
        bufs[s][ph][...] = sc
        tops[s * 2 + ph] = jnp.max(sc, axis=0, keepdims=True)

    def absorb(s, kind, k, ph):
        w = steps[s * 2 + kind, k]
        n = w >> 7
        nn = n & 15
        c0 = w & 127
        js = [meta[nn, c0 + u] for u in range(CH)]
        vt = jnp.concatenate([kv[j >> 1, j & 1, 128:208, :] for j in js], axis=1)
        mx, acc = mref[n], aref[n]
        if kind == 0:
            inside = firsts[nn] > 0
            mx = jnp.where(inside, sink, mx)
            acc = jnp.where(inside, blank, acc)
        new = jnp.maximum(mx, tops[s * 2 + ph])
        p = jnp.exp2(bufs[s][ph][...] - new).astype(BF)
        alpha = jnp.exp2(mx - new)
        mref[n] = new
        aref[n] = acc * alpha + jnp.dot(vt, p, preferred_element_type=F32)

    for kind in (1, 0):
        for s in range(2):
            scores(s, kind, 0, 0)

        def it(k2, cr):
            for ph in range(2):
                k = k2 * 2 + ph
                for s in range(2):
                    scores(s, kind, k + 1, 1 - ph)
                for s in range(2):
                    absorb(s, kind, k, ph)
            return cr

        lax.fori_loop(0, totals[kind] >> 1, it, 0)

    def fin(n4, cr):
        for u in range(4):
            a = aref[n4 * 4 + u]
            out = a[:64] / a[64:65]
            out = jnp.concatenate([out[:, :128], out[:, 128:]], axis=0)
            o_ref[n4 * 2 + u // 2, 128 * (u % 2):128 * (u % 2) + 128, :] = out.T.astype(BF)
        return cr

    lax.fori_loop(0, 4, fin, 0)


def return_kernel(o_ref, out_ref, relay, s_sem, r_sem, q_sem):
    h, c, y, z = place()
    me = c * 4 + y
    barrier = pltpu.get_barrier_semaphore()
    for d in range(1, 8):
        i = (me + d) % 8
        pl.semaphore_signal(barrier, inc=1, device_id=device(i % 4, z, i // 4), device_id_type=MESH)
    pl.semaphore_wait(barrier, 7)

    def cols(m):
        return pl.ds(pl.multiple_of(m * 128, 128), 128)

    swap = Swap(lambda i: o_ref.at[i], lambda m: out_ref.at[:, cols(m)], relay, (s_sem, r_sem, q_sem), c, y, z)
    swap.start()
    out_ref[:, cols(me)] = o_ref[me]
    swap.forward()
    swap.finish()


def body(tokens, norm_gain, w_query, w_key, w_value, sinks, doc_lengths, tile_mask):
    vm = pl.BlockSpec(memory_space=pltpu.VMEM)
    anym = pl.BlockSpec(memory_space=pl.ANY)
    smem = pl.BlockSpec(memory_space=pltpu.SMEM)
    feats = tokens.shape[1]
    dma = pltpu.SemaphoreType.DMA
    kv, q, lists = pl.pallas_call(
        project_kernel,
        out_shape=(
            jax.ShapeDtypeStruct((65, 2, 208, 128), BF),
            jax.ShapeDtypeStruct((8, ROWS, 128), BF),
            jax.ShapeDtypeStruct((24, 128), jnp.int32),
        ),
        in_specs=[smem] + [anym] * 6,
        out_specs=(anym, vm, vm),
        scratch_shapes=[
            pltpu.VMEM((4, feats, ROWS), BF),
            pltpu.VMEM((4, ROWS, feats), BF),
            pltpu.VMEM((1, 4 * feats), F32),
            pltpu.VMEM((NT, NT), jnp.int32),
            pltpu.VMEM((4 * feats, 1024), BF),
            pltpu.VMEM((4 * feats, 256), BF),
            pltpu.VMEM((2, ROWS, 128), BF),
            pltpu.VMEM((64, ROWS, 128), BF),
            pltpu.VMEM((65, 2, 208, 128), BF),
            pltpu.VMEM((8, ROWS, 128), BF),
            pltpu.VMEM((2, ROWS, 128), BF),
            dma((6,)), dma((6,)), dma((6,)), dma((64,)), dma((64,)), dma, dma((65,)), dma((9,)), dma((8,)), dma((2,)),
        ],
        compiler_params=pltpu.CompilerParams(collective_id=0, has_side_effects=True),
        name="project",
    )(doc_lengths, tokens.T, norm_gain, tile_mask, w_query, w_key, w_value)
    o = pl.pallas_call(
        attend_kernel,
        out_shape=jax.ShapeDtypeStruct((8, ROWS, 128), BF),
        in_specs=[smem, smem, smem, vm, anym],
        out_specs=vm,
        scratch_shapes=[
            pltpu.VMEM((65, 2, 208, 128), BF),
            pltpu.VMEM((16, 128, 256), BF),
            pltpu.VMEM((18, 1, 256), F32),
            pltpu.VMEM((18, 80, 256), F32),
        ] + [pltpu.VMEM((CH * TILE, 256), F32)] * 4 + [pltpu.VMEM((4, 1, 256), F32), pltpu.VMEM((16, 1, 256), jnp.int32), pltpu.SMEM((4, 256), jnp.int32), dma],
        name="attend",
    )(lists, doc_lengths, sinks, q, kv)
    return pl.pallas_call(
        return_kernel,
        out_shape=jax.ShapeDtypeStruct((ROWS, 1024), BF),
        in_specs=[vm],
        out_specs=vm,
        scratch_shapes=[pltpu.VMEM((2, ROWS, 128), BF), dma((9,)), dma((8,)), dma((2,))],
        compiler_params=pltpu.CompilerParams(collective_id=1, has_side_effects=True),
        name="give_back",
    )(o)


def solution(mesh):
    in_specs = (
        P(("grp", "blk"), "head"),
        P(),
        P(None, "head"),
        P(None, "head"),
        P(None, "head"),
        P("head"),
        P(),
        P(),
    )
    out_specs = P(("grp", "blk"), "head")
    return jax.shard_map(body, mesh=mesh, in_specs=in_specs, out_specs=out_specs, check_vma=False)
```

```python
import functools

import jax
import jax.numpy as jnp
from jax import lax
from jax.experimental import pallas as pl
from jax.experimental.pallas import tpu as pltpu
from jax.sharding import PartitionSpec as P

MESH = pl.DeviceIdType.MESH
HD = 64
TILE = 128
ROWS = 256
NT = 128
CH = 4
EPS = 1e-05
ROPE_BASE = 150000.0
LOG2E = 1.4426950408889634
ACTIONS = (
    (0, 0, 0, -1), (0, 0, 0, 1), (0, 1, -1, 0), (0, 1, 1, 0), (1, 0, 0, -1), (2, 0, 0, 1), (5, 1, -1, 0),
    (4, 0, 0, -1), (1, 1, -1, 0), (2, 1, 1, 0), (6, 0, 0, 0), (6, 1, 0, 0), (1, 1, 1, 0), (2, 1, -1, 0),
    (6, 0, 0, 0), (6, 1, 0, 0), (0, 1, 0, -1), (0, 1, 0, 1), (0, 0, -1, 0), (0, 0, 1, 0), (1, 1, 0, -1),
    (2, 1, 0, 1), (6, 0, 0, 0), (6, 1, 0, 0), (6, 0, 0, 0), (6, 1, 0, 0), (0, 0, 0, -2), (0, 0, 0, 2),
    (0, 1, 2, 0), (0, 0, 1, -1), (1, 0, 0, -2), (2, 1, 2, 0), (1, 1, 2, 0), (2, 0, 0, 2), (3, 0, 0, -2),
    (4, 0, 0, 1), (0, 1, -1, -1), (0, 1, 1, 1), (1, 1, -1, -1), (2, 1, 1, 1), (3, 0, 0, 2), (4, 0, 0, -2),
    (0, 1, 1, -1), (0, 1, -1, 1), (1, 1, 1, -1), (2, 1, -1, 1), (3, 0, 0, -1), (4, 0, 0, 2), (0, 1, 0, -2),
    (0, 1, 0, 2), (3, 0, 0, 1), (0, 0, 0, -3), (0, 1, 2, 1), (1, 0, 0, -3), (2, 1, 2, 1), (4, 0, 0, -3),
    (1, 1, 0, -2), (2, 1, 0, 2), (3, 0, -1, 0), (0, 1, 2, -1), (0, 0, 0, 3), (0, 0, -1, -2), (0, 0, 1, 1),
    (4, 0, 0, 3), (1, 1, 2, -1), (3, 0, 0, -3), (4, 0, 1, -1), (0, 1, -1, -2), (0, 1, 1, 2), (0, 0, -1, 2),
    (0, 0, 1, -2), (2, 1, 1, 2), (1, 1, -1, -2), (3, 0, 0, 3), (4, 0, 1, 1), (0, 1, 1, -2), (0, 1, -1, 2),
    (0, 0, -1, -1), (0, 0, 1, 2), (2, 1, -1, 2), (1, 1, 1, -2), (0, 0, 0, -4), (0, 1, 2, 2), (0, 0, -1, 1),
    (0, 0, 1, -3), (2, 1, 2, 2), (3, 0, 0, -4), (4, 0, 0, -4), (3, 0, -1, -2), (4, 0, 1, -3), (0, 1, 0, -3),
    (0, 1, 0, 3), (0, 0, 2, 0), (0, 0, 1, 3), (1, 1, 0, -3), (3, 0, -1, 2), (4, 0, 1, 3), (0, 1, 2, -2),
    (0, 1, 1, 3), (0, 0, -1, -3), (0, 0, 2, -1), (2, 1, 1, 3), (1, 1, 2, -2), (0, 1, -1, -3), (0, 1, -1, 3),
    (0, 0, -1, 3), (0, 0, 2, 1), (1, 1, -1, -3), (0, 1, 1, -3), (0, 1, 2, 3), (0, 0, -1, -4), (0, 0, 1, -4),
    (2, 1, 2, 3), (3, 0, -1, -4), (0, 1, 0, -4), (0, 0, 2, -2), (0, 0, 2, -3), (0, 1, 1, 4), (0, 1, 2, -3),
    (0, 0, 2, 2), (0, 0, 2, 3), (0, 1, -1, -4), (0, 1, 2, 4), (0, 0, 2, -4),
)
BF = jnp.bfloat16
F32 = jnp.float32

def place():
    h = lax.axis_index("head")
    g = lax.axis_index("grp")
    b = lax.axis_index("blk")
    c = g % 2
    y = (g // 2) * 2 + b // 8
    z = b % 8
    return h, c, y, z


def device(yy, zz, core):
    return {"grp": (yy // 2) * 2 + core, "blk": (yy % 2) * 8 + zz}


def shard_id(yy, zz, core):
    return (yy // 2) * 32 + core * 16 + (yy % 2) * 8 + zz


class Swap:
    def __init__(self, src, dst, relay, sems, c, y, z):
        self.src, self.dst, self.relay = src, dst, relay
        self.s_sem, self.r_sem, self.q_sem = sems
        self.c, self.y, self.z = c, y, z
        self.me = c * 4 + y
        self.up, self.down, self.far = (y + 1) % 4, (y + 3) % 4, (y + 2) % 4
        self.sent = []

    def go(self, src, dst, r_sem, target):
        cp = pltpu.make_async_remote_copy(
            src, dst, self.s_sem.at[len(self.sent)], r_sem, device_id=target, device_id_type=MESH)
        cp.start()
        self.sent.append(cp)

    def await_at(self, dst, r_sem):
        pltpu.make_async_remote_copy(
            dst, dst, self.s_sem.at[0], r_sem,
            device_id=device(self.y, self.z, 1 - self.c), device_id_type=MESH).wait_recv()

    def queue(self):
        c, z, me = self.c, self.z, self.me
        ups = [(self.far, self.relay.at[0], self.q_sem.at[0], device(self.up, z, c))]
        downs = [(4 + self.far, self.relay.at[1], self.q_sem.at[1], device(self.down, z, c))]
        for core in range(2):
            ups.append((core * 4 + self.up, self.dst(me), self.r_sem.at[me], device(self.up, z, core)))
            downs.append((core * 4 + self.down, self.dst(me), self.r_sem.at[me], device(self.down, z, core)))
        self.side = ((1 - c) * 4 + self.y, self.dst(me), self.r_sem.at[me], device(self.y, z, 1 - c))
        return ups, downs

    def step(self, entry):
        i, dst, r_sem, target = entry
        self.go(self.src(i), dst, r_sem, target)

    def start(self):
        for pair in zip(*self.queue()):
            for entry in pair:
                self.step(entry)
        self.step(self.side)

    def forward(self):
        c, z = self.c, self.z
        below, above = c * 4 + self.down, c * 4 + self.up
        self.await_at(self.relay.at[0], self.q_sem.at[0])
        self.go(self.relay.at[0], self.dst(below), self.r_sem.at[below], device(self.up, z, 0))
        self.await_at(self.relay.at[1], self.q_sem.at[1])
        self.go(self.relay.at[1], self.dst(above), self.r_sem.at[above], device(self.down, z, 1))

    def finish(self):
        for d in range(1, 8):
            i = (self.me + d) % 8
            self.await_at(self.dst(i), self.r_sem.at[i])
        for cp in self.sent:
            cp.wait_send()


def turned(x, cos, sin):
    lane = lax.broadcasted_iota(jnp.int32, x.shape, 1)
    other = jnp.where(lane % 64 < 32, pltpu.roll(x, 96, 1), pltpu.roll(x, 32, 1))
    return x * cos + other * sin


def angles(base):
    lane = lax.broadcasted_iota(jnp.int32, (1, 128), 1)
    freq = jnp.zeros((1, 128), F32)
    for i in range(HD // 2):
        freq = jnp.where(lane % 32 == i, ROPE_BASE ** (-2.0 * i / HD), freq)
    pos = lax.broadcasted_iota(jnp.int32, (ROWS, 128), 0) + base
    ang = pos.astype(F32) * freq
    sin = jnp.sin(ang)
    return jnp.cos(ang), jnp.where(lane % 64 < 32, -sin, sin)


def doc_start(doc_len, pos):
    end = jnp.int32(0)
    first = jnp.zeros_like(pos)
    for d in range(doc_len.shape[0]):
        end = end + doc_len[d]
        first = jnp.maximum(first, jnp.where(end <= pos, end, 0))
    return first


def key_lists(doc_len, tile_mask, z, lists):
    n = lax.broadcasted_iota(jnp.int32, (1, 128), 1)
    i = n // 2
    yy, core = i % 4, i // 4
    tile = shard_id(yy, z, core) * 2 + n % 2
    first = doc_start(doc_len, tile * TILE)
    last = doc_start(doc_len, tile * TILE + TILE - 1)
    j = lax.broadcasted_iota(jnp.int32, (NT, 128), 0)
    k = lax.broadcasted_iota(jnp.int32, (NT, 128), 1)
    pick = jnp.where(j == tile, 1.0, 0.0).astype(BF)
    listed = jnp.dot(tile_mask[...].astype(F32).T.astype(BF), pick, preferred_element_type=F32) > 0.5
    active = (listed | (j == tile)) & (j <= tile) & (j * TILE + TILE > first)
    act = jnp.where(active, 1.0, 0.0).astype(BF)
    lower = jnp.where(k < j, 1.0, 0.0).astype(BF)
    before = jnp.dot(lower, act, preferred_element_type=F32).astype(jnp.int32)
    spot = jnp.where(active, jnp.where(j == tile, 0, before + 1), -1)
    count = jnp.sum(jnp.where(active, 1, 0), axis=0, keepdims=True)
    for r in range(16):
        hit = spot[:, r:r + 1] == k
        lists[r:r + 1, :] = jnp.sum(jnp.where(hit, j - NT, 0), axis=0, keepdims=True) + NT
    lists[16:17, :] = tile
    lists[17:18, :] = (count + CH - 1) // CH
    lists[18:19, :] = jnp.where(first == last, 0, 1)
    lists[19:24, :] = jnp.zeros((5, 128), jnp.int32)


def project_kernel(
    doc_len, tok_hbm, gain_hbm, mask_hbm, wq_hbm, wk_hbm, wv_hbm,
    kv_out, q_out, lists,
    xt, xb, gain, mask, wq, wkv, kvs, kvb, kvu, qs, relay,
    wsem, xs_sem, xr_sem, ks_sem, kr_sem, ps_sem, us_sem, qs_sem, qr_sem, qq_sem, own_sem,
):
    h, c, y, z = place()
    me = c * 4 + y
    feats = xb.shape[2]
    half = ROWS // 2

    copies = [
        pltpu.make_async_copy(tok_hbm, xt.at[h], wsem.at[0]),
        pltpu.make_async_copy(gain_hbm, gain.at[0], wsem.at[1]),
        pltpu.make_async_copy(mask_hbm, mask, wsem.at[2]),
        pltpu.make_async_copy(wk_hbm, wkv.at[:, 0:128], wsem.at[3]),
        pltpu.make_async_copy(wv_hbm, wkv.at[:, 128:256], wsem.at[4]),
        pltpu.make_async_copy(wq_hbm, wq, wsem.at[5]),
    ]
    for cp in copies:
        cp.start()

    def plane(dy, dz):
        return device((y + dy + 4) % 4, (z + dz + 8) % 8, c)

    def mate(d):
        i = (me + d) % 8
        return i, device(i % 4, z, i // 4)

    partner = device(y, z, 1 - c)
    ahead, behind, across = (h + 1) % 4, (h + 3) % 4, (h + 2) % 4
    barrier = pltpu.get_barrier_semaphore()
    for x in (ahead, behind):
        pl.semaphore_signal(barrier, inc=1, device_id={"head": x}, device_id_type=MESH)
    for dz in (1, -1):
        pl.semaphore_signal(barrier, inc=1, device_id=plane(0, dz), device_id_type=MESH)
    for d in range(1, 8):
        pl.semaphore_signal(barrier, inc=1, device_id=mate(d)[1], device_id_type=MESH)
    pl.semaphore_wait(barrier, 11)
    copies[0].wait()

    xsent = []
    top, low = pl.ds(0, half), pl.ds(half, half)

    def xsend(n, src, rows, to):
        cp = pltpu.make_async_remote_copy(
            xt.at[src, :, rows], xt.at[src, :, rows], xs_sem.at[n], xr_sem.at[n],
            device_id={"head": to}, device_id_type=MESH)
        cp.start()
        xsent.append(cp)

    def xwait(n, src, rows):
        pltpu.make_async_remote_copy(
            xt.at[src, :, rows], xt.at[src, :, rows], xs_sem.at[n], xr_sem.at[n],
            device_id={"head": ahead}, device_id_type=MESH).wait_recv()

    xsend(0, h, top, ahead)
    xsend(1, h, low, behind)
    xsend(2, h, low, ahead)
    xsend(3, h, top, behind)
    cos, sin = angles(shard_id(y, z, c) * ROWS)
    xwait(0, behind, top)
    xsend(4, behind, top, ahead)
    xwait(1, ahead, low)
    xsend(5, ahead, low, behind)

    copies[2].wait()
    key_lists(doc_len, mask, z, lists)
    kvu[64] = jnp.zeros((2, 208, 128), BF)
    copies[1].wait()

    def squares(i):
        w = xt[i].astype(F32).T
        xb[i] = w.astype(BF)
        return jnp.sum(w * w, axis=1, keepdims=True)

    total = squares(h)
    xwait(2, behind, low)
    total = total + squares(behind)
    xwait(3, ahead, top)
    total = total + squares(ahead)
    xwait(4, across, top)
    xwait(5, across, low)
    total = total + squares(across)
    scale = lax.rsqrt(total / (4 * feats) + EPS)
    for cp in xsent:
        cp.wait_send()
    copies[3].wait()
    copies[4].wait()
    kvp = jnp.zeros((ROWS, 256), F32)
    for i in range(4):
        w = xb[i].astype(F32) * scale * gain[:, i * feats:(i + 1) * feats]
        w = w.astype(BF)
        xb[i] = w
        kvp = kvp + jnp.dot(w, wkv[i * feats:(i + 1) * feats, :], preferred_element_type=F32)
    k = turned(kvp[:, :128], cos, sin)
    v = kvp[:, 128:]
    lane = lax.broadcasted_iota(jnp.int32, (64, 128), 1)
    for e in range(2):
        k0, k1 = k[128 * e:128 * e + 64], k[128 * e + 64:128 * e + 128]
        vt = v[128 * e:128 * (e + 1)].T.astype(BF)
        kvs[0, 128 * e:128 * e + 64, :] = jnp.where(lane < 64, k0, pltpu.roll(k1, 64, 1)).astype(BF)
        kvs[1, 128 * e:128 * e + 64, :] = jnp.where(lane < 64, pltpu.roll(k0, 64, 1), k1).astype(BF)
        for cc in range(2):
            kvs[cc, 128 * e + 64:128 * e + 128, :] = vt[64 * cc:64 * (cc + 1)]
    own = shard_id(y, z, c)
    other = shard_id(y, z, 1 - c)
    pcopy = pltpu.make_async_remote_copy(
        kvs.at[1 - c], kvb.at[own], ps_sem, kr_sem.at[own], device_id=partner, device_id_type=MESH)
    pcopy.start()
    kvb[own] = kvs[c]

    sends, outs = [], []
    null = pltpu.make_async_copy(kvu.at[64], kv_out.at[64], us_sem.at[64])
    null.start()
    outs.append(null)

    def send(sid, target):
        cp = pltpu.make_async_remote_copy(
            kvb.at[sid], kvb.at[sid], ks_sem.at[len(sends)], kr_sem.at[sid],
            device_id=target, device_id_type=MESH)
        cp.start()
        sends.append(cp)

    def arrived(sid):
        pltpu.make_async_remote_copy(
            kvb.at[sid], kvb.at[sid], ps_sem, kr_sem.at[sid],
            device_id=partner, device_id_type=MESH).wait_recv()

    def unpack(sid):
        for e in range(2):
            k2 = kvb[sid, 128 * e:128 * e + 64, :].astype(F32)
            r2 = pltpu.roll(k2, 64, 1)
            kvu[sid, e, 0:64, :] = jnp.where(lane < 64, k2, r2).astype(BF)
            kvu[sid, e, 64:128, :] = jnp.where(lane < 64, r2, k2).astype(BF)
            kvu[sid, e, 128:192, :] = kvb[sid, 128 * e + 64:128 * e + 128, :]
            kvu[sid, e, 192:208, :] = jnp.ones((16, 128), BF)
        cp = pltpu.make_async_copy(kvu.at[sid], kv_out.at[sid], us_sem.at[sid])
        cp.start()
        outs.append(cp)

    def block(dy, dz, core):
        return shard_id((y + dy + 4) % 4, (z + dz + 8) % 8, core)

    def q_block(n):
        acc = jnp.zeros((ROWS, 256), F32)
        for i in range(4):
            acc = acc + jnp.dot(
                xb[i], wq[i * feats:(i + 1) * feats, n * 256:(n + 1) * 256], preferred_element_type=F32)
        for u in range(2):
            qs[n * 2 + u] = (turned(acc[:, u * 128:(u + 1) * 128], cos, sin) * 0.125).astype(BF)

    for sid in (own, other):
        if sid is other:
            arrived(other)
        for dy, dz in ((0, 1), (0, -1), (1, 0), (-1, 0)):
            send(sid, plane(dy, dz))

    swap = Swap(lambda i: qs.at[i], lambda m: q_out.at[m], relay, (qs_sem, qr_sem, qq_sem), c, y, z)
    copies[5].wait()
    for n in range(4):
        q_block(n)
    lines = swap.queue()
    swap.step(swap.side)
    keep = pltpu.make_async_copy(qs.at[me], q_out.at[me], own_sem)
    keep.start()
    outs.append(keep)
    fresh = [own, other]
    waits = 0
    for op, part, dy, dz in ACTIONS:
        if op == 6:
            if lines[part]:
                swap.step(lines[part].pop(0))
            continue
        sid = block(dy, dz, part)
        if op == 0:
            arrived(sid)
            fresh.append(sid)
            waits += 1
            if waits == 32:
                swap.forward()
            if waits > 12 and waits % 4 != 0:
                unpack(fresh.pop(0))
        elif op == 5:
            sgn = 1 - 2 * c
            send(shard_id((y - sgn + 4) % 4, z, 1), plane(sgn, 0))
        else:
            send(sid, plane(*((0, 1), (0, -1), (1, 0), (-1, 0))[op - 1]))
    for sid in fresh:
        unpack(sid)
    swap.finish()
    for cp in outs:
        cp.wait()
    for cp in sends + [pcopy]:
        cp.wait_send()


def attend_kernel(
    meta, doc_len, sinks, q_hbm, kv_hbm, o_ref,
    q_ref, kv, qsel, mref, aref, buf0, buf1, buf2, buf3, tops, firsts, steps, sem, q_sem,
):
    q_load = pltpu.make_async_copy(q_hbm, q_ref, q_sem)
    q_load.start()
    load = pltpu.make_async_copy(kv_hbm, kv, sem)
    load.start()
    bufs = ((buf0, buf1), (buf2, buf3))
    _, c, y, _ = place()
    base = (c * 4 + y) * 2
    lane = lax.broadcasted_iota(jnp.int32, (1, 256), 1)
    sub = lax.broadcasted_iota(jnp.int32, (TILE, 256), 0)
    sink = jnp.where(lane < 128, sinks[base], sinks[base + 1]) * LOG2E

    blank = jnp.concatenate([jnp.zeros((64, 256), F32), jnp.ones((16, 256), F32)], axis=0)

    def prep(n4, cr):
        for u in range(4):
            n = n4 * 4 + u
            qt = (q_ref[n >> 1, 128 * (u & 1):128 * (u & 1) + 128, :].astype(F32) * LOG2E).T
            qt = jnp.concatenate([qt[:64], qt[64:]], axis=1)
            hi = qt.astype(BF)
            lo = (qt - hi.astype(F32)).astype(BF)
            qsel[n] = jnp.concatenate([hi, lo], axis=0)
            tile = meta[16, n] * TILE
            firsts[n] = doc_start(doc_len, tile + (lane & 127)) - tile
            mref[n] = sink
            aref[n] = blank
        return cr


    for n in range(16, 18):
        mref[n] = sink
        aref[n] = blank

    counts = []
    for s in range(2):
        def add(i, cr):
            n = i * 2 + s
            steps[s * 2, i] = n << 7

            def put(ci, k):
                steps[s * 2 + 1, k] = (n << 7) + ci * CH
                return k + 1

            return lax.fori_loop(1, meta[17, n], put, cr)

        counts.append(lax.fori_loop(0, 8, add, jnp.int32(0)))
        steps[s * 2, 8] = (16 + s) << 7
    most = (jnp.maximum(counts[0], counts[1]) + 1) & ~1
    for s in range(2):
        def fill(k, cr):
            steps[s * 2 + 1, k] = (16 + s) << 7
            return cr
        lax.fori_loop(counts[s], most + 1, fill, 0)
    totals = (jnp.int32(8), most)
    q_load.wait()
    lax.fori_loop(0, 4, prep, 0)
    load.wait()

    def scores(s, kind, k, ph):
        w = steps[s * 2 + kind, k]
        nn = (w >> 7) & 15
        c0 = w & 127
        js = [meta[nn, c0 + u] for u in range(CH)]
        ks = [kv[j >> 1, j & 1, 0:128, :] for j in js]
        sc = jnp.dot(jnp.concatenate(ks, axis=0), qsel[nn], preferred_element_type=F32)
        if kind == 0:
            first = firsts[nn]
            parts = []
            for u in range(CH):
                if u == 0:
                    ok = (sub >= first) & (sub <= (lane & 127))
                else:
                    ok = sub >= first + (meta[16, nn] - js[u]) * TILE
                parts.append(jnp.where(ok, sc[u * 128:(u + 1) * 128], -1e30))
            sc = jnp.concatenate(parts, axis=0)
        bufs[s][ph][...] = sc
        tops[s * 2 + ph] = jnp.max(sc, axis=0, keepdims=True)

    def absorb(s, kind, k, ph):
        w = steps[s * 2 + kind, k]
        n = w >> 7
        nn = n & 15
        c0 = w & 127
        js = [meta[nn, c0 + u] for u in range(CH)]
        vt = jnp.concatenate([kv[j >> 1, j & 1, 128:208, :] for j in js], axis=1)
        mx, acc = mref[n], aref[n]
        if kind == 0:
            inside = firsts[nn] > 0
            mx = jnp.where(inside, sink, mx)
            acc = jnp.where(inside, blank, acc)
        new = jnp.maximum(mx, tops[s * 2 + ph])
        p = jnp.exp2(bufs[s][ph][...] - new).astype(BF)
        alpha = jnp.exp2(mx - new)
        mref[n] = new
        aref[n] = acc * alpha + jnp.dot(vt, p, preferred_element_type=F32)

    for kind in (1, 0):
        for s in range(2):
            scores(s, kind, 0, 0)

        def it(k2, cr):
            for ph in range(2):
                k = k2 * 2 + ph
                for s in range(2):
                    scores(s, kind, k + 1, 1 - ph)
                for s in range(2):
                    absorb(s, kind, k, ph)
            return cr

        lax.fori_loop(0, totals[kind] >> 1, it, 0)

    def fin(n4, cr):
        for u in range(4):
            a = aref[n4 * 4 + u]
            out = a[:64] / a[64:65]
            out = jnp.concatenate([out[:, :128], out[:, 128:]], axis=0)
            o_ref[n4 * 2 + u // 2, 128 * (u % 2):128 * (u % 2) + 128, :] = out.T.astype(BF)
        return cr

    lax.fori_loop(0, 4, fin, 0)


def return_kernel(o_ref, out_ref, relay, s_sem, r_sem, q_sem, own_sem):
    h, c, y, z = place()
    me = c * 4 + y
    barrier = pltpu.get_barrier_semaphore()
    for d in range(1, 8):
        i = (me + d) % 8
        pl.semaphore_signal(barrier, inc=1, device_id=device(i % 4, z, i // 4), device_id_type=MESH)
    pl.semaphore_wait(barrier, 7)

    def cols(m):
        return pl.ds(pl.multiple_of(m * 128, 128), 128)

    swap = Swap(lambda i: o_ref.at[i], lambda m: out_ref.at[:, cols(m)], relay, (s_sem, r_sem, q_sem), c, y, z)
    swap.start()
    keep = pltpu.make_async_copy(o_ref.at[me], out_ref.at[:, cols(me)], own_sem)
    keep.start()
    swap.forward()
    swap.finish()
    keep.wait()


def body(tokens, norm_gain, w_query, w_key, w_value, sinks, doc_lengths, tile_mask):
    vm = pl.BlockSpec(memory_space=pltpu.VMEM)
    anym = pl.BlockSpec(memory_space=pl.ANY)
    smem = pl.BlockSpec(memory_space=pltpu.SMEM)
    feats = tokens.shape[1]
    dma = pltpu.SemaphoreType.DMA
    kv, q, lists = pl.pallas_call(
        project_kernel,
        out_shape=(
            jax.ShapeDtypeStruct((65, 2, 208, 128), BF),
            jax.ShapeDtypeStruct((8, ROWS, 128), BF),
            jax.ShapeDtypeStruct((24, 128), jnp.int32),
        ),
        in_specs=[smem] + [anym] * 6,
        out_specs=(anym, anym, vm),
        scratch_shapes=[
            pltpu.VMEM((4, feats, ROWS), BF),
            pltpu.VMEM((4, ROWS, feats), BF),
            pltpu.VMEM((1, 4 * feats), F32),
            pltpu.VMEM((NT, NT), jnp.int32),
            pltpu.VMEM((4 * feats, 1024), BF),
            pltpu.VMEM((4 * feats, 256), BF),
            pltpu.VMEM((2, ROWS, 128), BF),
            pltpu.VMEM((64, ROWS, 128), BF),
            pltpu.VMEM((65, 2, 208, 128), BF),
            pltpu.VMEM((8, ROWS, 128), BF),
            pltpu.VMEM((2, ROWS, 128), BF),
            dma((6,)), dma((6,)), dma((6,)), dma((64,)), dma((64,)), dma, dma((65,)), dma((9,)), dma((8,)), dma((2,)), dma,
        ],
        compiler_params=pltpu.CompilerParams(collective_id=0, has_side_effects=True),
        name="project",
    )(doc_lengths, tokens.T, norm_gain, tile_mask, w_query, w_key, w_value)
    o = pl.pallas_call(
        attend_kernel,
        out_shape=jax.ShapeDtypeStruct((8, ROWS, 128), BF),
        in_specs=[smem, smem, smem, anym, anym],
        out_specs=vm,
        scratch_shapes=[
            pltpu.VMEM((8, ROWS, 128), BF),
            pltpu.VMEM((65, 2, 208, 128), BF),
            pltpu.VMEM((16, 128, 256), BF),
            pltpu.VMEM((18, 1, 256), F32),
            pltpu.VMEM((18, 80, 256), F32),
        ] + [pltpu.VMEM((CH * TILE, 256), F32)] * 4 + [pltpu.VMEM((4, 1, 256), F32), pltpu.VMEM((16, 1, 256), jnp.int32), pltpu.SMEM((4, 256), jnp.int32), dma, dma],
        name="attend",
    )(lists, doc_lengths, sinks, q, kv)
    return pl.pallas_call(
        return_kernel,
        out_shape=jax.ShapeDtypeStruct((ROWS, 1024), BF),
        in_specs=[anym],
        out_specs=anym,
        scratch_shapes=[pltpu.VMEM((2, ROWS, 128), BF), dma((9,)), dma((8,)), dma((2,)), dma],
        compiler_params=pltpu.CompilerParams(collective_id=1, has_side_effects=True),
        name="give_back",
    )(o)


def solution(mesh):
    in_specs = (
        P(("grp", "blk"), "head"),
        P(),
        P(None, "head"),
        P(None, "head"),
        P(None, "head"),
        P("head"),
        P(),
        P(),
    )
    out_specs = P(("grp", "blk"), "head")
    return jax.shard_map(body, mesh=mesh, in_specs=in_specs, out_specs=out_specs, check_vma=False)
```

```python
import functools

import jax
import jax.numpy as jnp
from jax import lax
from jax.experimental import pallas as pl
from jax.experimental.pallas import tpu as pltpu
from jax.sharding import PartitionSpec as P

MESH = pl.DeviceIdType.MESH
HD = 64
TILE = 128
ROWS = 256
NT = 128
CH = 4
EPS = 1e-05
ROPE_BASE = 150000.0
LOG2E = 1.4426950408889634
ACTIONS = (
    (0, 0, 0, -1), (0, 0, 0, 1), (0, 1, -1, 0), (0, 1, 1, 0), (1, 0, 0, -1), (2, 0, 0, 1), (5, 1, -1, 0),
    (4, 0, 0, -1), (1, 1, -1, 0), (2, 1, 1, 0), (6, 0, 0, 0), (6, 1, 0, 0), (1, 1, 1, 0), (2, 1, -1, 0),
    (6, 0, 0, 0), (6, 1, 0, 0), (0, 1, 0, -1), (0, 1, 0, 1), (0, 0, -1, 0), (0, 0, 1, 0), (1, 1, 0, -1),
    (2, 1, 0, 1), (6, 0, 0, 0), (6, 1, 0, 0), (6, 0, 0, 0), (6, 1, 0, 0), (0, 0, 0, -2), (0, 0, 0, 2),
    (0, 1, 2, 0), (0, 0, 1, -1), (1, 0, 0, -2), (2, 1, 2, 0), (1, 1, 2, 0), (2, 0, 0, 2), (3, 0, 0, -2),
    (4, 0, 0, 1), (0, 1, -1, -1), (0, 1, 1, 1), (1, 1, -1, -1), (2, 1, 1, 1), (3, 0, 0, 2), (4, 0, 0, -2),
    (0, 1, 1, -1), (0, 1, -1, 1), (1, 1, 1, -1), (2, 1, -1, 1), (3, 0, 0, -1), (4, 0, 0, 2), (0, 1, 0, -2),
    (0, 1, 0, 2), (3, 0, 0, 1), (0, 0, 0, -3), (0, 1, 2, 1), (1, 0, 0, -3), (2, 1, 2, 1), (4, 0, 0, -3),
    (1, 1, 0, -2), (2, 1, 0, 2), (3, 0, -1, 0), (0, 1, 2, -1), (0, 0, 0, 3), (0, 0, -1, -2), (0, 0, 1, 1),
    (4, 0, 0, 3), (1, 1, 2, -1), (3, 0, 0, -3), (4, 0, 1, -1), (0, 1, -1, -2), (0, 1, 1, 2), (0, 0, -1, 2),
    (0, 0, 1, -2), (2, 1, 1, 2), (1, 1, -1, -2), (3, 0, 0, 3), (4, 0, 1, 1), (0, 1, 1, -2), (0, 1, -1, 2),
    (0, 0, -1, -1), (0, 0, 1, 2), (2, 1, -1, 2), (1, 1, 1, -2), (0, 0, 0, -4), (0, 1, 2, 2), (0, 0, -1, 1),
    (0, 0, 1, -3), (2, 1, 2, 2), (3, 0, 0, -4), (4, 0, 0, -4), (3, 0, -1, -2), (4, 0, 1, -3), (0, 1, 0, -3),
    (0, 1, 0, 3), (0, 0, 2, 0), (0, 0, 1, 3), (1, 1, 0, -3), (3, 0, -1, 2), (4, 0, 1, 3), (0, 1, 2, -2),
    (0, 1, 1, 3), (0, 0, -1, -3), (0, 0, 2, -1), (2, 1, 1, 3), (1, 1, 2, -2), (0, 1, -1, -3), (0, 1, -1, 3),
    (0, 0, -1, 3), (0, 0, 2, 1), (1, 1, -1, -3), (0, 1, 1, -3), (0, 1, 2, 3), (0, 0, -1, -4), (0, 0, 1, -4),
    (2, 1, 2, 3), (3, 0, -1, -4), (0, 1, 0, -4), (0, 0, 2, -2), (0, 0, 2, -3), (0, 1, 1, 4), (0, 1, 2, -3),
    (0, 0, 2, 2), (0, 0, 2, 3), (0, 1, -1, -4), (0, 1, 2, 4), (0, 0, 2, -4),
)
BF = jnp.bfloat16
F32 = jnp.float32

def place():
    h = lax.axis_index("head")
    g = lax.axis_index("grp")
    b = lax.axis_index("blk")
    c = g % 2
    y = (g // 2) * 2 + b // 8
    z = b % 8
    return h, c, y, z


def device(yy, zz, core):
    return {"grp": (yy // 2) * 2 + core, "blk": (yy % 2) * 8 + zz}


def shard_id(yy, zz, core):
    return (yy // 2) * 32 + core * 16 + (yy % 2) * 8 + zz


class Swap:
    def __init__(self, src, dst, relay, sems, c, y, z):
        self.src, self.dst, self.relay = src, dst, relay
        self.s_sem, self.r_sem, self.q_sem = sems
        self.c, self.y, self.z = c, y, z
        self.me = c * 4 + y
        self.up, self.down, self.far = (y + 1) % 4, (y + 3) % 4, (y + 2) % 4
        self.sent = []

    def go(self, src, dst, r_sem, target):
        cp = pltpu.make_async_remote_copy(
            src, dst, self.s_sem.at[len(self.sent)], r_sem, device_id=target, device_id_type=MESH)
        cp.start()
        self.sent.append(cp)

    def await_at(self, dst, r_sem):
        pltpu.make_async_remote_copy(
            dst, dst, self.s_sem.at[0], r_sem,
            device_id=device(self.y, self.z, 1 - self.c), device_id_type=MESH).wait_recv()

    def queue(self):
        c, z, me = self.c, self.z, self.me
        ups = [(self.far, self.relay.at[0], self.q_sem.at[0], device(self.up, z, c))]
        downs = [(4 + self.far, self.relay.at[1], self.q_sem.at[1], device(self.down, z, c))]
        for core in range(2):
            ups.append((core * 4 + self.up, self.dst(me), self.r_sem.at[me], device(self.up, z, core)))
            downs.append((core * 4 + self.down, self.dst(me), self.r_sem.at[me], device(self.down, z, core)))
        self.side = ((1 - c) * 4 + self.y, self.dst(me), self.r_sem.at[me], device(self.y, z, 1 - c))
        return ups, downs

    def step(self, entry):
        i, dst, r_sem, target = entry
        self.go(self.src(i), dst, r_sem, target)

    def start(self):
        for pair in zip(*self.queue()):
            for entry in pair:
                self.step(entry)
        self.step(self.side)

    def forward(self):
        c, z = self.c, self.z
        below, above = c * 4 + self.down, c * 4 + self.up
        self.await_at(self.relay.at[0], self.q_sem.at[0])
        self.go(self.relay.at[0], self.dst(below), self.r_sem.at[below], device(self.up, z, 0))
        self.await_at(self.relay.at[1], self.q_sem.at[1])
        self.go(self.relay.at[1], self.dst(above), self.r_sem.at[above], device(self.down, z, 1))

    def finish(self):
        for d in range(1, 8):
            i = (self.me + d) % 8
            self.await_at(self.dst(i), self.r_sem.at[i])
        for cp in self.sent:
            cp.wait_send()


def turned(x, cos, sin):
    lane = lax.broadcasted_iota(jnp.int32, x.shape, 1)
    other = jnp.where(lane % 64 < 32, pltpu.roll(x, 96, 1), pltpu.roll(x, 32, 1))
    return x * cos + other * sin


def angles(base):
    lane = lax.broadcasted_iota(jnp.int32, (1, 128), 1)
    freq = jnp.zeros((1, 128), F32)
    for i in range(HD // 2):
        freq = jnp.where(lane % 32 == i, ROPE_BASE ** (-2.0 * i / HD), freq)
    pos = lax.broadcasted_iota(jnp.int32, (ROWS, 128), 0) + base
    ang = pos.astype(F32) * freq
    sin = jnp.sin(ang)
    return jnp.cos(ang), jnp.where(lane % 64 < 32, -sin, sin)


def doc_start(doc_len, pos):
    end = jnp.int32(0)
    first = jnp.zeros_like(pos)
    for d in range(doc_len.shape[0]):
        end = end + doc_len[d]
        first = jnp.maximum(first, jnp.where(end <= pos, end, 0))
    return first


def key_lists(doc_len, tile_mask, z, lists):
    n = lax.broadcasted_iota(jnp.int32, (1, 128), 1)
    i = n // 2
    yy, core = i % 4, i // 4
    tile = shard_id(yy, z, core) * 2 + n % 2
    first = doc_start(doc_len, tile * TILE)
    last = doc_start(doc_len, tile * TILE + TILE - 1)
    j = lax.broadcasted_iota(jnp.int32, (NT, 128), 0)
    k = lax.broadcasted_iota(jnp.int32, (NT, 128), 1)
    pick = jnp.where(j == tile, 1.0, 0.0).astype(BF)
    listed = jnp.dot(tile_mask[...].astype(F32).T.astype(BF), pick, preferred_element_type=F32) > 0.5
    active = (listed | (j == tile)) & (j <= tile) & (j * TILE + TILE > first)
    act = jnp.where(active, 1.0, 0.0).astype(BF)
    lower = jnp.where(k < j, 1.0, 0.0).astype(BF)
    before = jnp.dot(lower, act, preferred_element_type=F32).astype(jnp.int32)
    spot = jnp.where(active, jnp.where(j == tile, 0, before + 1), -1)
    count = jnp.sum(jnp.where(active, 1, 0), axis=0, keepdims=True)
    for r in range(16):
        hit = spot[:, r:r + 1] == k
        lists[r:r + 1, :] = jnp.sum(jnp.where(hit, j - NT, 0), axis=0, keepdims=True) + NT
    lists[16:17, :] = tile
    lists[17:18, :] = (count + CH - 1) // CH
    lists[18:19, :] = jnp.where(first == last, 0, 1)
    lists[19:24, :] = jnp.zeros((5, 128), jnp.int32)


def project_kernel(
    doc_len, tok_hbm, gain_hbm, mask_hbm, wq_hbm, wk_hbm, wv_hbm,
    kv_out, q_out, lists,
    xt, xb, gain, mask, wq, wkv, kvs, kvb, kvu, qs, relay,
    wsem, xs_sem, xr_sem, ks_sem, kr_sem, ps_sem, us_sem, qs_sem, qr_sem, qq_sem, own_sem,
):
    h, c, y, z = place()
    me = c * 4 + y
    feats = xb.shape[2]
    half = ROWS // 2

    copies = [
        pltpu.make_async_copy(tok_hbm, xt.at[h], wsem.at[0]),
        pltpu.make_async_copy(gain_hbm, gain.at[0], wsem.at[1]),
        pltpu.make_async_copy(mask_hbm, mask, wsem.at[2]),
        pltpu.make_async_copy(wk_hbm, wkv.at[:, 0:128], wsem.at[3]),
        pltpu.make_async_copy(wv_hbm, wkv.at[:, 128:256], wsem.at[4]),
        pltpu.make_async_copy(wq_hbm, wq, wsem.at[5]),
    ]
    for cp in copies:
        cp.start()

    def plane(dy, dz):
        return device((y + dy + 4) % 4, (z + dz + 8) % 8, c)

    def mate(d):
        i = (me + d) % 8
        return i, device(i % 4, z, i // 4)

    partner = device(y, z, 1 - c)
    ahead, behind, across = (h + 1) % 4, (h + 3) % 4, (h + 2) % 4
    barrier = pltpu.get_barrier_semaphore()
    for x in (ahead, behind):
        pl.semaphore_signal(barrier, inc=1, device_id={"head": x}, device_id_type=MESH)
    for dz in (1, -1):
        pl.semaphore_signal(barrier, inc=1, device_id=plane(0, dz), device_id_type=MESH)
    for d in range(1, 8):
        pl.semaphore_signal(barrier, inc=1, device_id=mate(d)[1], device_id_type=MESH)
    pl.semaphore_wait(barrier, 11)
    copies[0].wait()

    xsent = []
    top, low = pl.ds(0, half), pl.ds(half, half)

    def xsend(n, src, rows, to):
        cp = pltpu.make_async_remote_copy(
            xt.at[src, :, rows], xt.at[src, :, rows], xs_sem.at[n], xr_sem.at[n],
            device_id={"head": to}, device_id_type=MESH)
        cp.start()
        xsent.append(cp)

    def xwait(n, src, rows):
        pltpu.make_async_remote_copy(
            xt.at[src, :, rows], xt.at[src, :, rows], xs_sem.at[n], xr_sem.at[n],
            device_id={"head": ahead}, device_id_type=MESH).wait_recv()

    xsend(0, h, top, ahead)
    xsend(1, h, low, behind)
    xsend(2, h, low, ahead)
    xsend(3, h, top, behind)
    cos, sin = angles(shard_id(y, z, c) * ROWS)
    xwait(0, behind, top)
    xsend(4, behind, top, ahead)
    xwait(1, ahead, low)
    xsend(5, ahead, low, behind)

    copies[2].wait()
    key_lists(doc_len, mask, z, lists)
    kvu[64] = jnp.zeros((2, 208, 128), BF)
    copies[1].wait()

    def squares(i):
        w = xt[i].astype(F32).T
        xb[i] = w.astype(BF)
        return jnp.sum(w * w, axis=1, keepdims=True)

    total = squares(h)
    xwait(2, behind, low)
    total = total + squares(behind)
    xwait(3, ahead, top)
    total = total + squares(ahead)
    xwait(4, across, top)
    xwait(5, across, low)
    total = total + squares(across)
    scale = lax.rsqrt(total / (4 * feats) + EPS)
    for cp in xsent:
        cp.wait_send()
    copies[3].wait()
    copies[4].wait()
    kvp = jnp.zeros((ROWS, 256), F32)
    for i in range(4):
        w = xb[i].astype(F32) * scale * gain[:, i * feats:(i + 1) * feats]
        w = w.astype(BF)
        xb[i] = w
        kvp = kvp + jnp.dot(w, wkv[i * feats:(i + 1) * feats, :], preferred_element_type=F32)
    k = turned(kvp[:, :128], cos, sin)
    v = kvp[:, 128:]
    lane = lax.broadcasted_iota(jnp.int32, (64, 128), 1)
    for e in range(2):
        k0, k1 = k[128 * e:128 * e + 64], k[128 * e + 64:128 * e + 128]
        vt = v[128 * e:128 * (e + 1)].T.astype(BF)
        kvs[0, 128 * e:128 * e + 64, :] = jnp.where(lane < 64, k0, pltpu.roll(k1, 64, 1)).astype(BF)
        kvs[1, 128 * e:128 * e + 64, :] = jnp.where(lane < 64, pltpu.roll(k0, 64, 1), k1).astype(BF)
        for cc in range(2):
            kvs[cc, 128 * e + 64:128 * e + 128, :] = vt[64 * cc:64 * (cc + 1)]
    own = shard_id(y, z, c)
    other = shard_id(y, z, 1 - c)
    pcopy = pltpu.make_async_remote_copy(
        kvs.at[1 - c], kvb.at[own], ps_sem, kr_sem.at[own], device_id=partner, device_id_type=MESH)
    pcopy.start()
    kvb[own] = kvs[c]

    sends, outs = [], []
    null = pltpu.make_async_copy(kvu.at[64], kv_out.at[64], us_sem.at[64])
    null.start()
    outs.append(null)

    def send(sid, target):
        cp = pltpu.make_async_remote_copy(
            kvb.at[sid], kvb.at[sid], ks_sem.at[len(sends)], kr_sem.at[sid],
            device_id=target, device_id_type=MESH)
        cp.start()
        sends.append(cp)

    def arrived(sid):
        pltpu.make_async_remote_copy(
            kvb.at[sid], kvb.at[sid], ps_sem, kr_sem.at[sid],
            device_id=partner, device_id_type=MESH).wait_recv()

    def unpack(sid):
        for e in range(2):
            k2 = kvb[sid, 128 * e:128 * e + 64, :].astype(F32)
            r2 = pltpu.roll(k2, 64, 1)
            kvu[sid, e, 0:64, :] = jnp.where(lane < 64, k2, r2).astype(BF)
            kvu[sid, e, 64:128, :] = jnp.where(lane < 64, r2, k2).astype(BF)
            kvu[sid, e, 128:192, :] = kvb[sid, 128 * e + 64:128 * e + 128, :]
            kvu[sid, e, 192:208, :] = jnp.ones((16, 128), BF)
        cp = pltpu.make_async_copy(kvu.at[sid], kv_out.at[sid], us_sem.at[sid])
        cp.start()
        outs.append(cp)

    def block(dy, dz, core):
        return shard_id((y + dy + 4) % 4, (z + dz + 8) % 8, core)

    def q_block(n):
        acc = jnp.zeros((ROWS, 256), F32)
        for i in range(4):
            acc = acc + jnp.dot(
                xb[i], wq[i * feats:(i + 1) * feats, n * 256:(n + 1) * 256], preferred_element_type=F32)
        for u in range(2):
            qs[n * 2 + u] = (turned(acc[:, u * 128:(u + 1) * 128], cos, sin) * 0.125).astype(BF)

    for sid in (own, other):
        if sid is other:
            arrived(other)
        for dy, dz in ((0, 1), (0, -1), (1, 0), (-1, 0)):
            send(sid, plane(dy, dz))

    swap = Swap(lambda i: qs.at[i], lambda m: q_out.at[m], relay, (qs_sem, qr_sem, qq_sem), c, y, z)
    copies[5].wait()
    for n in range(4):
        q_block(n)
    lines = swap.queue()
    swap.step(swap.side)
    keep = pltpu.make_async_copy(qs.at[me], q_out.at[me], own_sem)
    keep.start()
    outs.append(keep)
    fresh = [own, other]
    waits = 0
    for op, part, dy, dz in ACTIONS:
        if op == 6:
            if lines[part]:
                swap.step(lines[part].pop(0))
            continue
        sid = block(dy, dz, part)
        if op == 0:
            for _ in range(2):
                if waits > 14 and fresh:
                    unpack(fresh.pop(0))
            arrived(sid)
            fresh.append(sid)
            waits += 1
            if waits == 32:
                swap.forward()
        elif op == 5:
            sgn = 1 - 2 * c
            send(shard_id((y - sgn + 4) % 4, z, 1), plane(sgn, 0))
        else:
            send(sid, plane(*((0, 1), (0, -1), (1, 0), (-1, 0))[op - 1]))
    for sid in fresh:
        unpack(sid)
    swap.finish()
    for cp in outs:
        cp.wait()
    for cp in sends + [pcopy]:
        cp.wait_send()


def attend_kernel(
    meta, doc_len, sinks, q_hbm, kv_hbm, o_ref,
    q_ref, kv, qsel, mref, aref, buf0, buf1, buf2, buf3, tops, firsts, steps, sem, q_sem,
):
    q_load = pltpu.make_async_copy(q_hbm, q_ref, q_sem)
    q_load.start()
    load = pltpu.make_async_copy(kv_hbm, kv, sem)
    load.start()
    bufs = ((buf0, buf1), (buf2, buf3))
    _, c, y, _ = place()
    base = (c * 4 + y) * 2
    lane = lax.broadcasted_iota(jnp.int32, (1, 256), 1)
    sub = lax.broadcasted_iota(jnp.int32, (TILE, 256), 0)
    sink = jnp.where(lane < 128, sinks[base], sinks[base + 1]) * LOG2E

    blank = jnp.concatenate([jnp.zeros((64, 256), F32), jnp.ones((16, 256), F32)], axis=0)

    def prep(n4, cr):
        for u in range(4):
            n = n4 * 4 + u
            qt = (q_ref[n >> 1, 128 * (u & 1):128 * (u & 1) + 128, :].astype(F32) * LOG2E).T
            qt = jnp.concatenate([qt[:64], qt[64:]], axis=1)
            hi = qt.astype(BF)
            lo = (qt - hi.astype(F32)).astype(BF)
            qsel[n] = jnp.concatenate([hi, lo], axis=0)
            tile = meta[16, n] * TILE
            firsts[n] = doc_start(doc_len, tile + (lane & 127)) - tile
            mref[n] = sink
            aref[n] = blank
        return cr


    for n in range(16, 18):
        mref[n] = sink
        aref[n] = blank

    counts = []
    for s in range(2):
        def add(i, cr):
            n = i * 2 + s
            steps[s * 2, i] = n << 7

            def put(ci, k):
                steps[s * 2 + 1, k] = (n << 7) + ci * CH
                return k + 1

            return lax.fori_loop(1, meta[17, n], put, cr)

        counts.append(lax.fori_loop(0, 8, add, jnp.int32(0)))
        steps[s * 2, 8] = (16 + s) << 7
    most = (jnp.maximum(counts[0], counts[1]) + 1) & ~1
    for s in range(2):
        def fill(k, cr):
            steps[s * 2 + 1, k] = (16 + s) << 7
            return cr
        lax.fori_loop(counts[s], most + 1, fill, 0)
    totals = (jnp.int32(8), most)
    q_load.wait()
    lax.fori_loop(0, 4, prep, 0)
    load.wait()

    def scores(s, kind, k, ph):
        w = steps[s * 2 + kind, k]
        nn = (w >> 7) & 15
        c0 = w & 127
        js = [meta[nn, c0 + u] for u in range(CH)]
        ks = [kv[j >> 1, j & 1, 0:128, :] for j in js]
        sc = jnp.dot(jnp.concatenate(ks, axis=0), qsel[nn], preferred_element_type=F32)
        if kind == 0:
            first = firsts[nn]
            parts = []
            for u in range(CH):
                if u == 0:
                    ok = (sub >= first) & (sub <= (lane & 127))
                else:
                    ok = sub >= first + (meta[16, nn] - js[u]) * TILE
                parts.append(jnp.where(ok, sc[u * 128:(u + 1) * 128], -1e30))
            sc = jnp.concatenate(parts, axis=0)
        bufs[s][ph][...] = sc
        tops[s * 2 + ph] = jnp.max(sc, axis=0, keepdims=True)

    def absorb(s, kind, k, ph):
        w = steps[s * 2 + kind, k]
        n = w >> 7
        nn = n & 15
        c0 = w & 127
        js = [meta[nn, c0 + u] for u in range(CH)]
        vt = jnp.concatenate([kv[j >> 1, j & 1, 128:208, :] for j in js], axis=1)
        mx, acc = mref[n], aref[n]
        if kind == 0:
            inside = firsts[nn] > 0
            mx = jnp.where(inside, sink, mx)
            acc = jnp.where(inside, blank, acc)
        new = jnp.maximum(mx, tops[s * 2 + ph])
        p = jnp.exp2(bufs[s][ph][...] - new).astype(BF)
        alpha = jnp.exp2(mx - new)
        mref[n] = new
        aref[n] = acc * alpha + jnp.dot(vt, p, preferred_element_type=F32)

    for kind in (1, 0):
        for s in range(2):
            scores(s, kind, 0, 0)

        def it(k2, cr):
            for ph in range(2):
                k = k2 * 2 + ph
                for s in range(2):
                    scores(s, kind, k + 1, 1 - ph)
                for s in range(2):
                    absorb(s, kind, k, ph)
            return cr

        lax.fori_loop(0, totals[kind] >> 1, it, 0)

    def fin(n4, cr):
        for u in range(4):
            a = aref[n4 * 4 + u]
            out = a[:64] / a[64:65]
            out = jnp.concatenate([out[:, :128], out[:, 128:]], axis=0)
            o_ref[n4 * 2 + u // 2, 128 * (u % 2):128 * (u % 2) + 128, :] = out.T.astype(BF)
        return cr

    lax.fori_loop(0, 4, fin, 0)


def return_kernel(o_ref, out_ref, relay, s_sem, r_sem, q_sem, own_sem):
    h, c, y, z = place()
    me = c * 4 + y
    barrier = pltpu.get_barrier_semaphore()
    for d in range(1, 8):
        i = (me + d) % 8
        pl.semaphore_signal(barrier, inc=1, device_id=device(i % 4, z, i // 4), device_id_type=MESH)
    pl.semaphore_wait(barrier, 7)

    def cols(m):
        return pl.ds(pl.multiple_of(m * 128, 128), 128)

    swap = Swap(lambda i: o_ref.at[i], lambda m: out_ref.at[:, cols(m)], relay, (s_sem, r_sem, q_sem), c, y, z)
    swap.start()
    keep = pltpu.make_async_copy(o_ref.at[me], out_ref.at[:, cols(me)], own_sem)
    keep.start()
    swap.forward()
    swap.finish()
    keep.wait()


def body(tokens, norm_gain, w_query, w_key, w_value, sinks, doc_lengths, tile_mask):
    vm = pl.BlockSpec(memory_space=pltpu.VMEM)
    anym = pl.BlockSpec(memory_space=pl.ANY)
    smem = pl.BlockSpec(memory_space=pltpu.SMEM)
    feats = tokens.shape[1]
    dma = pltpu.SemaphoreType.DMA
    kv, q, lists = pl.pallas_call(
        project_kernel,
        out_shape=(
            jax.ShapeDtypeStruct((65, 2, 208, 128), BF),
            jax.ShapeDtypeStruct((8, ROWS, 128), BF),
            jax.ShapeDtypeStruct((24, 128), jnp.int32),
        ),
        in_specs=[smem] + [anym] * 6,
        out_specs=(anym, anym, vm),
        scratch_shapes=[
            pltpu.VMEM((4, feats, ROWS), BF),
            pltpu.VMEM((4, ROWS, feats), BF),
            pltpu.VMEM((1, 4 * feats), F32),
            pltpu.VMEM((NT, NT), jnp.int32),
            pltpu.VMEM((4 * feats, 1024), BF),
            pltpu.VMEM((4 * feats, 256), BF),
            pltpu.VMEM((2, ROWS, 128), BF),
            pltpu.VMEM((64, ROWS, 128), BF),
            pltpu.VMEM((65, 2, 208, 128), BF),
            pltpu.VMEM((8, ROWS, 128), BF),
            pltpu.VMEM((2, ROWS, 128), BF),
            dma((6,)), dma((6,)), dma((6,)), dma((64,)), dma((64,)), dma, dma((65,)), dma((9,)), dma((8,)), dma((2,)), dma,
        ],
        compiler_params=pltpu.CompilerParams(collective_id=0, has_side_effects=True),
        name="project",
    )(doc_lengths, tokens.T, norm_gain, tile_mask, w_query, w_key, w_value)
    o = pl.pallas_call(
        attend_kernel,
        out_shape=jax.ShapeDtypeStruct((8, ROWS, 128), BF),
        in_specs=[smem, smem, smem, anym, anym],
        out_specs=vm,
        scratch_shapes=[
            pltpu.VMEM((8, ROWS, 128), BF),
            pltpu.VMEM((65, 2, 208, 128), BF),
            pltpu.VMEM((16, 128, 256), BF),
            pltpu.VMEM((18, 1, 256), F32),
            pltpu.VMEM((18, 80, 256), F32),
        ] + [pltpu.VMEM((CH * TILE, 256), F32)] * 4 + [pltpu.VMEM((4, 1, 256), F32), pltpu.VMEM((16, 1, 256), jnp.int32), pltpu.SMEM((4, 256), jnp.int32), dma, dma],
        name="attend",
    )(lists, doc_lengths, sinks, q, kv)
    return pl.pallas_call(
        return_kernel,
        out_shape=jax.ShapeDtypeStruct((ROWS, 1024), BF),
        in_specs=[anym],
        out_specs=anym,
        scratch_shapes=[pltpu.VMEM((2, ROWS, 128), BF), dma((9,)), dma((8,)), dma((2,)), dma],
        compiler_params=pltpu.CompilerParams(collective_id=1, has_side_effects=True),
        name="give_back",
    )(o)


def solution(mesh):
    in_specs = (
        P(("grp", "blk"), "head"),
        P(),
        P(None, "head"),
        P(None, "head"),
        P(None, "head"),
        P("head"),
        P(),
        P(),
    )
    out_specs = P(("grp", "blk"), "head")
    return jax.shard_map(body, mesh=mesh, in_specs=in_specs, out_specs=out_specs, check_vma=False)
```
